256 devices in a mesh: dp: 128 (over z, y, x), mp: 2 (over core).
Axes of the slice: x: 4, y: 4, z: 8, core: 2. Of those that a mesh axis runs over, the one named last changes fastest.
Arguments:
- tokens: bfloat16 [16384, 4096], P('dp')
- key_cot: bfloat16 [16384, 1024], P('dp', 'mp'), may hold values from -6 to 6
- routes: int32 [16384, 1], P('dp'), may hold values from 0 to 127; in each aligned block of 128 rows (0 to 127, 128 to 255, ...) at most 2 rows name the same one
- counts: int32 [128, 4], P('dp'), may hold values from 1 to 64, 128 in all within a row
- widths: int32 [4], replicated, may hold values from 2 to 8, as said below
- key_weight: bfloat16 [4096, 1024], P('dp', 'mp')
Outputs:
- row_grads: bfloat16 [32768, 4096], P('dp', 'mp')
- key_grad: float32 [4096, 1024], P('dp', 'mp')
The draws below stay inside these ranges and needn't reach their ends.
Inputs may be any that keep to these rules, and one draw needn't show every extreme that they name: `routes`: within the rows of one index of dp no destination is named more than 2 times, a bound that some block reaches. Each index of dp has 4 counts that sum to 128. widths[0] = 8 (the full net), widths[1] = 8 // 4 (the smallest), the other two lie strictly between.
All inputs are finite; a program needn't handle non-finite values.
Results may differ from the reference program's by a relative error of at most 0.0058.
Values may be sent and summed in bfloat16 or wider, within the bound.
A program may use at most 64 MiB of HBM per device.

```python
import math
import jax
import jax.numpy as jnp
import numpy as np
from jax import lax

D = 4096
KV_HEADS = 8
HEAD_DIM = 128
NSUB = 4
ROWS = 128
MOST = 2
RECV = 256
TOKENS = 16384
N_DP = 128
N_MP = 2


def log_scales(key, shape, low, high):
    return jnp.exp(jax.random.uniform(key, shape, jnp.float32, jnp.log(low), jnp.log(high)))


def draw_tokens(key, part):
    first_key, second_key, third_key = jax.random.split(key, 3)
    row_scale = log_scales(second_key, (TOKENS, 1), 0.3, 3.0)
    col_scale = log_scales(third_key, (1, D), 0.3, 3.0)
    base = jax.random.normal(first_key, (TOKENS, D), jnp.float32)
    return (base * row_scale * col_scale).astype(jnp.bfloat16)


def draw_key_weight(key, part):
    first_key, second_key, third_key = jax.random.split(key, 3)
    row_scale = log_scales(second_key, (D, 1), 0.3, 3.0)
    col_scale = log_scales(third_key, (1, KV_HEADS * HEAD_DIM), 0.3, 3.0)
    base = jax.random.normal(first_key, (D, KV_HEADS * HEAD_DIM), jnp.float32)
    return (base * row_scale * col_scale / jnp.sqrt(jnp.float32(D))).astype(jnp.bfloat16)


def draw_widths(key, part):
    middle = jax.random.randint(jax.random.fold_in(key, 7), (2,), KV_HEADS // 4 + 1, KV_HEADS).astype(jnp.int32)
    ends = jnp.array([KV_HEADS, KV_HEADS // 4], jnp.int32)
    return jnp.concatenate([ends, middle])


def levels(key, extent, shards, least, largest):
    loudness = 1.0
    for axis_at, blocks in shards:
        draws = jax.random.uniform(jax.random.fold_in(jax.random.fold_in(key, 6), axis_at), (blocks,), jnp.float32, least / len(shards), largest / len(shards))
        loudness = loudness * jnp.repeat(jnp.exp(draws), extent[axis_at] // blocks).reshape((-1,) + (1,) * (len(extent) - 1 - axis_at))
    return loudness


def length_profile(count, total, limit, lean):
    portions = [(1 << 20) // math.isqrt(standing ** lean) + 1 for standing in range(2, count + 1)]
    rest, holding = total - limit - (count - 1), [1] * (count - 1)
    while rest > 0:
        movable = [i for i in range(count - 1) if holding[i] < limit]
        pool, budget = sum([portions[i] for i in movable]), rest
        for i in movable:
            extra = min(limit - holding[i], max(1, budget * portions[i] // pool), rest)
            holding[i] = holding[i] + extra
            rest = rest - extra
    return np.array([limit] + holding)


def ragged_sizes(own_key, number_of, total, bound, lean):
    if number_of == 2:
        one = jax.random.randint(own_key, (), max(1, total - bound), min(bound, total - 1) + 1)
        return jnp.stack([one, total - one])
    tallies = jnp.asarray(length_profile(number_of, total, bound, lean), jnp.int32)
    pairs = (number_of - 1) // 2
    giver, taker = tallies[1:1 + 2 * pairs:2], tallies[2:2 + 2 * pairs:2]
    room = jnp.minimum(giver - 1, bound - taker)
    moved = jax.random.randint(jax.random.fold_in(own_key, 1), (pairs,), 0, 1 << 20) % (room + 1)
    tallies = tallies.at[1:1 + 2 * pairs:2].set(giver - moved).at[2:2 + 2 * pairs:2].set(taker + moved)
    return tallies[jax.random.permutation(jax.random.fold_in(own_key, 2), number_of)]


def deal_out(stream_key, own, number, rows, count, top, most, slope):
    order = jax.random.permutation(stream_key, count)
    packed, ordinary = load_shares(count, rows * top, most, slope, True), load_shares(count, rows * top, most, slope, False)
    places = jnp.arange(count)

    def named(sizes, turn):
        used = int((sizes > 0).sum())
        fixed = max(1, used // 4)
        shifted = fixed + (places - fixed + turn * (used - fixed)) % max(1, count - fixed)
        return jnp.zeros((count,), jnp.int32).at[order[jnp.where(places < fixed, places, shifted)]].set(jnp.asarray(sizes, jnp.int32))

    sizes = jnp.where(number % 4 == 0, named(packed, number // 4), named(ordinary, number - number // 4 - 1))
    mixed = jax.random.permutation(jax.random.fold_in(own, 3), count)
    giver, receiver = mixed[0:count // 2 * 2:2], mixed[1:count // 2 * 2:2]
    margin = jnp.minimum(sizes[giver] - 1, most - sizes[receiver]) // 2
    margin = jnp.where((giver == order[0]) | (receiver == order[0]) | (sizes[receiver] == 0), 0, jnp.maximum(margin, 0))
    shifted = jax.random.randint(jax.random.fold_in(own, 4), (count // 2,), 0, 1 << 20) % (margin + 1)
    sizes = sizes.at[giver].add(-shifted).at[receiver].add(shifted)
    members = jnp.searchsorted(jnp.cumsum(sizes), jnp.arange(rows * top), side="right").astype(jnp.int32)
    listing = members.reshape(top, rows).T
    listing = listing[jax.random.permutation(jax.random.fold_in(own, 1), rows)]
    turn = jax.random.randint(jax.random.fold_in(own, 2), (rows, 1), 0, top)
    return jnp.take_along_axis(listing, (jnp.arange(top)[None, :] + turn) % top, axis=1)


def load_shares(amount, total, limit, skew, full):
    weights = [(1 << 20) // math.isqrt(rank ** skew) + 1 for rank in range(1, amount + 1)]
    largest = limit if full else min(limit, max(-(-total // amount), total * weights[0] // sum(weights)))
    least = 1 if total - largest >= amount - 1 else 0
    holding, spare = [largest] + [least] * (amount - 1), total - largest - least * (amount - 1)
    while spare > 0:
        candidates = [i for i in range(1, amount) if holding[i] < largest] or [i for i in range(1, amount) if holding[i] < limit]
        pool, left = sum([weights[i] for i in candidates]), spare
        for i in candidates:
            more = min(limit - holding[i], max(1, left * weights[i] // pool), spare)
            holding[i] = holding[i] + more
            spare = spare - more
    return np.array(holding)


def gaussian(stream_key, extent, scale, limit, shards=(), held_as=jnp.bfloat16):
    gain = levels(stream_key, extent, shards, -0.22, 0.18) if shards else 1.0
    result = jax.random.normal(stream_key, extent, jnp.float32) * scale * gain
    return jnp.minimum(jnp.maximum(result, -limit), limit).astype(held_as)


def setup_inputs(seed: int = 0) -> dict:
    seeds = jax.random.split(jax.random.key(seed), 7)
    tokens = draw_tokens(jax.random.fold_in(seeds[6], 71), 0)
    key_cot = gaussian(seeds[1], (TOKENS, KV_HEADS * HEAD_DIM), 1.0, 6.0, ((0, 128), (1, 2)))
    routes_keys = jax.random.split(jax.random.fold_in(seeds[2], 1), TOKENS // ROWS)
    routes_turns = jax.random.permutation(jax.random.fold_in(seeds[2], 3), TOKENS // ROWS)
    routes = jax.vmap(lambda own, number: deal_out(jax.random.fold_in(seeds[2], 2), own, number, ROWS, N_DP, 1, MOST, 2))(routes_keys, routes_turns).reshape((TOKENS, 1))
    counts = jax.vmap(lambda own: ragged_sizes(own, NSUB, ROWS, ROWS // 2, 2))(jax.random.split(seeds[3], N_DP)).reshape((N_DP, NSUB)).astype(jnp.int32)
    widths = draw_widths(jax.random.fold_in(seeds[6], 71), 0)
    key_weight = draw_key_weight(jax.random.fold_in(seeds[6], 71), 0)
    return {"tokens": tokens, "key_cot": key_cot, "routes": routes, "counts": counts, "widths": widths, "key_weight": key_weight}


epsilon = 1e-06

def subnet_of_rows(counts):
    bounds = jnp.cumsum(counts, axis=1)
    positions = jnp.arange(ROWS, dtype=jnp.int32)
    above = positions[None, :, None] >= bounds[:, None, :NSUB - 1]
    return lax.optimization_barrier(jnp.sum(above.astype(jnp.int32), axis=2))

def block_grads(block_tokens, block_cot, head_mask, key_weight):
    hidden = block_tokens
    key_proj = jnp.dot(hidden, key_weight, preferred_element_type=jnp.float32)
    row_count = key_proj.shape[0]
    per_head = key_proj.reshape(row_count, KV_HEADS, HEAD_DIM)
    head_scale = jnp.sqrt(lax.optimization_barrier(jnp.mean(per_head * per_head, axis=2, keepdims=True)) + epsilon)
    outputs = per_head / head_scale
    upstream = block_cot.astype(jnp.float32).reshape(row_count, KV_HEADS, HEAD_DIM) * head_mask[:, :, None]
    key_delta = (upstream - outputs * lax.optimization_barrier(jnp.mean(upstream * outputs, axis=2, keepdims=True))) / head_scale
    delta_low = key_delta.reshape(row_count, KV_HEADS * HEAD_DIM).astype(jnp.bfloat16)
    group_cols = KV_HEADS * HEAD_DIM // N_MP
    feature_delta = jnp.zeros((row_count, D), jnp.float32)
    for group_index in range(N_MP):
        first_col = group_index * group_cols
        part_delta = lax.dot_general(delta_low[:, first_col:first_col + group_cols], key_weight[:, first_col:first_col + group_cols], (((1,), (1,)), ((), ())), preferred_element_type=jnp.float32)
        rounded = lax.optimization_barrier(part_delta.astype(jnp.bfloat16))
        feature_delta = feature_delta + rounded.astype(jnp.float32)
    weight_term = lax.dot_general(hidden, delta_low, (((0,), (0,)), ((), ())), preferred_element_type=jnp.float32)
    return (feature_delta.astype(jnp.bfloat16), weight_term)

def reference(tokens, key_cot, routes, counts, widths, key_weight):
    subnet = subnet_of_rows(counts)
    row_width = widths[subnet]
    head_mask = (jnp.arange(KV_HEADS, dtype=jnp.int32)[None, None, :] < row_width[:, :, None]).astype(jnp.float32)
    token_blocks = tokens.reshape(N_DP, ROWS, D)
    cot_blocks = key_cot.reshape(N_DP, ROWS, KV_HEADS * HEAD_DIM)

    def step_block(total, inputs):
        input_grad, weight_term = block_grads(inputs[0], inputs[1], inputs[2], key_weight)
        return (total + weight_term, input_grad)
    start_total = jnp.zeros((D, KV_HEADS * HEAD_DIM), jnp.float32)
    total, input_grads = lax.scan(step_block, start_total, (token_blocks, cot_blocks, head_mask))
    key_grad = total / jnp.sqrt(jnp.float32(TOKENS))
    destination = routes[:, 0].reshape(N_DP, ROWS)
    one_hot = (destination[:, :, None] == jnp.arange(N_DP, dtype=jnp.int32)[None, None, :]).astype(jnp.int32)
    earlier = lax.optimization_barrier(jnp.sum(jnp.cumsum(one_hot, axis=1) * one_hot, axis=2)) - 1
    sources = jnp.arange(N_DP, dtype=jnp.int32)[:, None]
    target = (destination * RECV + sources * MOST + earlier).reshape(TOKENS).astype(jnp.int32)
    row_grads = jnp.zeros((N_DP * RECV, D), jnp.bfloat16).at[target].set(input_grads.reshape(TOKENS, D))
    return (row_grads, key_grad)
```

```python
import jax
import jax.numpy as jnp
from jax import lax
from jax.experimental import pallas as pl
from jax.experimental.pallas import tpu as pltpu
from jax.sharding import PartitionSpec as P

HEAD_DIM = 128
EPSILON = 1e-06
MESH = pl.DeviceIdType.MESH
NZ, NY, NX = 8, 4, 4
ROWS, WIDTH, COLS, FEATS = 128, 4096, 512, 32
HEADS = COLS // HEAD_DIM
A = (384, 512)
BC = (0, 384)
F32, BF16 = jnp.float32, jnp.bfloat16


def kernel(tokens, cot, routes, counts, widths, shard, rows_out, grad_out,
           W, tokT, dW, dl, D, S, R1, R2, R3, Rf, G, DXs, DXr,
           aZs, aZr, a1, aYs, aYr, a2, aXs, aXr,
           bXs, bXr, b1, bYs, bYr, cYs, cYr, c1, cXs, cXr, Zf, Zs, Zr,
           send_sem, recv_sem):
    me, m = lax.axis_index("dp"), lax.axis_index("mp")
    x, y, z = lax.rem(me, NX), lax.rem(me // NX, NY), me // (NX * NY)

    def device(zz, yy, xx, mm):
        return ((zz * NY + yy) * NX + xx, mm)

    def along(axis, j):
        return {"x": device(z, y, j, m), "y": device(z, j, x, m), "z": device(j, y, x, m)}[axis]

    place = {"x": (NX, x), "y": (NY, y), "z": (NZ, z)}

    def turn(axis, by):
        n, i = place[axis]
        return lax.rem(i + (by % n), n)

    copies = []

    def send(src, dst, to):
        at = len(copies)
        copy = pltpu.make_async_remote_copy(
            src_ref=src, dst_ref=dst, send_sem=send_sem.at[at], recv_sem=recv_sem.at[at],
            device_id=to, device_id_type=MESH)
        copy.start()
        copies.append(copy)
        return copy

    class Direct:
        def __init__(self, axis, src, dst):
            n, i = place[axis]
            self.sent = []
            for o in range(1, n):
                j = turn(axis, o)
                self.sent.append(send(src(j), dst(o), along(axis, j)))

        def wait(self):
            for copy in self.sent:
                copy.wait_recv()

    class Gather:
        def __init__(self, axis, region):
            self.axis, self.region, self.n = axis, region, place[axis][0]
            self.last = ()

        def wait(self):
            for copy in self.last:
                copy.wait_recv()

        def step(self, k):
            self.wait()
            halves = (0, 1) if k == self.n // 2 else (None, None)
            right = self.region(turn(self.axis, -(k - 1)), halves[0])
            left = self.region(turn(self.axis, k - 1), halves[1])
            self.last = (send(right, right, along(self.axis, turn(self.axis, 1))),
                         send(left, left, along(self.axis, turn(self.axis, -1))))

    class Reduce:
        def __init__(self, axis, lead, local, sbuf, rbuf):
            self.axis, self.lead, self.local, self.sbuf, self.rbuf = axis, lead, local, sbuf, rbuf
            self.n = place[axis][0]
            self.last = ()

        def step(self, t):
            n, lead = self.n, self.lead
            now = []
            for d in range(2):
                if t > 1:
                    self.last[d].wait_recv()
                by = n // 2 - t + 1
                j = turn(self.axis, by if d == 0 else -by)
                to = along(self.axis, turn(self.axis, 1 if d == 0 else -1))
                first, count = d * (lead // 2), lead // 2

                def plain(l, _):
                    self.sbuf[d, t - 1, l] = self.local(j, l).astype(BF16)
                    return 0

                def added(l, _):
                    self.sbuf[d, t - 1, l] = (self.local(j, l) + self.rbuf[d, t - 2, l].astype(F32)).astype(BF16)
                    return 0

                if t == 1:
                    lax.fori_loop(first, first + count, plain, 0)
                    part = pl.ds(first, count)
                    now.append(send(self.sbuf.at[d, t - 1, part], self.rbuf.at[d, t - 1, part], to))
                    continue
                if t == 2:
                    lax.fori_loop(first, first + count, added, 0)
                    lax.fori_loop(lead // 2 - first, lead - first, plain, 0)
                else:
                    lax.fori_loop(0, lead, added, 0)
                now.append(send(self.sbuf.at[d, t - 1], self.rbuf.at[d, t - 1], to))
            self.last = tuple(now)

        def finish(self, out):
            for copy in self.last:
                copy.wait_recv()
            i, s = place[self.axis][1], self.n // 2 - 1

            def body(l, _):
                out(l, self.local(i, l) + self.rbuf[0, s, l].astype(F32) + self.rbuf[1, s, l].astype(F32))
                return 0

            lax.fori_loop(0, self.lead, body, 0)

    barrier = pltpu.get_barrier_semaphore()
    peers = [along(axis, turn(axis, o)) for axis in "xyz" for o in range(1, place[axis][0])]
    peers.append(device(z, y, x, 1 - m))
    for peer in peers:
        pl.semaphore_signal(barrier, inc=1, device_id=peer, device_id_type=MESH)
    W[z, y, x] = shard[...]
    pl.semaphore_wait(barrier, len(peers))

    up, down = pl.ds(0, 16), pl.ds(16, 16)
    ca, cb = pl.ds(A[0], A[1] - A[0]), pl.ds(BC[0], BC[1] - BC[0])

    def zs(half):
        return pl.ds(0, NZ) if half is None else pl.ds(half * (NZ // 2), NZ // 2)

    def ys(half):
        return pl.ds(0, NY) if half is None else pl.ds(half * (NY // 2), NY // 2)

    every = pl.ds(0, NX)
    all_y = pl.ds(0, NY)
    own_bc = W.at[z, y, x, :, cb]
    bc_z = Direct("z", lambda j: own_bc, lambda o: own_bc)
    own_a = W.at[z, y, x, :, ca]
    a_x = Direct("x", lambda j: own_a, lambda o: own_a)

    def flip(s, _):
        cols = pl.ds(pl.multiple_of(s * 512, 512), 512)
        tokT[s] = tokens[:, cols].T
        return 0

    lax.fori_loop(0, 8, flip, 0)
    named = jnp.broadcast_to(routes[...], (ROWS, ROWS))
    first_index = lax.broadcasted_iota(jnp.int32, (ROWS, ROWS), 0)
    second_index = lax.broadcasted_iota(jnp.int32, (ROWS, ROWS), 1)
    same = (named == named.astype(F32).T.astype(jnp.int32)) & (first_index < second_index)
    earlier = jnp.sum(same.astype(F32), axis=0, keepdims=True).astype(jnp.int32)
    slot = (routes[...] * 2 + earlier) * HEADS

    a_x.wait()
    own_ay = W.at[z, y, every, :, ca]
    a_y = Direct("y", lambda j: own_ay, lambda o: own_ay)
    bc_z.wait()
    b_y = Gather("y", lambda j, h: W.at[zs(h), j, x, up, cb])
    c_x = Gather("x", lambda j, h: W.at[zs(h), y, j, down, cb])
    b_y.step(1)
    c_x.step(1)
    a_y.wait()
    a_z = Gather("z", lambda j, h: W.at[j, ys(h), every, :, ca])
    a_z.step(1)
    b_y.step(2)
    c_x.step(2)
    b_y.wait()
    b_x = Gather("x", lambda j, h: W.at[zs(h), all_y, j, up, cb])
    b_x.step(1)
    c_x.wait()
    c_y = Gather("y", lambda j, h: W.at[zs(h), j, every, down, cb])
    c_y.step(1)
    a_z.step(2)
    a_z.step(3)
    a_z.step(4)
    a_z.wait()

    position = lax.broadcasted_iota(jnp.int32, (ROWS, 1), 0)
    bound0 = counts[0, 0]
    bound1 = bound0 + counts[0, 1]
    bound2 = bound1 + counts[0, 2]
    row_width = jnp.where(position < bound0, widths[0], jnp.where(
        position < bound1, widths[1], jnp.where(position < bound2, widths[2], widths[3])))

    def grads(lo, hi):
        proj = jnp.zeros((ROWS, hi - lo), F32)
        for s in range(NZ):
            slab = W[s, :, :, :, lo:hi].reshape(512, hi - lo)
            proj += jnp.dot(tokens[:, s * 512:(s + 1) * 512], slab, preferred_element_type=F32)
        for h in range(lo // HEAD_DIM, hi // HEAD_DIM):
            cols = slice(h * HEAD_DIM, (h + 1) * HEAD_DIM)
            own = proj[:, h * HEAD_DIM - lo:(h + 1) * HEAD_DIM - lo]
            inverse = 1.0 / jnp.sqrt(jnp.mean(own * own, axis=1, keepdims=True) + EPSILON)
            outputs = own * inverse
            head_mask = (m * HEADS + h < row_width).astype(F32)
            upstream = cot[:, cols].astype(F32) * head_mask
            delta = (upstream - outputs * jnp.mean(upstream * outputs, axis=1, keepdims=True)) * inverse
            dl[:, cols] = delta.astype(BF16)
            D[h] = delta.astype(BF16)

        def term(s, _):
            part = jnp.dot(tokT[s], dl[:, lo:hi], preferred_element_type=F32)
            dW[s, :, :, :, lo:hi] = part.reshape(NY, NX, FEATS, hi - lo)
            return 0

        lax.fori_loop(0, NZ, term, 0)

    grads(*A)
    ra_z = Reduce("z", NY, lambda j, l: dW[j, l, :, :, A[0]:A[1]], aZs, aZr)
    ra_z.step(1)
    b_x.step(2)
    c_y.step(2)
    ra_z.step(2)
    b_x.wait()
    c_y.wait()
    grads(*BC)
    rb_x = Reduce("x", NZ, lambda j, l: dW[l, :, j, 0:16, BC[0]:BC[1]], bXs, bXr)
    rc_y = Reduce("y", NZ, lambda j, l: dW[l, j, :, 16:32, BC[0]:BC[1]], cYs, cYr)
    rb_x.step(1)
    rc_y.step(1)
    ra_z.step(3)

    def pack(s, _):
        at = lax.broadcasted_iota(jnp.int32, (ROWS, ROWS), 0) + s * ROWS
        total = jnp.zeros((ROWS, HEAD_DIM), F32)
        for h in range(HEADS):
            total += jnp.dot((at == slot + h).astype(F32).astype(BF16), D[h], preferred_element_type=F32)
        S[s] = total.reshape(NY, NX, 8, HEAD_DIM).astype(BF16)
        return 0

    lax.fori_loop(0, NZ, pack, 0)
    r_z = Direct("z", lambda j: S.at[j], lambda o: R1.at[z])
    R1[z] = S[z]
    ra_z.step(4)
    rb_x.step(2)
    rc_y.step(2)
    r_z.wait()
    all_z = pl.ds(0, NZ)
    r_y = Direct("y", lambda j: R1.at[all_z, j], lambda o: R2.at[all_z, y])

    def keep_y(s, _):
        R2[s, y] = R1[s, y]
        return 0

    lax.fori_loop(0, NZ, keep_y, 0)

    def put_a1(l, v):
        a1[l] = v

    ra_z.finish(put_a1)

    def cast_a1(l, _):
        aYs[l] = a1[l].astype(BF16)
        return 0

    lax.fori_loop(0, NY, cast_a1, 0)
    ra_y = Direct("y", lambda j: aYs.at[j], lambda o: aYr.at[o - 1])
    r_y.wait()
    r_x = Direct("x", lambda j: R2.at[all_z, all_y, j], lambda o: R3.at[all_z, all_y, x])

    def keep_x(s, _):
        R3[s, :, x] = R2[s, :, x]
        return 0

    lax.fori_loop(0, NZ, keep_x, 0)

    def put_b1(l, v):
        b1[l] = v

    def put_c1(l, v):
        c1[l] = v

    rb_x.finish(put_b1)
    rc_y.finish(put_c1)
    rb_y = Reduce("y", NZ, lambda j, l: b1[l, j], bYs, bYr)
    rc_x = Reduce("x", NZ, lambda j, l: c1[l, j], cXs, cXr)
    rb_y.step(1)
    rc_x.step(1)
    ra_y.wait()
    total = a1[y]
    for o in range(NY - 1):
        total += aYr[o].astype(F32)
    a2[...] = total
    aXs[...] = total.astype(BF16)
    ra_x = Direct("x", lambda j: aXs.at[j], lambda o: aXr.at[o - 1])

    r_x.wait()
    Rf[...] = R3[...].astype(F32).reshape(8 * ROWS, HEAD_DIM)
    for h in range(HEADS):
        G[:, h * HEAD_DIM:(h + 1) * HEAD_DIM] = Rf[pl.ds(h, 2 * ROWS, stride=HEADS), :].astype(BF16)

    def product(tile):
        return lax.dot_general(G[...], W[tile].reshape(512, COLS), (((1,), (1,)), ((), ())),
                               preferred_element_type=F32).astype(BF16)

    partner = device(z, y, x, 1 - m)
    halves = []
    for t in range(4):
        DXs[t] = product((1 - m) * 4 + t)
        halves.append(send(DXs.at[t], DXr.at[t], partner))
    rb_y.step(2)
    rc_x.step(2)
    for t in range(4):
        own = product(m * 4 + t).astype(F32)
        halves[t].wait_recv()
        rows_out[:, t * 512:(t + 1) * 512] = (own + DXr[t].astype(F32)).astype(BF16)

    ra_x.wait()
    total = a2[x]
    for o in range(NX - 1):
        total += aXr[o].astype(F32)
    scale = 1.0 / 128.0
    grad_out[:, A[0]:A[1]] = total * scale

    def put_b2(l, v):
        Zf[l, 0:16] = v

    def put_c2(l, v):
        Zf[l, 16:32] = v

    rb_y.finish(put_b2)
    rc_x.finish(put_c2)

    def cast_z(l, _):
        Zs[l] = Zf[l].astype(BF16)
        return 0

    lax.fori_loop(0, NZ, cast_z, 0)
    r_bc = Direct("z", lambda j: Zs.at[j], lambda o: Zr.at[o - 1])
    r_bc.wait()
    total = Zf[z]
    for o in range(NZ - 1):
        total += Zr[o].astype(F32)
    grad_out[:, BC[0]:BC[1]] = total * scale
    for copy in copies:
        copy.wait_send()


N_COPIES = 160


def per_device(tokens, key_cot, routes, counts, widths, key_weight):
    vmem = pl.BlockSpec(memory_space=pltpu.VMEM)
    smem = pl.BlockSpec(memory_space=pltpu.SMEM)
    buffers = [
        ((NZ, NY, NX, FEATS, COLS), BF16),
        ((8, 512, ROWS), BF16),
        ((NZ, NY, NX, FEATS, COLS), F32),
        ((ROWS, COLS), BF16),
        ((HEADS, ROWS, HEAD_DIM), BF16),
        ((NZ, NY, NX, 8, HEAD_DIM), BF16),
        ((NZ, NY, NX, 8, HEAD_DIM), BF16),
        ((NZ, NY, NX, 8, HEAD_DIM), BF16),
        ((NZ, NY, NX, 8, HEAD_DIM), BF16),
        ((8 * ROWS, HEAD_DIM), F32),
        ((2 * ROWS, COLS), BF16),
        ((4, 2 * ROWS, 512), BF16),
        ((4, 2 * ROWS, 512), BF16),
        ((2, 4, NY, NX, FEATS, 128), BF16),
        ((2, 4, NY, NX, FEATS, 128), BF16),
        ((NY, NX, FEATS, 128), F32),
        ((NY, NX, FEATS, 128), BF16),
        ((NY - 1, NX, FEATS, 128), BF16),
        ((NX, FEATS, 128), F32),
        ((NX, FEATS, 128), BF16),
        ((NX - 1, FEATS, 128), BF16),
        ((2, 2, NZ, NY, 16, 384), BF16),
        ((2, 2, NZ, NY, 16, 384), BF16),
        ((NZ, NY, 16, 384), F32),
        ((2, 2, NZ, 16, 384), BF16),
        ((2, 2, NZ, 16, 384), BF16),
        ((2, 2, NZ, NX, 16, 384), BF16),
        ((2, 2, NZ, NX, 16, 384), BF16),
        ((NZ, NX, 16, 384), F32),
        ((2, 2, NZ, 16, 384), BF16),
        ((2, 2, NZ, 16, 384), BF16),
        ((NZ, FEATS, 384), F32),
        ((NZ, FEATS, 384), BF16),
        ((NZ - 1, FEATS, 384), BF16),
    ]
    return pl.pallas_call(
        kernel,
        out_shape=(jax.ShapeDtypeStruct((2 * ROWS, WIDTH // 2), BF16), jax.ShapeDtypeStruct((FEATS, COLS), F32)),
        in_specs=[vmem, vmem, vmem, smem, smem, vmem],
        out_specs=(vmem, vmem),
        scratch_shapes=[pltpu.VMEM(shape, dtype) for shape, dtype in buffers]
        + [pltpu.SemaphoreType.DMA((N_COPIES,)), pltpu.SemaphoreType.DMA((N_COPIES,))],
        compiler_params=pltpu.CompilerParams(
            collective_id=0, has_side_effects=True, vmem_limit_bytes=58 << 20),
    )(tokens, key_cot, routes.reshape(1, ROWS), counts, widths, key_weight)


def solution(mesh):
    return jax.shard_map(
        per_device,
        mesh=mesh,
        in_specs=(P("dp", None), P("dp", "mp"), P("dp", None), P("dp", None), P(), P("dp", "mp")),
        out_specs=(P("dp", "mp"), P("dp", "mp")),
        check_vma=False,
    )
```

```python
import jax
import jax.numpy as jnp
from jax import lax
from jax.experimental import pallas as pl
from jax.experimental.pallas import tpu as pltpu
from jax.sharding import PartitionSpec as P

HEAD_DIM = 128
EPSILON = 1e-06
MESH = pl.DeviceIdType.MESH
NZ, NY, NX = 8, 4, 4
ROWS, WIDTH, COLS, FEATS = 128, 4096, 512, 32
HEADS = COLS // HEAD_DIM
A = (384, 512)
BC = (0, 384)
F32, BF16 = jnp.float32, jnp.bfloat16


def kernel(tokens, cot, routes, counts, widths, shard, rows_out, grad_out,
           W, tokT, dW, dl, D, S, R1, R3, Rf, G, DXs, DXr,
           aZs, aZr, a1, aYs, aYr, a2, aXs, aXr,
           bXs, bXr, b1, bYs, bYr, cYs, cYr, c1, cXs, cXr, Zf, Zs, Zr,
           send_sem, recv_sem):
    me, m = lax.axis_index("dp"), lax.axis_index("mp")
    x, y, z = lax.rem(me, NX), lax.rem(me // NX, NY), me // (NX * NY)

    def device(zz, yy, xx, mm):
        return ((zz * NY + yy) * NX + xx, mm)

    def along(axis, j):
        return {"x": device(z, y, j, m), "y": device(z, j, x, m), "z": device(j, y, x, m)}[axis]

    place = {"x": (NX, x), "y": (NY, y), "z": (NZ, z)}

    def turn(axis, by):
        n, i = place[axis]
        return lax.rem(i + (by % n), n)

    copies = []

    def send(src, dst, to):
        at = len(copies)
        copy = pltpu.make_async_remote_copy(
            src_ref=src, dst_ref=dst, send_sem=send_sem.at[at], recv_sem=recv_sem.at[at],
            device_id=to, device_id_type=MESH)
        copy.start()
        copies.append(copy)
        return copy

    class Direct:
        def __init__(self, axis, src, dst):
            n, i = place[axis]
            self.sent = []
            for o in range(1, n):
                j = turn(axis, o)
                self.sent.append(send(src(j), dst(o), along(axis, j)))

        def wait(self):
            for copy in self.sent:
                copy.wait_recv()

    class Gather:
        def __init__(self, axis, region):
            self.axis, self.region, self.n = axis, region, place[axis][0]
            self.last = ()

        def wait(self):
            for copy in self.last:
                copy.wait_recv()

        def step(self, k):
            self.wait()
            halves = (0, 1) if k == self.n // 2 else (None, None)
            right = self.region(turn(self.axis, -(k - 1)), halves[0])
            left = self.region(turn(self.axis, k - 1), halves[1])
            self.last = (send(right, right, along(self.axis, turn(self.axis, 1))),
                         send(left, left, along(self.axis, turn(self.axis, -1))))

    class Reduce:
        def __init__(self, axis, lead, local, sbuf, rbuf):
            self.axis, self.lead, self.local, self.sbuf, self.rbuf = axis, lead, local, sbuf, rbuf
            self.n = place[axis][0]
            self.last = ()

        def put(self, d, t, j, lo, hi, arrived):
            value = self.local(j, lo, hi)
            if arrived:
                value += self.rbuf[d, t - 2, lo:hi].astype(F32)
            self.sbuf[d, t - 1, lo:hi] = value.astype(BF16)

        def step(self, t):
            n, lead = self.n, self.lead
            now = []
            for d in range(2):
                if t > 1:
                    self.last[d].wait_recv()
                by = n // 2 - t + 1
                j = turn(self.axis, by if d == 0 else -by)
                to = along(self.axis, turn(self.axis, 1 if d == 0 else -1))
                half = lead // 2
                first = d * half
                if t == 1:
                    self.put(d, t, j, first, first + half, False)
                    part = pl.ds(first, half)
                    now.append(send(self.sbuf.at[d, t - 1, part], self.rbuf.at[d, t - 1, part], to))
                    continue
                if t == 2:
                    self.put(d, t, j, first, first + half, True)
                    self.put(d, t, j, half - first, lead - first, False)
                else:
                    for lo in range(0, lead, half):
                        self.put(d, t, j, lo, lo + half, True)
                now.append(send(self.sbuf.at[d, t - 1], self.rbuf.at[d, t - 1], to))
            self.last = tuple(now)

        def finish(self):
            for copy in self.last:
                copy.wait_recv()
            i, s = place[self.axis][1], self.n // 2 - 1
            return (self.local(i, 0, self.lead) + self.rbuf[0, s].astype(F32)) + self.rbuf[1, s].astype(F32)

    barrier = pltpu.get_barrier_semaphore()
    peers = [along(axis, turn(axis, o)) for axis in "xyz" for o in range(1, place[axis][0])]
    peers.append(device(z, y, x, 1 - m))
    for peer in peers:
        pl.semaphore_signal(barrier, inc=1, device_id=peer, device_id_type=MESH)
    W[z, y, x] = shard[...]
    pl.semaphore_wait(barrier, len(peers))

    up, down = pl.ds(0, 16), pl.ds(16, 16)
    ca, cb = pl.ds(A[0], A[1] - A[0]), pl.ds(BC[0], BC[1] - BC[0])
    every = pl.ds(0, NX)
    all_y = pl.ds(0, NY)

    def span(half, n=4):
        return pl.ds(0, n) if half is None else pl.ds(half * (n // 2), n // 2)

    class ChunkGather:
        def __init__(self, q):
            self.q = q

        def near(self):
            q = self.q
            b_own, c_own = W.at[q, y, x, up, cb], W.at[q, y, x, down, cb]
            self.b = Direct("y", lambda j: b_own, lambda o: b_own)
            self.c = Direct("x", lambda j: c_own, lambda o: c_own)

        def far(self, k):
            q = self.q
            if k == 1:
                self.b.wait()
                self.b = Gather("x", lambda j, h: W.at[q, span(h), j, up, cb])
            self.b.step(k)
            if k == 1:
                self.c.wait()
                self.c = Gather("y", lambda j, h: W.at[q, j, span(h), down, cb])
            self.c.step(k)

        def wait(self):
            self.b.wait()
            self.c.wait()

    own_bc = W.at[z, y, x, :, cb]
    bc_z = Direct("z", lambda j: own_bc, lambda o: own_bc)
    chunks = [ChunkGather(turn("z", -o)) for o in range(NZ)]
    chunks[0].near()
    own_a = W.at[z, y, x, :, ca]
    a_x = Direct("x", lambda j: own_a, lambda o: own_a)

    def arrive(*offsets):
        for o in offsets:
            bc_z.sent[o - 1].wait_recv()
            chunks[o].near()

    def far(k, *offsets):
        for o in offsets:
            chunks[o].far(k)

    def flip(s):
        tokT[s] = tokens[:, s * 512:(s + 1) * 512].T

    named = jnp.broadcast_to(routes[...], (ROWS, ROWS))
    first_index = lax.broadcasted_iota(jnp.int32, (ROWS, ROWS), 0)
    second_index = lax.broadcasted_iota(jnp.int32, (ROWS, ROWS), 1)
    same = (named == named.astype(F32).T.astype(jnp.int32)) & (first_index < second_index)
    earlier = jnp.sum(same.astype(F32), axis=0, keepdims=True).astype(jnp.int32)
    slot = (routes[...] * 2 + earlier) * HEADS

    def a_ring(oy):
        row = turn("y", -oy)
        return Gather("z", lambda j, h: W.at[j, row, span(h), :, ca])

    a_rings = [a_ring(oy) for oy in range(NY)]

    def a_far(k, *rings):
        for oy in rings:
            a_rings[oy].step(k)

    a_x.wait()
    own_ay = W.at[z, y, every, :, ca]
    a_y = Direct("y", lambda j: own_ay, lambda o: own_ay)
    a_far(1, 0)
    far(1, 0)
    arrive(1, 7)
    flip(0)
    arrive(2, 6)
    a_y.wait()
    a_far(1, 1, 2, 3)
    far(1, 1, 7)
    arrive(3, 5)
    a_far(2, 0)
    far(2, 0)
    arrive(4)
    far(1, 2, 6)
    flip(1)
    a_far(2, 1, 2, 3)
    far(2, 1, 7)
    far(1, 3, 5)
    flip(2)
    a_far(3, 0)
    far(2, 2, 6)
    far(1, 4)
    flip(3)
    a_far(3, 1, 2, 3)
    a_far(4, 0)
    far(2, 3, 5)
    flip(4)
    flip(5)
    far(2, 4)
    flip(6)
    flip(7)
    a_far(4, 1, 2, 3)
    for ring in a_rings:
        ring.wait()

    position = lax.broadcasted_iota(jnp.int32, (ROWS, 1), 0)
    bound0 = counts[0, 0]
    bound1 = bound0 + counts[0, 1]
    bound2 = bound1 + counts[0, 2]
    row_width = jnp.where(position < bound0, widths[0], jnp.where(
        position < bound1, widths[1], jnp.where(position < bound2, widths[2], widths[3])))

    def grads(lo, hi):
        proj = jnp.zeros((ROWS, hi - lo), F32)
        for s in range(NZ):
            slab = W[s, :, :, :, lo:hi].reshape(512, hi - lo)
            proj += jnp.dot(tokens[:, s * 512:(s + 1) * 512], slab, preferred_element_type=F32)
        for h in range(lo // HEAD_DIM, hi // HEAD_DIM):
            cols = slice(h * HEAD_DIM, (h + 1) * HEAD_DIM)
            own = proj[:, h * HEAD_DIM - lo:(h + 1) * HEAD_DIM - lo]
            inverse = 1.0 / jnp.sqrt(jnp.mean(own * own, axis=1, keepdims=True) + EPSILON)
            outputs = own * inverse
            head_mask = (m * HEADS + h < row_width).astype(F32)
            upstream = cot[:, cols].astype(F32) * head_mask
            delta = (upstream - outputs * jnp.mean(upstream * outputs, axis=1, keepdims=True)) * inverse
            dl[:, cols] = delta.astype(BF16)
            D[h] = delta.astype(BF16)

        def term(s, _):
            part = jnp.dot(tokT[s], dl[:, lo:hi], preferred_element_type=F32)
            dW[s, :, :, :, lo:hi] = part.reshape(NY, NX, FEATS, hi - lo)
            return 0

        lax.fori_loop(0, NZ, term, 0)

    grads(*A)
    ra_z = Reduce("z", NY, lambda j, lo, hi: dW[j, lo:hi, :, :, A[0]:A[1]], aZs, aZr)
    ra_z.step(1)
    for chunk in chunks:
        chunk.wait()
    grads(*BC)

    class ChunkReduce:
        def __init__(self, at, o):
            q = turn("z", -o)
            self.at, self.o, self.q = at, o, q
            self.b = Reduce("x", NY, lambda j, lo, hi: dW[q, lo:hi, j, 0:16, BC[0]:BC[1]], bXs.at[at], bXr.at[at])
            self.c = Reduce("y", NX, lambda j, lo, hi: dW[q, j, lo:hi, 16:32, BC[0]:BC[1]], cYs.at[at], cYr.at[at])

        def step(self, t):
            self.b.step(t)
            self.c.step(t)

        def near(self):
            at = self.at
            total = self.b.finish()
            b1[at] = total
            bYs[at] = total.astype(BF16)
            self.b = Direct("y", lambda j: bYs.at[at, j], lambda o: bYr.at[at, o - 1])
            total = self.c.finish()
            c1[at] = total
            cXs[at] = total.astype(BF16)
            self.c = Direct("x", lambda j: cXs.at[at, j], lambda o: cXr.at[at, o - 1])

        def across(self):
            at = self.at
            for part, mine, arrived, rows, i in ((self.b, b1, bYr, slice(0, 16), y), (self.c, c1, cXr, slice(16, 32), x)):
                part.wait()
                total = mine[at, i]
                for k in range(3):
                    total += arrived[at, k].astype(F32)
                if self.o == 0:
                    Zf[rows] = total
                else:
                    Zs[at, rows] = total.astype(BF16)
            if self.o:
                self.sent = send(Zs.at[at], Zr.at[self.o - 1], along("z", self.q))

    order = (4, 3, 5, 2, 6, 1, 7, 0)
    units = [ChunkReduce(at, o) for at, o in enumerate(order)]
    for unit in units[:4]:
        unit.step(1)

    def pack(s, _):
        at = lax.broadcasted_iota(jnp.int32, (ROWS, ROWS), 0) + s * ROWS
        total = jnp.zeros((ROWS, HEAD_DIM), F32)
        for h in range(HEADS):
            total += jnp.dot((at == slot + h).astype(F32).astype(BF16), D[h], preferred_element_type=F32)
        S[s] = total.reshape(NY, NX, 8, HEAD_DIM).astype(BF16)
        return 0

    lax.fori_loop(0, NZ, pack, 0)
    r_z = Direct("z", lambda j: S.at[j], lambda o: R1.at[z])
    R1[z] = S[z]
    for unit in units[4:]:
        unit.step(1)
    ra_z.step(2)
    units[0].step(2)
    units[1].step(2)
    units[2].step(2)
    units[3].step(2)
    r_z.wait()
    all_z = pl.ds(0, NZ)
    r_xy = []
    for oy in range(NY):
        for ox in range(NX):
            if oy or ox:
                jy, jx = turn("y", oy), turn("x", ox)
                r_xy.append(send(R1.at[all_z, jy, jx], R3.at[all_z, y, x], device(z, jy, jx, m)))

    def keep(s, _):
        R3[s, y, x] = R1[s, y, x]
        return 0

    lax.fori_loop(0, NZ, keep, 0)
    units[0].near()
    units[4].step(2)
    ra_z.step(3)
    units[1].near()
    units[5].step(2)
    units[2].near()
    units[6].step(2)
    units[0].across()
    units[3].near()
    units[7].step(2)
    units[1].across()
    ra_z.step(4)
    units[4].near()
    units[2].across()

    for copy in r_xy:
        copy.wait_recv()
    Rf[...] = R3[...].astype(F32).reshape(8 * ROWS, HEAD_DIM)
    for h in range(HEADS):
        G[:, h * HEAD_DIM:(h + 1) * HEAD_DIM] = Rf[pl.ds(h, 2 * ROWS, stride=HEADS), :].astype(BF16)

    def product(tile):
        return lax.dot_general(G[...], W[tile].reshape(512, COLS), (((1,), (1,)), ((), ())),
                               preferred_element_type=F32).astype(BF16)

    partner = device(z, y, x, 1 - m)
    halves = []

    def give(t):
        DXs[t] = product((1 - m) * 4 + t)
        halves.append(send(DXs.at[t], DXr.at[t], partner))

    def take(t):
        own = product(m * 4 + t).astype(F32)
        halves[t].wait_recv()
        rows_out[:, t * 512:(t + 1) * 512] = (own + DXr[t].astype(F32)).astype(BF16)

    give(0)
    units[5].near()
    units[3].across()
    give(1)
    units[6].near()
    units[4].across()
    total = ra_z.finish()
    a1[...] = total
    aYs[...] = total.astype(BF16)
    ra_y = Direct("y", lambda j: aYs.at[j], lambda o: aYr.at[o - 1])
    units[7].near()
    units[5].across()
    give(2)
    units[6].across()
    give(3)
    units[7].across()
    ra_y.wait()
    total = a1[y]
    for o in range(NY - 1):
        total += aYr[o].astype(F32)
    a2[...] = total
    aXs[...] = total.astype(BF16)
    ra_x = Direct("x", lambda j: aXs.at[j], lambda o: aXr.at[o - 1])
    for t in range(4):
        take(t)
    scale = 1.0 / 128.0
    total = Zf[...]
    for unit in units:
        if unit.o:
            unit.sent.wait_recv()
            total += Zr[unit.o - 1].astype(F32)
    grad_out[:, BC[0]:BC[1]] = total * scale
    ra_x.wait()
    total = a2[x]
    for o in range(NX - 1):
        total += aXr[o].astype(F32)
    grad_out[:, A[0]:A[1]] = total * scale
    for copy in copies:
        copy.wait_send()


N_COPIES = 400


def per_device(tokens, key_cot, routes, counts, widths, key_weight):
    vmem = pl.BlockSpec(memory_space=pltpu.VMEM)
    smem = pl.BlockSpec(memory_space=pltpu.SMEM)
    buffers = [
        ((NZ, NY, NX, FEATS, COLS), BF16),
        ((8, 512, ROWS), BF16),
        ((NZ, NY, NX, FEATS, COLS), F32),
        ((ROWS, COLS), BF16),
        ((HEADS, ROWS, HEAD_DIM), BF16),
        ((NZ, NY, NX, 8, HEAD_DIM), BF16),
        ((NZ, NY, NX, 8, HEAD_DIM), BF16),
        ((NZ, NY, NX, 8, HEAD_DIM), BF16),
        ((8 * ROWS, HEAD_DIM), F32),
        ((2 * ROWS, COLS), BF16),
        ((4, 2 * ROWS, 512), BF16),
        ((4, 2 * ROWS, 512), BF16),
        ((2, 4, NY, NX, FEATS, 128), BF16),
        ((2, 4, NY, NX, FEATS, 128), BF16),
        ((NY, NX, FEATS, 128), F32),
        ((NY, NX, FEATS, 128), BF16),
        ((NY - 1, NX, FEATS, 128), BF16),
        ((NX, FEATS, 128), F32),
        ((NX, FEATS, 128), BF16),
        ((NX - 1, FEATS, 128), BF16),
        ((NZ, 2, 2, NY, 16, 384), BF16),
        ((NZ, 2, 2, NY, 16, 384), BF16),
        ((NZ, NY, 16, 384), F32),
        ((NZ, NY, 16, 384), BF16),
        ((NZ, NY - 1, 16, 384), BF16),
        ((NZ, 2, 2, NX, 16, 384), BF16),
        ((NZ, 2, 2, NX, 16, 384), BF16),
        ((NZ, NX, 16, 384), F32),
        ((NZ, NX, 16, 384), BF16),
        ((NZ, NX - 1, 16, 384), BF16),
        ((FEATS, 384), F32),
        ((NZ, FEATS, 384), BF16),
        ((NZ - 1, FEATS, 384), BF16),
    ]
    return pl.pallas_call(
        kernel,
        out_shape=(jax.ShapeDtypeStruct((2 * ROWS, WIDTH // 2), BF16), jax.ShapeDtypeStruct((FEATS, COLS), F32)),
        in_specs=[vmem, vmem, vmem, smem, smem, vmem],
        out_specs=(vmem, vmem),
        scratch_shapes=[pltpu.VMEM(shape, dtype) for shape, dtype in buffers]
        + [pltpu.SemaphoreType.DMA((N_COPIES,)), pltpu.SemaphoreType.DMA((N_COPIES,))],
        compiler_params=pltpu.CompilerParams(
            collective_id=0, has_side_effects=True, vmem_limit_bytes=58 << 20),
    )(tokens, key_cot, routes.reshape(1, ROWS), counts, widths, key_weight)


def solution(mesh):
    return jax.shard_map(
        per_device,
        mesh=mesh,
        in_specs=(P("dp", None), P("dp", "mp"), P("dp", None), P("dp", None), P(), P("dp", "mp")),
        out_specs=(P("dp", "mp"), P("dp", "mp")),
        check_vma=False,
    )
```

```python
import math

import jax
import jax.numpy as jnp
from jax import lax
from jax.experimental import pallas as pl
from jax.experimental.pallas import tpu as pltpu
from jax.sharding import PartitionSpec as P

HEAD_DIM = 128
EPSILON = 1e-06
MESH = pl.DeviceIdType.MESH
NZ, NY, NX = 8, 4, 4
ROWS, WIDTH, COLS, FEATS = 128, 4096, 512, 32
SLAB = WIDTH // NZ
HEADS = COLS // HEAD_DIM
A0, A1 = 384, 512
F32, BF16 = jnp.float32, jnp.bfloat16
SENDS, ARRIVALS = 48, 78


def kernel(tokens, cot, routes, counts, widths, shard, rows_out, grad_out,
           W, tokT, dW, proj, dl, D, hot, S, R1, R3, Rf, G, DXs, DXr,
           aZs, aZr, a1, aYs, aYr, a2, aXs, aXr,
           bXs, bXr, b1, bYs, bYr, cYs, cYr, c1, cXs, cXr, Zf, Zs, Zr,
           send_sem, recv_sem):
    me, m = lax.axis_index("dp"), lax.axis_index("mp")
    x, y, z = lax.rem(me, NX), lax.rem(me // NX, NY), me // (NX * NY)

    def device(zz, yy, xx, mm):
        return ((zz * NY + yy) * NX + xx, mm)

    place = {"x": (NX, x), "y": (NY, y), "z": (NZ, z)}

    def turn(axis, by):
        n, i = place[axis]
        return lax.rem(i + (by % n), n)

    def along(axis, by):
        j = turn(axis, by)
        return {"x": device(z, y, j, m), "y": device(z, j, x, m), "z": device(j, y, x, m)}[axis]

    partner = device(z, y, x, 1 - m)
    copies, groups = [], []

    class Group:
        def __init__(self, ref):
            self.ref, self.sem, self.bytes, self.done = ref, recv_sem.at[len(groups)], 0, False
            groups.append(self)

        def send(self, src, dst, to):
            at = len(copies)
            if at >= SENDS:
                copies[at - SENDS].wait_send()
            copy = pltpu.make_async_remote_copy(
                src_ref=src, dst_ref=dst, send_sem=send_sem.at[at % SENDS], recv_sem=self.sem,
                device_id=to, device_id_type=MESH)
            copy.start()
            copies.append(copy)
            self.bytes += math.prod(src.shape) * src.dtype.itemsize

        def wait(self):
            assert self.bytes == math.prod(self.ref.shape) * self.ref.dtype.itemsize
            self.done = True
            pltpu.make_async_remote_copy(
                src_ref=self.ref, dst_ref=self.ref, send_sem=send_sem.at[0], recv_sem=self.sem,
                device_id=partner, device_id_type=MESH).wait_recv()

    barrier = pltpu.get_barrier_semaphore()
    peers = [along(axis, o) for axis in "xyz" for o in range(1, place[axis][0])] + [partner]
    for peer in peers:
        pl.semaphore_signal(barrier, inc=1, device_id=peer, device_id_type=MESH)
    W[z, y, x] = shard[...]
    pl.semaphore_wait(barrier, len(peers))

    up, down = pl.ds(0, 16), pl.ds(16, 16)
    ca, cb = pl.ds(A0, A1 - A0), pl.ds(0, A0)
    every = pl.ds(0, 4)

    def span(half):
        return every if half is None else pl.ds(half * 2, 2)

    def ring(group, axis, k, region):
        halves = (0, 1) if k == place[axis][0] // 2 else (None, None)
        right, left = region(turn(axis, 1 - k), halves[0]), region(turn(axis, k - 1), halves[1])
        group.send(right, right, along(axis, 1))
        group.send(left, left, along(axis, -1))

    class Chunk:
        def __init__(self, q):
            self.q = q

        def near(self):
            q = self.q
            self.group = Group(W.at[pl.ds(0, 6), 0, 0, up, cb])
            upper, lower = W.at[q, y, x, up, cb], W.at[q, y, x, down, cb]
            for o in range(1, 4):
                self.group.send(upper, upper, along("y", o))
                self.group.send(lower, lower, along("x", o))

        def far(self, k):
            q = self.q
            self.group.wait()
            self.group = Group(W.at[pl.ds(0, 4 // k), every, 0, up, cb])
            ring(self.group, "x", k, lambda j, h: W.at[q, span(h), j, up, cb])
            ring(self.group, "y", k, lambda j, h: W.at[q, j, span(h), down, cb])

    chunks = [Chunk(turn("z", -o)) for o in range(NZ)]
    own_bc = W.at[z, y, x, :, cb]
    from_z = {}
    for o in (4, 3, 5, 2, 6, 1, 7):
        from_z[o] = Group(W.at[0, 0, 0, :, cb])
        from_z[o].send(own_bc, own_bc, along("z", o))
    chunks[0].near()
    own_a = W.at[z, y, x, :, ca]
    a_x = Group(W.at[pl.ds(0, 3), 0, 0, :, ca])
    for o in range(1, NX):
        a_x.send(own_a, own_a, along("x", o))

    def arrive(*offsets):
        for o in offsets:
            from_z[o].wait()
            chunks[o].near()

    def far(k, *offsets):
        for o in offsets:
            chunks[o].far(k)

    a_last = {}

    def a_far(k, first, last):
        if k > 1:
            a_last[first].wait()
        a_last[first] = Group(W.at[pl.ds(0, 1 if k == 4 else 2), pl.ds(0, last - first), every, :, ca])
        for oy in range(first, last):
            row = turn("y", -oy)
            ring(a_last[first], "z", k, lambda j, h: W.at[j, row, span(h), :, ca])

    named = jnp.broadcast_to(routes[...], (ROWS, ROWS))
    first_index = lax.broadcasted_iota(jnp.int32, (ROWS, ROWS), 0)
    second_index = lax.broadcasted_iota(jnp.int32, (ROWS, ROWS), 1)
    same = (named == named.astype(F32).T.astype(jnp.int32)) & (first_index < second_index)
    earlier = jnp.sum(same.astype(F32), axis=0, keepdims=True).astype(jnp.int32)
    slot = (routes[...] * 2 + earlier) * HEADS

    def prepare(s):
        tokT[s] = tokens[:, s * SLAB:(s + 1) * SLAB].T
        for h in range(HEADS):
            hot[s, :, h * ROWS:(h + 1) * ROWS] = (first_index + s * ROWS == slot + h).astype(F32).astype(BF16)

    def forward(o):
        q = chunks[o].q
        columns = pl.ds(pl.multiple_of(q * SLAB, SLAB), SLAB)
        term = jnp.dot(tokens[:, columns], W[q].reshape(SLAB, COLS), preferred_element_type=F32)
        if o == 0:
            proj[...] = term
        else:
            proj[...] += term

    a_x.wait()
    a_y = Group(W.at[pl.ds(0, 3), 0, every, :, ca])
    own_ay = W.at[z, y, every, :, ca]
    for o in range(1, NY):
        a_y.send(own_ay, own_ay, along("y", o))
    a_far(1, 0, 1)
    far(1, 0)
    arrive(1, 7)
    arrive(2, 6)
    a_y.wait()
    a_far(1, 1, 4)
    far(1, 1, 7)
    arrive(3, 5)
    a_far(2, 0, 1)
    far(2, 0)
    arrive(4)
    far(1, 2, 6)
    prepare(0)
    a_far(2, 1, 4)
    far(2, 1, 7)
    far(1, 3, 5)
    prepare(1)
    prepare(2)
    a_far(3, 0, 1)
    far(2, 2, 6)
    far(1, 4)
    prepare(3)
    prepare(4)
    a_far(3, 1, 4)
    a_far(4, 0, 1)
    far(2, 3, 5)
    far(2, 4)
    prepare(5)
    prepare(6)
    chunks[0].group.wait()
    forward(0)
    prepare(7)
    chunks[1].group.wait()
    forward(1)
    chunks[7].group.wait()
    forward(7)
    a_far(4, 1, 4)
    for o in (2, 6, 3, 5):
        chunks[o].group.wait()
        forward(o)
    a_last[0].wait()
    a_last[1].wait()
    chunks[4].group.wait()
    forward(4)

    position = lax.broadcasted_iota(jnp.int32, (ROWS, 1), 0)
    bound0 = counts[0, 0]
    bound1 = bound0 + counts[0, 1]
    bound2 = bound1 + counts[0, 2]
    row_width = jnp.where(position < bound0, widths[0], jnp.where(
        position < bound1, widths[1], jnp.where(position < bound2, widths[2], widths[3])))
    for h in range(HEADS):
        cols = slice(h * HEAD_DIM, (h + 1) * HEAD_DIM)
        own = proj[:, cols]
        inverse = 1.0 / jnp.sqrt(jnp.mean(own * own, axis=1, keepdims=True) + EPSILON)
        outputs = own * inverse
        head_mask = (m * HEADS + h < row_width).astype(F32)
        upstream = cot[:, cols].astype(F32) * head_mask
        delta = (upstream - outputs * jnp.mean(upstream * outputs, axis=1, keepdims=True)) * inverse
        dl[:, cols] = delta.astype(BF16)
        D[h * ROWS:(h + 1) * ROWS] = delta.astype(BF16)

    def reduce(group, axis, lead, t, local, sbuf, rbuf):
        n, half = place[axis][0], lead // 2
        for d in range(2):
            by = n // 2 - t + 1
            j = turn(axis, by if d == 0 else -by)

            def put(lo, hi, arrived):
                value = local(j, lo, hi)
                if arrived:
                    value += rbuf[d, t - 2, lo:hi].astype(F32)
                sbuf[d, t - 1, lo:hi] = value.astype(BF16)

            first = d * half
            part = pl.ds(0, lead)
            if t == 1:
                put(first, first + half, False)
                part = pl.ds(first, half)
            elif t == 2:
                put(first, first + half, True)
                put(half - first, lead - first, False)
            else:
                put(0, half, True)
                put(half, lead, True)
            group.send(sbuf.at[d, t - 1, part], rbuf.at[d, t - 1, part], along(axis, 1 if d == 0 else -1))

    def ring_sum(axis, lead, local, rbuf):
        n, i = place[axis]
        s = n // 2 - 1
        return (local(i, 0, lead) + rbuf[0, s].astype(F32)) + rbuf[1, s].astype(F32)

    def a_local(j, lo, hi):
        return dW[j, lo:hi, :, :, A0:A1]

    a_group = {}

    def a_step(t):
        if t > 1:
            a_group[t - 1].wait()
        a_group[t] = Group(aZr.at[0, 0] if t == 1 else aZr.at[:, 0])
        reduce(a_group[t], "z", NY, t, a_local, aZs, aZr)

    class Unit:
        def __init__(self, at, o):
            self.at, self.o, self.q = at, o, turn("z", -o)
            q = self.q
            self.b_local = lambda j, lo, hi: dW[q, lo:hi, j, 0:16, 0:A0]
            self.c_local = lambda j, lo, hi: dW[q, j, lo:hi, 16:32, 0:A0]

        def term(self):
            part = jnp.dot(tokT[self.q], dl[...], preferred_element_type=F32)
            dW[self.q] = part.reshape(NY, NX, FEATS, COLS)

        def step(self, t):
            at = self.at
            if t > 1:
                self.group.wait()
            self.group = Group(bXr.at[at, :, 0] if t == 1 else bXr.at[at])
            reduce(self.group, "x", NY, t, self.b_local, bXs.at[at], bXr.at[at])
            reduce(self.group, "y", NX, t, self.c_local, cYs.at[at], cYr.at[at])

        def near(self):
            at = self.at
            self.group.wait()
            self.group = Group(W.at[pl.ds(0, 6), 0, 0, up, cb])
            total = ring_sum("x", NY, self.b_local, bXr.at[at])
            b1[at] = total
            bYs[at] = total.astype(BF16)
            for o in range(1, 4):
                self.group.send(bYs.at[at, turn("y", o)], bYr.at[at, o - 1], along("y", o))
            total = ring_sum("y", NX, self.c_local, cYr.at[at])
            c1[at] = total
            cXs[at] = total.astype(BF16)
            for o in range(1, 4):
                self.group.send(cXs.at[at, turn("x", o)], cXr.at[at, o - 1], along("x", o))

        def across(self):
            at = self.at
            self.group.wait()
            for mine, arrived, rows, i in ((b1, bYr, slice(0, 16), y), (c1, cXr, slice(16, 32), x)):
                total = mine[at, i]
                for k in range(3):
                    total += arrived[at, k].astype(F32)
                if self.o == 0:
                    Zf[rows] = total
                else:
                    Zs[at, rows] = total.astype(BF16)
            if self.o:
                to_z.send(Zs.at[at], Zr.at[self.o - 1], along("z", -self.o))

    to_z = Group(Zr)
    units = [Unit(at, o) for at, o in enumerate((4, 3, 5, 2, 6, 1, 7, 0))]
    for unit in units[:4]:
        unit.term()
        unit.step(1)

    r_z = Group(R1.at[pl.ds(0, 7)])
    S_order = (4, 3, 5, 2, 6, 1, 7, 0)
    for o in S_order:
        j = turn("z", o)
        packed = jnp.dot(hot[j], D[...], preferred_element_type=F32)
        packed = packed.reshape(NY, NX, 8, HEAD_DIM).astype(BF16)
        if o:
            S[j] = packed
            r_z.send(S.at[j], R1.at[z], along("z", o))
        else:
            R1[z] = packed
    for unit in units[4:]:
        unit.term()
        unit.step(1)
    a_step(1)
    for unit in units[:4]:
        unit.step(2)
    a_step(2)
    all_z = pl.ds(0, NZ)
    r_z.wait()
    r_xy = Group(W.at[pl.ds(0, 5), pl.ds(0, 3), pl.ds(0, 2), :, ca])
    for oy in range(NY):
        for ox in range(NX):
            jy, jx = turn("y", oy), turn("x", ox)
            if oy or ox:
                r_xy.send(R1.at[all_z, jy, jx], R3.at[all_z, y, x], device(z, jy, jx, m))
    for s in range(NZ):
        R3[s, y, x] = R1[s, y, x]
    units[0].near()
    units[4].step(2)
    units[1].near()
    units[5].step(2)
    a_step(3)
    units[2].near()
    units[6].step(2)
    units[0].across()
    units[3].near()
    units[7].step(2)
    units[1].across()
    units[4].near()
    units[2].across()
    a_step(4)

    r_xy.wait()
    Rf[...] = R3[...].astype(F32).reshape(8 * ROWS, HEAD_DIM)
    for h in range(HEADS):
        G[:, h * HEAD_DIM:(h + 1) * HEAD_DIM] = Rf[pl.ds(h, 2 * ROWS, stride=HEADS), :].astype(BF16)

    def product(tile):
        return lax.dot_general(G[...], W[tile].reshape(SLAB, COLS), (((1,), (1,)), ((), ())),
                               preferred_element_type=F32).astype(BF16)

    halves = []

    def give(t):
        DXs[t] = product((1 - m) * 4 + t)
        group = Group(DXr.at[t])
        group.send(DXs.at[t], DXr.at[t], partner)
        halves.append(group)

    def take(t):
        own = product(m * 4 + t).astype(F32)
        halves[t].wait()
        rows_out[:, t * SLAB:(t + 1) * SLAB] = (own + DXr[t].astype(F32)).astype(BF16)

    give(0)
    units[5].near()
    units[3].across()
    give(1)
    units[6].near()
    units[4].across()
    a_group[4].wait()
    total = ring_sum("z", NY, a_local, aZr)
    a1[...] = total
    aYs[...] = total.astype(BF16)
    ra_y = Group(aYr)
    for o in range(1, NY):
        ra_y.send(aYs.at[turn("y", o)], aYr.at[o - 1], along("y", o))
    units[7].near()
    units[5].across()
    give(2)
    units[6].across()
    give(3)
    ra_y.wait()
    total = a1[y]
    for o in range(NY - 1):
        total += aYr[o].astype(F32)
    a2[...] = total
    aXs[...] = total.astype(BF16)
    ra_x = Group(aXr)
    for o in range(1, NX):
        ra_x.send(aXs.at[turn("x", o)], aXr.at[o - 1], along("x", o))
    units[7].across()
    for t in range(4):
        take(t)
    scale = 1.0 / 128.0
    to_z.wait()
    total = Zf[...]
    for o in range(NZ - 1):
        total += Zr[o].astype(F32)
    grad_out[:, 0:A0] = total * scale
    ra_x.wait()
    total = a2[x]
    for o in range(NX - 1):
        total += aXr[o].astype(F32)
    grad_out[:, A0:A1] = total * scale
    assert len(groups) == ARRIVALS
    for copy in copies[-SENDS:]:
        copy.wait_send()


def per_device(tokens, key_cot, routes, counts, widths, key_weight):
    vmem = pl.BlockSpec(memory_space=pltpu.VMEM)
    smem = pl.BlockSpec(memory_space=pltpu.SMEM)
    buffers = [
        ((NZ, NY, NX, FEATS, COLS), BF16),
        ((NZ, SLAB, ROWS), BF16),
        ((NZ, NY, NX, FEATS, COLS), F32),
        ((ROWS, COLS), F32),
        ((ROWS, COLS), BF16),
        ((HEADS * ROWS, HEAD_DIM), BF16),
        ((NZ, ROWS, HEADS * ROWS), BF16),
        ((NZ, NY, NX, 8, HEAD_DIM), BF16),
        ((NZ, NY, NX, 8, HEAD_DIM), BF16),
        ((NZ, NY, NX, 8, HEAD_DIM), BF16),
        ((8 * ROWS, HEAD_DIM), F32),
        ((2 * ROWS, COLS), BF16),
        ((4, 2 * ROWS, SLAB), BF16),
        ((4, 2 * ROWS, SLAB), BF16),
        ((2, 4, NY, NX, FEATS, 128), BF16),
        ((2, 4, NY, NX, FEATS, 128), BF16),
        ((NY, NX, FEATS, 128), F32),
        ((NY, NX, FEATS, 128), BF16),
        ((NY - 1, NX, FEATS, 128), BF16),
        ((NX, FEATS, 128), F32),
        ((NX, FEATS, 128), BF16),
        ((NX - 1, FEATS, 128), BF16),
        ((NZ, 2, 2, NY, 16, 384), BF16),
        ((NZ, 2, 2, NY, 16, 384), BF16),
        ((NZ, NY, 16, 384), F32),
        ((NZ, NY, 16, 384), BF16),
        ((NZ, NY - 1, 16, 384), BF16),
        ((NZ, 2, 2, NX, 16, 384), BF16),
        ((NZ, 2, 2, NX, 16, 384), BF16),
        ((NZ, NX, 16, 384), F32),
        ((NZ, NX, 16, 384), BF16),
        ((NZ, NX - 1, 16, 384), BF16),
        ((FEATS, 384), F32),
        ((NZ, FEATS, 384), BF16),
        ((NZ - 1, FEATS, 384), BF16),
    ]
    return pl.pallas_call(
        kernel,
        out_shape=(jax.ShapeDtypeStruct((2 * ROWS, WIDTH // 2), BF16), jax.ShapeDtypeStruct((FEATS, COLS), F32)),
        in_specs=[vmem, vmem, vmem, smem, smem, vmem],
        out_specs=(vmem, vmem),
        scratch_shapes=[pltpu.VMEM(shape, dtype) for shape, dtype in buffers]
        + [pltpu.SemaphoreType.DMA((SENDS,)), pltpu.SemaphoreType.DMA((ARRIVALS,))],
        compiler_params=pltpu.CompilerParams(
            collective_id=0, has_side_effects=True, vmem_limit_bytes=58 << 20),
    )(tokens, key_cot, routes.reshape(1, ROWS), counts, widths, key_weight)


def solution(mesh):
    return jax.shard_map(
        per_device,
        mesh=mesh,
        in_specs=(P("dp", None), P("dp", "mp"), P("dp", None), P("dp", None), P(), P("dp", "mp")),
        out_specs=(P("dp", "mp"), P("dp", "mp")),
        check_vma=False,
    )
```

```python
import math

import jax
import jax.numpy as jnp
from jax import lax
from jax.experimental import pallas as pl
from jax.experimental.pallas import tpu as pltpu
from jax.sharding import PartitionSpec as P

HEAD_DIM = 128
EPSILON = 1e-06
MESH = pl.DeviceIdType.MESH
NZ, NY, NX = 8, 4, 4
ROWS, WIDTH, COLS, FEATS = 128, 4096, 512, 32
SLAB = WIDTH // NZ
HEADS = COLS // HEAD_DIM
A0, A1 = 384, 512
F32, BF16 = jnp.float32, jnp.bfloat16
SENDS, ARRIVALS = 48, 78


def kernel(tokens, cot, routes, counts, widths, shard, rows_out, grad_out,
           W, tokT, dW, proj, dl, D, hot, S, R1, R3, Rf, G, DXs, DXr,
           aZs, aZr, a1, aYs, aYr, a2, aXs, aXr,
           bXs, bXr, b1, bYs, bYr, cYs, cYr, c1, cXs, cXr, Zf, Zs, Zr,
           send_sem, recv_sem):
    me, m = lax.axis_index("dp"), lax.axis_index("mp")
    x, y, z = lax.rem(me, NX), lax.rem(me // NX, NY), me // (NX * NY)

    def device(zz, yy, xx, mm):
        return ((zz * NY + yy) * NX + xx, mm)

    place = {"x": (NX, x), "y": (NY, y), "z": (NZ, z)}

    def turn(axis, by):
        n, i = place[axis]
        return lax.rem(i + (by % n), n)

    def along(axis, by):
        j = turn(axis, by)
        return {"x": device(z, y, j, m), "y": device(z, j, x, m), "z": device(j, y, x, m)}[axis]

    partner = device(z, y, x, 1 - m)
    copies, groups = [], []

    class Group:
        def __init__(self, ref):
            self.ref, self.sem, self.bytes, self.done = ref, recv_sem.at[len(groups)], 0, False
            groups.append(self)

        def send(self, src, dst, to):
            at = len(copies)
            if at >= SENDS:
                copies[at - SENDS].wait_send()
            copy = pltpu.make_async_remote_copy(
                src_ref=src, dst_ref=dst, send_sem=send_sem.at[at % SENDS], recv_sem=self.sem,
                device_id=to, device_id_type=MESH)
            copy.start()
            copies.append(copy)
            self.bytes += math.prod(src.shape) * src.dtype.itemsize

        def wait(self):
            assert self.bytes == math.prod(self.ref.shape) * self.ref.dtype.itemsize
            self.done = True
            pltpu.make_async_remote_copy(
                src_ref=self.ref, dst_ref=self.ref, send_sem=send_sem.at[0], recv_sem=self.sem,
                device_id=partner, device_id_type=MESH).wait_recv()

    barrier = pltpu.get_barrier_semaphore()
    peers = [along(axis, o) for axis in "xyz" for o in range(1, place[axis][0])] + [partner]
    for peer in peers:
        pl.semaphore_signal(barrier, inc=1, device_id=peer, device_id_type=MESH)
    W[z, y, x] = shard[...]
    pl.semaphore_wait(barrier, len(peers))

    up, down = pl.ds(0, 16), pl.ds(16, 16)
    ca, cb = pl.ds(A0, A1 - A0), pl.ds(0, A0)
    every = pl.ds(0, 4)

    def span(half):
        return every if half is None else pl.ds(half * 2, 2)

    def ring(group, axis, k, region):
        halves = (0, 1) if k == place[axis][0] // 2 else (None, None)
        right, left = region(turn(axis, 1 - k), halves[0]), region(turn(axis, k - 1), halves[1])
        group.send(right, right, along(axis, 1))
        group.send(left, left, along(axis, -1))

    class Chunk:
        def __init__(self, q):
            self.q = q

        def near(self):
            q = self.q
            self.group = Group(W.at[pl.ds(0, 6), 0, 0, up, cb])
            upper, lower = W.at[q, y, x, up, cb], W.at[q, y, x, down, cb]
            for o in range(1, 4):
                self.group.send(upper, upper, along("y", o))
                self.group.send(lower, lower, along("x", o))

        def far(self, k):
            q = self.q
            self.group.wait()
            self.group = Group(W.at[pl.ds(0, 4 // k), every, 0, up, cb])
            ring(self.group, "x", k, lambda j, h: W.at[q, span(h), j, up, cb])
            ring(self.group, "y", k, lambda j, h: W.at[q, j, span(h), down, cb])

    chunks = [Chunk(turn("z", -o)) for o in range(NZ)]
    own_bc = W.at[z, y, x, :, cb]
    from_z = {}
    for o in (4, 3, 5, 2, 6, 1, 7):
        from_z[o] = Group(W.at[0, 0, 0, :, cb])
        from_z[o].send(own_bc, own_bc, along("z", o))
    chunks[0].near()
    own_a = W.at[z, y, x, :, ca]
    a_x = Group(W.at[pl.ds(0, 3), 0, 0, :, ca])
    for o in range(1, NX):
        a_x.send(own_a, own_a, along("x", o))

    def arrive(*offsets):
        for o in offsets:
            from_z[o].wait()
            chunks[o].near()

    def far(k, *offsets):
        for o in offsets:
            chunks[o].far(k)

    a_last = {}

    def a_far(k, first, last):
        if k > 1:
            a_last[first].wait()
        a_last[first] = Group(W.at[pl.ds(0, 1 if k == 4 else 2), pl.ds(0, last - first), every, :, ca])
        for oy in range(first, last):
            row = turn("y", -oy)
            ring(a_last[first], "z", k, lambda j, h: W.at[j, row, span(h), :, ca])

    named = jnp.broadcast_to(routes[...], (ROWS, ROWS))
    first_index = lax.broadcasted_iota(jnp.int32, (ROWS, ROWS), 0)
    second_index = lax.broadcasted_iota(jnp.int32, (ROWS, ROWS), 1)
    same = (named == named.astype(F32).T.astype(jnp.int32)) & (first_index < second_index)
    earlier = jnp.sum(same.astype(F32), axis=0, keepdims=True).astype(jnp.int32)
    slot = (routes[...] * 2 + earlier) * HEADS

    def prepare(s):
        tokT[s] = tokens[:, s * SLAB:(s + 1) * SLAB].T
        for h in range(HEADS):
            hot[s, :, h * ROWS:(h + 1) * ROWS] = (first_index + s * ROWS == slot + h).astype(F32).astype(BF16)

    started = []

    def forward(o):
        q = chunks[o].q
        columns = pl.ds(pl.multiple_of(q * SLAB, SLAB), SLAB)
        term = jnp.dot(tokens[:, columns], W[q].reshape(SLAB, COLS), preferred_element_type=F32)
        if not started:
            started.append(o)
            proj[...] = term
        else:
            proj[...] += term

    a_y = Group(W.at[pl.ds(0, 3), 0, every, :, ca])

    def a_row():
        a_x.wait()
        own = W.at[z, y, every, :, ca]
        for o in range(1, NY):
            a_y.send(own, own, along("y", o))

    position = lax.broadcasted_iota(jnp.int32, (ROWS, 1), 0)
    bound0 = counts[0, 0]
    bound1 = bound0 + counts[0, 1]
    bound2 = bound1 + counts[0, 2]
    row_width = jnp.where(position < bound0, widths[0], jnp.where(
        position < bound1, widths[1], jnp.where(position < bound2, widths[2], widths[3])))

    def norm_grads():
        for h in range(HEADS):
            cols = slice(h * HEAD_DIM, (h + 1) * HEAD_DIM)
            own = proj[:, cols]
            inverse = 1.0 / jnp.sqrt(jnp.mean(own * own, axis=1, keepdims=True) + EPSILON)
            outputs = own * inverse
            head_mask = (m * HEADS + h < row_width).astype(F32)
            upstream = cot[:, cols].astype(F32) * head_mask
            delta = (upstream - outputs * jnp.mean(upstream * outputs, axis=1, keepdims=True)) * inverse
            dl[:, cols] = delta.astype(BF16)
            D[h * ROWS:(h + 1) * ROWS] = delta.astype(BF16)

    def reduce(group, axis, lead, t, local, sbuf, rbuf):
        n, half = place[axis][0], lead // 2
        for d in range(2):
            by = n // 2 - t + 1
            j = turn(axis, by if d == 0 else -by)

            def put(lo, hi, arrived):
                value = local(j, lo, hi)
                if arrived:
                    value += rbuf[d, t - 2, lo:hi].astype(F32)
                sbuf[d, t - 1, lo:hi] = value.astype(BF16)

            first = d * half
            part = pl.ds(0, lead)
            if t == 1:
                put(first, first + half, False)
                part = pl.ds(first, half)
            elif t == 2:
                put(first, first + half, True)
                put(half - first, lead - first, False)
            else:
                put(0, half, True)
                put(half, lead, True)
            group.send(sbuf.at[d, t - 1, part], rbuf.at[d, t - 1, part], along(axis, 1 if d == 0 else -1))

    def ring_sum(axis, lead, local, rbuf):
        n, i = place[axis]
        s = n // 2 - 1
        return (local(i, 0, lead) + rbuf[0, s].astype(F32)) + rbuf[1, s].astype(F32)

    def a_local(j, lo, hi):
        return dW[j, lo:hi, :, :, A0:A1]

    a_group = {}

    def a_step(t):
        if t > 1:
            a_group[t - 1].wait()
        a_group[t] = Group(aZr.at[0, 0] if t == 1 else aZr.at[:, 0])
        reduce(a_group[t], "z", NY, t, a_local, aZs, aZr)

    class Unit:
        def __init__(self, at, o):
            self.at, self.o, self.q = at, o, turn("z", -o)
            q = self.q
            self.b_local = lambda j, lo, hi: dW[q, lo:hi, j, 0:16, 0:A0]
            self.c_local = lambda j, lo, hi: dW[q, j, lo:hi, 16:32, 0:A0]

        def term(self):
            part = jnp.dot(tokT[self.q], dl[...], preferred_element_type=F32)
            dW[self.q] = part.reshape(NY, NX, FEATS, COLS)

        def step(self, t):
            at = self.at
            if t > 1:
                self.group.wait()
            self.group = Group(bXr.at[at, :, 0] if t == 1 else bXr.at[at])
            reduce(self.group, "x", NY, t, self.b_local, bXs.at[at], bXr.at[at])
            reduce(self.group, "y", NX, t, self.c_local, cYs.at[at], cYr.at[at])

        def near(self):
            at = self.at
            self.group.wait()
            self.group = Group(W.at[pl.ds(0, 6), 0, 0, up, cb])
            total = ring_sum("x", NY, self.b_local, bXr.at[at])
            b1[at] = total
            bYs[at] = total.astype(BF16)
            for o in range(1, 4):
                self.group.send(bYs.at[at, turn("y", o)], bYr.at[at, o - 1], along("y", o))
            total = ring_sum("y", NX, self.c_local, cYr.at[at])
            c1[at] = total
            cXs[at] = total.astype(BF16)
            for o in range(1, 4):
                self.group.send(cXs.at[at, turn("x", o)], cXr.at[at, o - 1], along("x", o))

        def across(self):
            at = self.at
            self.group.wait()
            for mine, arrived, rows, i in ((b1, bYr, slice(0, 16), y), (c1, cXr, slice(16, 32), x)):
                total = mine[at, i]
                for k in range(3):
                    total += arrived[at, k].astype(F32)
                if self.o == 0:
                    Zf[rows] = total
                else:
                    Zs[at, rows] = total.astype(BF16)
            if self.o:
                to_z.send(Zs.at[at], Zr.at[self.o - 1], along("z", -self.o))

    to_z = Group(Zr)
    units = [Unit(at, o) for at, o in enumerate((4, 3, 5, 2, 6, 1, 7, 0))]

    r_z = Group(R1.at[pl.ds(0, 7)])
    r_xy = Group(W.at[pl.ds(0, 5), pl.ds(0, 3), pl.ds(0, 2), :, ca])
    all_z = pl.ds(0, NZ)

    def pack(o):
        j = turn("z", o)
        packed = jnp.dot(hot[j], D[...], preferred_element_type=F32)
        packed = packed.reshape(NY, NX, 8, HEAD_DIM).astype(BF16)
        if o:
            S[j] = packed
            r_z.send(S.at[j], R1.at[z], along("z", o))
        else:
            R1[z] = packed

    def route_plane():
        r_z.wait()
        for oy in range(NY):
            for ox in range(NX):
                jy, jx = turn("y", oy), turn("x", ox)
                if oy or ox:
                    r_xy.send(R1.at[all_z, jy, jx], R3.at[all_z, y, x], device(z, jy, jx, m))
        for s in range(NZ):
            R3[s, y, x] = R1[s, y, x]

    def unpack():
        r_xy.wait()
        Rf[...] = R3[...].astype(F32).reshape(8 * ROWS, HEAD_DIM)
        for h in range(HEADS):
            G[:, h * HEAD_DIM:(h + 1) * HEAD_DIM] = Rf[pl.ds(h, 2 * ROWS, stride=HEADS), :].astype(BF16)

    def product(tile):
        return lax.dot_general(G[...], W[tile].reshape(SLAB, COLS), (((1,), (1,)), ((), ())),
                               preferred_element_type=F32).astype(BF16)

    halves = []

    def give(t):
        DXs[t] = product((1 - m) * 4 + t)
        group = Group(DXr.at[t])
        group.send(DXs.at[t], DXr.at[t], partner)
        halves.append(group)

    def take(t):
        own = product(m * 4 + t).astype(F32)
        halves[t].wait()
        rows_out[:, t * SLAB:(t + 1) * SLAB] = (own + DXr[t].astype(F32)).astype(BF16)

    ra_y, ra_x = Group(aYr), Group(aXr)
    scale = 1.0 / 128.0

    def a_over_y():
        a_group[4].wait()
        total = ring_sum("z", NY, a_local, aZr)
        a1[...] = total
        aYs[...] = total.astype(BF16)
        for o in range(1, NY):
            ra_y.send(aYs.at[turn("y", o)], aYr.at[o - 1], along("y", o))

    def a_over_x():
        ra_y.wait()
        total = a1[y]
        for o in range(NY - 1):
            total += aYr[o].astype(F32)
        a2[...] = total
        aXs[...] = total.astype(BF16)
        for o in range(1, NX):
            ra_x.send(aXs.at[turn("x", o)], aXr.at[o - 1], along("x", o))

    def finish_bc():
        to_z.wait()
        total = Zf[...]
        for o in range(NZ - 1):
            total += Zr[o].astype(F32)
        grad_out[:, 0:A0] = total * scale

    def finish_a():
        ra_x.wait()
        total = a2[x]
        for o in range(NX - 1):
            total += aXr[o].astype(F32)
        grad_out[:, A0:A1] = total * scale

    prepare(4)
    a_row()
    chunks[0].far(1)
    a_far(1, 0, 1)
    prepare(0)
    arrive(4)
    arrive(6)
    arrive(7)
    arrive(1)
    a_far(2, 0, 1)
    arrive(3)
    a_y.wait()
    a_far(1, 1, 4)
    arrive(2)
    prepare(6)
    chunks[0].far(2)
    arrive(5)
    a_far(3, 0, 1)
    chunks[4].far(1)
    prepare(1)
    chunks[6].far(1)
    chunks[3].far(1)
    a_far(2, 1, 4)
    prepare(7)
    chunks[2].far(1)
    prepare(5)
    chunks[1].far(1)
    chunks[7].far(1)
    chunks[5].far(1)
    chunks[3].far(2)
    a_far(3, 1, 4)
    a_far(4, 0, 1)
    chunks[2].far(2)
    prepare(3)
    chunks[1].far(2)
    chunks[6].far(2)
    chunks[0].group.wait()
    forward(0)
    chunks[4].far(2)
    chunks[5].far(2)
    chunks[7].far(2)
    a_far(4, 1, 4)
    chunks[4].group.wait()
    chunks[6].group.wait()
    forward(6)
    chunks[3].group.wait()
    forward(3)
    chunks[5].group.wait()
    forward(5)
    chunks[1].group.wait()
    forward(1)
    chunks[2].group.wait()
    forward(2)
    prepare(2)
    chunks[7].group.wait()
    forward(7)
    a_last[0].wait()
    a_last[1].wait()
    forward(4)
    norm_grads()
    pack(4)
    units[4].term()
    units[2].term()
    units[1].term()
    units[3].term()
    units[0].term()
    units[5].term()
    units[7].term()
    units[6].term()
    a_step(1)
    units[1].step(1)
    units[4].step(1)
    units[3].step(1)
    pack(5)
    pack(3)
    units[6].step(1)
    units[7].step(1)
    pack(0)
    units[0].step(1)
    units[1].step(2)
    a_step(2)
    pack(6)
    units[2].step(1)
    units[5].step(1)
    units[4].step(2)
    pack(2)
    units[6].step(2)
    units[1].near()
    pack(1)
    units[3].step(2)
    pack(7)
    units[2].step(2)
    a_step(3)
    units[5].step(2)
    units[0].step(2)
    units[4].near()
    route_plane()
    a_step(4)
    units[2].near()
    units[5].near()
    units[3].near()
    units[0].near()
    units[1].across()
    units[7].step(2)
    units[6].near()
    a_over_y()
    units[2].across()
    unpack()
    give(0)
    units[0].across()
    units[5].across()
    units[4].across()
    give(1)
    give(2)
    units[3].across()
    units[7].near()
    give(3)
    units[6].across()
    a_over_x()
    take(0)
    take(1)
    take(2)
    take(3)
    units[7].across()
    finish_bc()
    finish_a()
    assert len(groups) == ARRIVALS
    for copy in copies[-SENDS:]:
        copy.wait_send()


def per_device(tokens, key_cot, routes, counts, widths, key_weight):
    vmem = pl.BlockSpec(memory_space=pltpu.VMEM)
    smem = pl.BlockSpec(memory_space=pltpu.SMEM)
    buffers = [
        ((NZ, NY, NX, FEATS, COLS), BF16),
        ((NZ, SLAB, ROWS), BF16),
        ((NZ, NY, NX, FEATS, COLS), F32),
        ((ROWS, COLS), F32),
        ((ROWS, COLS), BF16),
        ((HEADS * ROWS, HEAD_DIM), BF16),
        ((NZ, ROWS, HEADS * ROWS), BF16),
        ((NZ, NY, NX, 8, HEAD_DIM), BF16),
        ((NZ, NY, NX, 8, HEAD_DIM), BF16),
        ((NZ, NY, NX, 8, HEAD_DIM), BF16),
        ((8 * ROWS, HEAD_DIM), F32),
        ((2 * ROWS, COLS), BF16),
        ((4, 2 * ROWS, SLAB), BF16),
        ((4, 2 * ROWS, SLAB), BF16),
        ((2, 4, NY, NX, FEATS, 128), BF16),
        ((2, 4, NY, NX, FEATS, 128), BF16),
        ((NY, NX, FEATS, 128), F32),
        ((NY, NX, FEATS, 128), BF16),
        ((NY - 1, NX, FEATS, 128), BF16),
        ((NX, FEATS, 128), F32),
        ((NX, FEATS, 128), BF16),
        ((NX - 1, FEATS, 128), BF16),
        ((NZ, 2, 2, NY, 16, 384), BF16),
        ((NZ, 2, 2, NY, 16, 384), BF16),
        ((NZ, NY, 16, 384), F32),
        ((NZ, NY, 16, 384), BF16),
        ((NZ, NY - 1, 16, 384), BF16),
        ((NZ, 2, 2, NX, 16, 384), BF16),
        ((NZ, 2, 2, NX, 16, 384), BF16),
        ((NZ, NX, 16, 384), F32),
        ((NZ, NX, 16, 384), BF16),
        ((NZ, NX - 1, 16, 384), BF16),
        ((FEATS, 384), F32),
        ((NZ, FEATS, 384), BF16),
        ((NZ - 1, FEATS, 384), BF16),
    ]
    return pl.pallas_call(
        kernel,
        out_shape=(jax.ShapeDtypeStruct((2 * ROWS, WIDTH // 2), BF16), jax.ShapeDtypeStruct((FEATS, COLS), F32)),
        in_specs=[vmem, vmem, vmem, smem, smem, vmem],
        out_specs=(vmem, vmem),
        scratch_shapes=[pltpu.VMEM(shape, dtype) for shape, dtype in buffers]
        + [pltpu.SemaphoreType.DMA((SENDS,)), pltpu.SemaphoreType.DMA((ARRIVALS,))],
        compiler_params=pltpu.CompilerParams(
            collective_id=0, has_side_effects=True, vmem_limit_bytes=58 << 20),
    )(tokens, key_cot, routes.reshape(1, ROWS), counts, widths, key_weight)


def solution(mesh):
    return jax.shard_map(
        per_device,
        mesh=mesh,
        in_specs=(P("dp", None), P("dp", "mp"), P("dp", None), P("dp", None), P(), P("dp", "mp")),
        out_specs=(P("dp", "mp"), P("dp", "mp")),
        check_vma=False,
    )
```

```python
import math

import jax
import jax.numpy as jnp
from jax import lax
from jax.experimental import pallas as pl
from jax.experimental.pallas import tpu as pltpu
from jax.sharding import PartitionSpec as P

HEAD_DIM = 128
EPSILON = 1e-06
MESH = pl.DeviceIdType.MESH
NZ, NY, NX = 8, 4, 4
ROWS, WIDTH, COLS, FEATS = 128, 4096, 512, 32
SLAB = WIDTH // NZ
HEADS = COLS // HEAD_DIM
A0, A1 = 384, 512
F32, BF16 = jnp.float32, jnp.bfloat16
SENDS, ARRIVALS = 48, 78


def kernel(tokens_in, cot, routes, counts, widths, shard, rows_out, grad_out,
           tokens, rows, W, tokT, dW, proj, dl, D, hot, S, R1, R3, Rf, G, DXs, DXr,
           aZs, aZr, a1, aYs, aYr, a2, aXs, aXr,
           bXs, bXr, b1, bYs, bYr, cYs, cYr, c1, cXs, cXr, Zf, Zs, Zr,
           local_sem, send_sem, recv_sem):
    me, m = lax.axis_index("dp"), lax.axis_index("mp")
    x, y, z = lax.rem(me, NX), lax.rem(me // NX, NY), me // (NX * NY)

    def device(zz, yy, xx, mm):
        return ((zz * NY + yy) * NX + xx, mm)

    place = {"x": (NX, x), "y": (NY, y), "z": (NZ, z)}

    def turn(axis, by):
        n, i = place[axis]
        return lax.rem(i + (by % n), n)

    def along(axis, by):
        j = turn(axis, by)
        return {"x": device(z, y, j, m), "y": device(z, j, x, m), "z": device(j, y, x, m)}[axis]

    partner = device(z, y, x, 1 - m)
    copies, groups = [], []

    class Group:
        def __init__(self, ref):
            self.ref, self.sem, self.bytes, self.done = ref, recv_sem.at[len(groups)], 0, False
            groups.append(self)

        def send(self, src, dst, to):
            at = len(copies)
            if at >= SENDS:
                copies[at - SENDS].wait_send()
            copy = pltpu.make_async_remote_copy(
                src_ref=src, dst_ref=dst, send_sem=send_sem.at[at % SENDS], recv_sem=self.sem,
                device_id=to, device_id_type=MESH)
            copy.start()
            copies.append(copy)
            self.bytes += math.prod(src.shape) * src.dtype.itemsize

        def wait(self):
            assert self.bytes == math.prod(self.ref.shape) * self.ref.dtype.itemsize
            self.done = True
            pltpu.make_async_remote_copy(
                src_ref=self.ref, dst_ref=self.ref, send_sem=send_sem.at[0], recv_sem=self.sem,
                device_id=partner, device_id_type=MESH).wait_recv()

    fetch = pltpu.make_async_copy(tokens_in, tokens, local_sem.at[0])
    fetch.start()

    barrier = pltpu.get_barrier_semaphore()
    peers = [along(axis, o) for axis in "xyz" for o in range(1, place[axis][0])] + [partner]
    for peer in peers:
        pl.semaphore_signal(barrier, inc=1, device_id=peer, device_id_type=MESH)
    W[z, y, x] = shard[...]
    pl.semaphore_wait(barrier, len(peers))

    up, down = pl.ds(0, 16), pl.ds(16, 16)
    ca, cb = pl.ds(A0, A1 - A0), pl.ds(0, A0)
    every = pl.ds(0, 4)

    def span(half):
        return every if half is None else pl.ds(half * 2, 2)

    def ring(group, axis, k, region):
        halves = (0, 1) if k == place[axis][0] // 2 else (None, None)
        right, left = region(turn(axis, 1 - k), halves[0]), region(turn(axis, k - 1), halves[1])
        group.send(right, right, along(axis, 1))
        group.send(left, left, along(axis, -1))

    class Chunk:
        def __init__(self, q):
            self.q = q

        def near(self):
            q = self.q
            self.group = Group(W.at[pl.ds(0, 6), 0, 0, up, cb])
            upper, lower = W.at[q, y, x, up, cb], W.at[q, y, x, down, cb]
            for o in range(1, 4):
                self.group.send(upper, upper, along("y", o))
                self.group.send(lower, lower, along("x", o))

        def far(self, k):
            q = self.q
            self.group.wait()
            self.group = Group(W.at[pl.ds(0, 4 // k), every, 0, up, cb])
            ring(self.group, "x", k, lambda j, h: W.at[q, span(h), j, up, cb])
            ring(self.group, "y", k, lambda j, h: W.at[q, j, span(h), down, cb])

    chunks = [Chunk(turn("z", -o)) for o in range(NZ)]
    own_bc = W.at[z, y, x, :, cb]
    from_z = {}
    for o in (4, 3, 5, 2, 6, 1, 7):
        from_z[o] = Group(W.at[0, 0, 0, :, cb])
        from_z[o].send(own_bc, own_bc, along("z", o))
    chunks[0].near()
    own_a = W.at[z, y, x, :, ca]
    a_x = Group(W.at[pl.ds(0, 3), 0, 0, :, ca])
    for o in range(1, NX):
        a_x.send(own_a, own_a, along("x", o))

    def arrive(*offsets):
        for o in offsets:
            from_z[o].wait()
            chunks[o].near()

    def far(k, *offsets):
        for o in offsets:
            chunks[o].far(k)

    a_last = {}

    def a_far(k, first, last):
        if k > 1:
            a_last[first].wait()
        a_last[first] = Group(W.at[pl.ds(0, 1 if k == 4 else 2), pl.ds(0, last - first), every, :, ca])
        for oy in range(first, last):
            row = turn("y", -oy)
            ring(a_last[first], "z", k, lambda j, h: W.at[j, row, span(h), :, ca])

    named = jnp.broadcast_to(routes[...], (ROWS, ROWS))
    first_index = lax.broadcasted_iota(jnp.int32, (ROWS, ROWS), 0)
    second_index = lax.broadcasted_iota(jnp.int32, (ROWS, ROWS), 1)
    same = (named == named.astype(F32).T.astype(jnp.int32)) & (first_index < second_index)
    earlier = jnp.sum(same.astype(F32), axis=0, keepdims=True).astype(jnp.int32)
    slot = (routes[...] * 2 + earlier) * HEADS

    def prepare(s):
        tokT[s] = tokens[:, s * SLAB:(s + 1) * SLAB].T
        for h in range(HEADS):
            hot[s, :, h * ROWS:(h + 1) * ROWS] = (first_index + s * ROWS == slot + h).astype(F32).astype(BF16)

    started = []

    def forward(o):
        q = chunks[o].q
        columns = pl.ds(pl.multiple_of(q * SLAB, SLAB), SLAB)
        term = jnp.dot(tokens[:, columns], W[q].reshape(SLAB, COLS), preferred_element_type=F32)
        if not started:
            started.append(o)
            proj[...] = term
        else:
            proj[...] += term

    a_y = Group(W.at[pl.ds(0, 3), 0, every, :, ca])

    def a_row():
        a_x.wait()
        own = W.at[z, y, every, :, ca]
        for o in range(1, NY):
            a_y.send(own, own, along("y", o))

    position = lax.broadcasted_iota(jnp.int32, (ROWS, 1), 0)
    bound0 = counts[0, 0]
    bound1 = bound0 + counts[0, 1]
    bound2 = bound1 + counts[0, 2]
    row_width = jnp.where(position < bound0, widths[0], jnp.where(
        position < bound1, widths[1], jnp.where(position < bound2, widths[2], widths[3])))

    def norm_grads():
        for h in range(HEADS):
            cols = slice(h * HEAD_DIM, (h + 1) * HEAD_DIM)
            own = proj[:, cols]
            inverse = 1.0 / jnp.sqrt(jnp.mean(own * own, axis=1, keepdims=True) + EPSILON)
            outputs = own * inverse
            head_mask = (m * HEADS + h < row_width).astype(F32)
            upstream = cot[:, cols].astype(F32) * head_mask
            delta = (upstream - outputs * jnp.mean(upstream * outputs, axis=1, keepdims=True)) * inverse
            dl[:, cols] = delta.astype(BF16)
            D[h * ROWS:(h + 1) * ROWS] = delta.astype(BF16)

    def reduce(group, axis, lead, t, local, sbuf, rbuf):
        n, half = place[axis][0], lead // 2
        for d in range(2):
            by = n // 2 - t + 1
            j = turn(axis, by if d == 0 else -by)

            def put(lo, hi, arrived):
                value = local(j, lo, hi)
                if arrived:
                    value += rbuf[d, t - 2, lo:hi].astype(F32)
                sbuf[d, t - 1, lo:hi] = value.astype(BF16)

            first = d * half
            part = pl.ds(0, lead)
            if t == 1:
                put(first, first + half, False)
                part = pl.ds(first, half)
            elif t == 2:
                put(first, first + half, True)
                put(half - first, lead - first, False)
            else:
                put(0, half, True)
                put(half, lead, True)
            group.send(sbuf.at[d, t - 1, part], rbuf.at[d, t - 1, part], along(axis, 1 if d == 0 else -1))

    def ring_sum(axis, lead, local, rbuf):
        n, i = place[axis]
        s = n // 2 - 1
        return (local(i, 0, lead) + rbuf[0, s].astype(F32)) + rbuf[1, s].astype(F32)

    def a_local(j, lo, hi):
        return dW[j, lo:hi, :, :, A0:A1]

    a_group = {}

    def a_step(t):
        if t > 1:
            a_group[t - 1].wait()
        a_group[t] = Group(aZr.at[0, 0] if t == 1 else aZr.at[:, 0])
        reduce(a_group[t], "z", NY, t, a_local, aZs, aZr)

    class Unit:
        def __init__(self, at, o):
            self.at, self.o, self.q = at, o, turn("z", -o)
            q = self.q
            self.b_local = lambda j, lo, hi: dW[q, lo:hi, j, 0:16, 0:A0]
            self.c_local = lambda j, lo, hi: dW[q, j, lo:hi, 16:32, 0:A0]

        def term(self):
            part = jnp.dot(tokT[self.q], dl[...], preferred_element_type=F32)
            dW[self.q] = part.reshape(NY, NX, FEATS, COLS)

        def step(self, t):
            at = self.at
            if t > 1:
                self.group.wait()
            self.group = Group(bXr.at[at, :, 0] if t == 1 else bXr.at[at])
            reduce(self.group, "x", NY, t, self.b_local, bXs.at[at], bXr.at[at])
            reduce(self.group, "y", NX, t, self.c_local, cYs.at[at], cYr.at[at])

        def near(self):
            at = self.at
            self.group.wait()
            self.group = Group(W.at[pl.ds(0, 6), 0, 0, up, cb])
            total = ring_sum("x", NY, self.b_local, bXr.at[at])
            b1[at] = total
            bYs[at] = total.astype(BF16)
            for o in range(1, 4):
                self.group.send(bYs.at[at, turn("y", o)], bYr.at[at, o - 1], along("y", o))
            total = ring_sum("y", NX, self.c_local, cYr.at[at])
            c1[at] = total
            cXs[at] = total.astype(BF16)
            for o in range(1, 4):
                self.group.send(cXs.at[at, turn("x", o)], cXr.at[at, o - 1], along("x", o))

        def across(self):
            at = self.at
            self.group.wait()
            for mine, arrived, rows, i in ((b1, bYr, slice(0, 16), y), (c1, cXr, slice(16, 32), x)):
                total = mine[at, i]
                for k in range(3):
                    total += arrived[at, k].astype(F32)
                if self.o == 0:
                    Zf[rows] = total
                else:
                    Zs[at, rows] = total.astype(BF16)
            if self.o:
                to_z.send(Zs.at[at], Zr.at[self.o - 1], along("z", -self.o))

    to_z = Group(Zr)
    units = [Unit(at, o) for at, o in enumerate((4, 3, 5, 2, 6, 1, 7, 0))]

    r_z = Group(R1.at[pl.ds(0, 7)])
    r_xy = Group(W.at[pl.ds(0, 5), pl.ds(0, 3), pl.ds(0, 2), :, ca])
    all_z = pl.ds(0, NZ)

    def pack(o):
        j = turn("z", o)
        packed = jnp.dot(hot[j], D[...], preferred_element_type=F32)
        packed = packed.reshape(NY, NX, 8, HEAD_DIM).astype(BF16)
        if o:
            S[j] = packed
            r_z.send(S.at[j], R1.at[z], along("z", o))
        else:
            R1[z] = packed

    def route_plane():
        r_z.wait()
        for oy in range(NY):
            for ox in range(NX):
                jy, jx = turn("y", oy), turn("x", ox)
                if oy or ox:
                    r_xy.send(R1.at[all_z, jy, jx], R3.at[all_z, y, x], device(z, jy, jx, m))
        for s in range(NZ):
            R3[s, y, x] = R1[s, y, x]

    def unpack():
        r_xy.wait()
        Rf[...] = R3[...].astype(F32).reshape(8 * ROWS, HEAD_DIM)
        for h in range(HEADS):
            G[:, h * HEAD_DIM:(h + 1) * HEAD_DIM] = Rf[pl.ds(h, 2 * ROWS, stride=HEADS), :].astype(BF16)

    def product(tile):
        return lax.dot_general(G[...], W[tile].reshape(SLAB, COLS), (((1,), (1,)), ((), ())),
                               preferred_element_type=F32).astype(BF16)

    halves, stores = [], []

    def give(t):
        DXs[t] = product((1 - m) * 4 + t)
        group = Group(DXr.at[t])
        group.send(DXs.at[t], DXr.at[t], partner)
        halves.append(group)

    def take(t):
        own = product(m * 4 + t).astype(F32)
        halves[t].wait()
        columns = pl.ds(t * SLAB, SLAB)
        rows[:, t * SLAB:(t + 1) * SLAB] = (own + DXr[t].astype(F32)).astype(BF16)
        stores.append(pltpu.make_async_copy(rows.at[:, columns], rows_out.at[:, columns], local_sem.at[1 + t]))
        stores[-1].start()

    ra_y, ra_x = Group(aYr), Group(aXr)
    scale = 1.0 / 128.0

    def a_over_y():
        a_group[4].wait()
        total = ring_sum("z", NY, a_local, aZr)
        a1[...] = total
        aYs[...] = total.astype(BF16)
        for o in range(1, NY):
            ra_y.send(aYs.at[turn("y", o)], aYr.at[o - 1], along("y", o))

    def a_over_x():
        ra_y.wait()
        total = a1[y]
        for o in range(NY - 1):
            total += aYr[o].astype(F32)
        a2[...] = total
        aXs[...] = total.astype(BF16)
        for o in range(1, NX):
            ra_x.send(aXs.at[turn("x", o)], aXr.at[o - 1], along("x", o))

    def finish_bc():
        to_z.wait()
        total = Zf[...]
        for o in range(NZ - 1):
            total += Zr[o].astype(F32)
        grad_out[:, 0:A0] = total * scale

    def finish_a():
        ra_x.wait()
        total = a2[x]
        for o in range(NX - 1):
            total += aXr[o].astype(F32)
        grad_out[:, A0:A1] = total * scale

    fetch.wait()
    prepare(4)
    a_row()
    chunks[0].far(1)
    a_far(1, 0, 1)
    prepare(0)
    arrive(4)
    arrive(6)
    arrive(7)
    arrive(1)
    a_far(2, 0, 1)
    arrive(3)
    a_y.wait()
    a_far(1, 1, 4)
    arrive(2)
    prepare(6)
    chunks[0].far(2)
    arrive(5)
    a_far(3, 0, 1)
    chunks[4].far(1)
    prepare(1)
    chunks[6].far(1)
    chunks[3].far(1)
    a_far(2, 1, 4)
    prepare(7)
    chunks[2].far(1)
    prepare(5)
    chunks[1].far(1)
    chunks[7].far(1)
    chunks[5].far(1)
    chunks[3].far(2)
    a_far(3, 1, 4)
    a_far(4, 0, 1)
    chunks[2].far(2)
    prepare(3)
    chunks[1].far(2)
    chunks[6].far(2)
    chunks[0].group.wait()
    forward(0)
    chunks[4].far(2)
    chunks[5].far(2)
    chunks[7].far(2)
    a_far(4, 1, 4)
    chunks[4].group.wait()
    chunks[6].group.wait()
    forward(6)
    chunks[3].group.wait()
    forward(3)
    chunks[5].group.wait()
    forward(5)
    chunks[1].group.wait()
    forward(1)
    chunks[2].group.wait()
    forward(2)
    prepare(2)
    chunks[7].group.wait()
    forward(7)
    a_last[0].wait()
    a_last[1].wait()
    forward(4)
    norm_grads()
    pack(4)
    units[4].term()
    units[2].term()
    units[1].term()
    units[3].term()
    units[0].term()
    units[5].term()
    units[7].term()
    units[6].term()
    a_step(1)
    units[1].step(1)
    units[4].step(1)
    units[3].step(1)
    pack(5)
    pack(3)
    units[6].step(1)
    units[7].step(1)
    pack(0)
    units[0].step(1)
    units[1].step(2)
    a_step(2)
    pack(6)
    units[2].step(1)
    units[5].step(1)
    units[4].step(2)
    pack(2)
    units[6].step(2)
    units[1].near()
    pack(1)
    units[3].step(2)
    pack(7)
    units[2].step(2)
    a_step(3)
    units[5].step(2)
    units[0].step(2)
    units[4].near()
    route_plane()
    a_step(4)
    units[2].near()
    units[5].near()
    units[3].near()
    units[0].near()
    units[1].across()
    units[7].step(2)
    units[6].near()
    a_over_y()
    units[2].across()
    unpack()
    give(0)
    units[0].across()
    units[5].across()
    units[4].across()
    give(1)
    give(2)
    units[3].across()
    units[7].near()
    give(3)
    units[6].across()
    a_over_x()
    take(0)
    take(1)
    take(2)
    take(3)
    units[7].across()
    finish_bc()
    finish_a()
    assert len(groups) == ARRIVALS
    for copy in copies[-SENDS:]:
        copy.wait_send()
    for store in stores:
        store.wait()


PIECES = 8


def hand_on(rows, grad, rows_out, grad_out, sem):
    copies = [pltpu.make_async_copy(grad, grad_out, sem.at[PIECES])]
    size = rows.shape[0] // PIECES
    for i in range(PIECES):
        part = pl.ds(i * size, size)
        copies.append(pltpu.make_async_copy(rows.at[part], rows_out.at[part], sem.at[i]))
    for copy in copies:
        copy.start()
    for copy in copies:
        copy.wait()


def per_device(tokens, key_cot, routes, counts, widths, key_weight):
    vmem = pl.BlockSpec(memory_space=pltpu.VMEM)
    smem = pl.BlockSpec(memory_space=pltpu.SMEM)
    anywhere = pl.BlockSpec(memory_space=pl.ANY)
    buffers = [
        ((ROWS, WIDTH), BF16),
        ((2 * ROWS, WIDTH // 2), BF16),
        ((NZ, NY, NX, FEATS, COLS), BF16),
        ((NZ, SLAB, ROWS), BF16),
        ((NZ, NY, NX, FEATS, COLS), F32),
        ((ROWS, COLS), F32),
        ((ROWS, COLS), BF16),
        ((HEADS * ROWS, HEAD_DIM), BF16),
        ((NZ, ROWS, HEADS * ROWS), BF16),
        ((NZ, NY, NX, 8, HEAD_DIM), BF16),
        ((NZ, NY, NX, 8, HEAD_DIM), BF16),
        ((NZ, NY, NX, 8, HEAD_DIM), BF16),
        ((8 * ROWS, HEAD_DIM), F32),
        ((2 * ROWS, COLS), BF16),
        ((4, 2 * ROWS, SLAB), BF16),
        ((4, 2 * ROWS, SLAB), BF16),
        ((2, 4, NY, NX, FEATS, 128), BF16),
        ((2, 4, NY, NX, FEATS, 128), BF16),
        ((NY, NX, FEATS, 128), F32),
        ((NY, NX, FEATS, 128), BF16),
        ((NY - 1, NX, FEATS, 128), BF16),
        ((NX, FEATS, 128), F32),
        ((NX, FEATS, 128), BF16),
        ((NX - 1, FEATS, 128), BF16),
        ((NZ, 2, 2, NY, 16, 384), BF16),
        ((NZ, 2, 2, NY, 16, 384), BF16),
        ((NZ, NY, 16, 384), F32),
        ((NZ, NY, 16, 384), BF16),
        ((NZ, NY - 1, 16, 384), BF16),
        ((NZ, 2, 2, NX, 16, 384), BF16),
        ((NZ, 2, 2, NX, 16, 384), BF16),
        ((NZ, NX, 16, 384), F32),
        ((NZ, NX, 16, 384), BF16),
        ((NZ, NX - 1, 16, 384), BF16),
        ((FEATS, 384), F32),
        ((NZ, FEATS, 384), BF16),
        ((NZ - 1, FEATS, 384), BF16),
    ]
    rows, grad = pl.pallas_call(
        kernel,
        out_shape=(jax.ShapeDtypeStruct((2 * ROWS, WIDTH // 2), BF16), jax.ShapeDtypeStruct((FEATS, COLS), F32)),
        in_specs=[anywhere, vmem, vmem, smem, smem, vmem],
        out_specs=(anywhere, vmem),
        scratch_shapes=[pltpu.VMEM(shape, dtype) for shape, dtype in buffers]
        + [pltpu.SemaphoreType.DMA((5,)), pltpu.SemaphoreType.DMA((SENDS,)), pltpu.SemaphoreType.DMA((ARRIVALS,))],
        compiler_params=pltpu.CompilerParams(
            collective_id=0, has_side_effects=True, vmem_limit_bytes=58 << 20),
    )(tokens, key_cot, routes.reshape(1, ROWS), counts, widths, key_weight)
    return pl.pallas_call(
        hand_on,
        out_shape=(jax.ShapeDtypeStruct(rows.shape, BF16), jax.ShapeDtypeStruct(grad.shape, F32)),
        in_specs=[anywhere, anywhere],
        out_specs=(anywhere, anywhere),
        scratch_shapes=[pltpu.SemaphoreType.DMA((PIECES + 1,))],
    )(rows, grad)


def solution(mesh):
    return jax.shard_map(
        per_device,
        mesh=mesh,
        in_specs=(P("dp", None), P("dp", "mp"), P("dp", None), P("dp", None), P(), P("dp", "mp")),
        out_specs=(P("dp", "mp"), P("dp", "mp")),
        check_vma=False,
    )
```

```python
import math

import jax
import jax.numpy as jnp
from jax import lax
from jax.experimental import pallas as pl
from jax.experimental.pallas import tpu as pltpu
from jax.sharding import PartitionSpec as P

HEAD_DIM = 128
EPSILON = 1e-06
MESH = pl.DeviceIdType.MESH
NZ, NY, NX = 8, 4, 4
ROWS, WIDTH, COLS, FEATS = 128, 4096, 512, 32
SLAB = WIDTH // NZ
HEADS = COLS // HEAD_DIM
A0, A1 = 384, 512
F32, BF16 = jnp.float32, jnp.bfloat16
SENDS, ARRIVALS = 48, 78


def kernel(tokens_in, cot, routes, counts, widths, shard, rows_out, grad_out,
           tokens, W, tokT, dW, proj, dl, D, hot, S, R1, R3, Rf, G, DXs, DXr,
           aZs, aZr, a1, aYs, aYr, a2, aXs, aXr,
           bXs, bXr, b1, bYs, bYr, cYs, cYr, c1, cXs, cXr, Zf, Zs, Zr,
           local_sem, send_sem, recv_sem):
    me, m = lax.axis_index("dp"), lax.axis_index("mp")
    x, y, z = lax.rem(me, NX), lax.rem(me // NX, NY), me // (NX * NY)

    def device(zz, yy, xx, mm):
        return ((zz * NY + yy) * NX + xx, mm)

    place = {"x": (NX, x), "y": (NY, y), "z": (NZ, z)}

    def turn(axis, by):
        n, i = place[axis]
        return lax.rem(i + (by % n), n)

    def along(axis, by):
        j = turn(axis, by)
        return {"x": device(z, y, j, m), "y": device(z, j, x, m), "z": device(j, y, x, m)}[axis]

    partner = device(z, y, x, 1 - m)
    copies, groups = [], []

    class Group:
        def __init__(self, ref):
            self.ref, self.sem, self.bytes, self.done = ref, recv_sem.at[len(groups)], 0, False
            groups.append(self)

        def send(self, src, dst, to):
            at = len(copies)
            if at >= SENDS:
                copies[at - SENDS].wait_send()
            copy = pltpu.make_async_remote_copy(
                src_ref=src, dst_ref=dst, send_sem=send_sem.at[at % SENDS], recv_sem=self.sem,
                device_id=to, device_id_type=MESH)
            copy.start()
            copies.append(copy)
            self.bytes += math.prod(src.shape) * src.dtype.itemsize

        def wait(self):
            assert self.bytes == math.prod(self.ref.shape) * self.ref.dtype.itemsize
            self.done = True
            pltpu.make_async_remote_copy(
                src_ref=self.ref, dst_ref=self.ref, send_sem=send_sem.at[0], recv_sem=self.sem,
                device_id=partner, device_id_type=MESH).wait_recv()

    fetch = pltpu.make_async_copy(tokens_in, tokens, local_sem.at[0])
    fetch.start()

    barrier = pltpu.get_barrier_semaphore()
    peers = [along(axis, o) for axis in "xyz" for o in range(1, place[axis][0])] + [partner]
    for peer in peers:
        pl.semaphore_signal(barrier, inc=1, device_id=peer, device_id_type=MESH)
    W[z, y, x] = shard[...]
    pl.semaphore_wait(barrier, len(peers))

    up, down = pl.ds(0, 16), pl.ds(16, 16)
    ca, cb = pl.ds(A0, A1 - A0), pl.ds(0, A0)
    every = pl.ds(0, 4)

    def span(half):
        return every if half is None else pl.ds(half * 2, 2)

    def ring(group, axis, k, region):
        halves = (0, 1) if k == place[axis][0] // 2 else (None, None)
        right, left = region(turn(axis, 1 - k), halves[0]), region(turn(axis, k - 1), halves[1])
        group.send(right, right, along(axis, 1))
        group.send(left, left, along(axis, -1))

    class Chunk:
        def __init__(self, q):
            self.q = q

        def near(self):
            q = self.q
            self.group = Group(W.at[pl.ds(0, 6), 0, 0, up, cb])
            upper, lower = W.at[q, y, x, up, cb], W.at[q, y, x, down, cb]
            for o in range(1, 4):
                self.group.send(upper, upper, along("y", o))
                self.group.send(lower, lower, along("x", o))

        def far(self, k):
            q = self.q
            self.group.wait()
            self.group = Group(W.at[pl.ds(0, 4 // k), every, 0, up, cb])
            ring(self.group, "x", k, lambda j, h: W.at[q, span(h), j, up, cb])
            ring(self.group, "y", k, lambda j, h: W.at[q, j, span(h), down, cb])

    chunks = [Chunk(turn("z", -o)) for o in range(NZ)]
    own_bc = W.at[z, y, x, :, cb]
    from_z = {}
    for o in (4, 3, 5, 2, 6, 1, 7):
        from_z[o] = Group(W.at[0, 0, 0, :, cb])
        from_z[o].send(own_bc, own_bc, along("z", o))
    chunks[0].near()
    own_a = W.at[z, y, x, :, ca]
    a_x = Group(W.at[pl.ds(0, 3), 0, 0, :, ca])
    for o in range(1, NX):
        a_x.send(own_a, own_a, along("x", o))

    def arrive(*offsets):
        for o in offsets:
            from_z[o].wait()
            chunks[o].near()

    def far(k, *offsets):
        for o in offsets:
            chunks[o].far(k)

    a_last = {}

    def a_far(k, first, last):
        if k > 1:
            a_last[first].wait()
        a_last[first] = Group(W.at[pl.ds(0, 1 if k == 4 else 2), pl.ds(0, last - first), every, :, ca])
        for oy in range(first, last):
            row = turn("y", -oy)
            ring(a_last[first], "z", k, lambda j, h: W.at[j, row, span(h), :, ca])

    named = jnp.broadcast_to(routes[...], (ROWS, ROWS))
    first_index = lax.broadcasted_iota(jnp.int32, (ROWS, ROWS), 0)
    second_index = lax.broadcasted_iota(jnp.int32, (ROWS, ROWS), 1)
    same = (named == named.astype(F32).T.astype(jnp.int32)) & (first_index < second_index)
    earlier = jnp.sum(same.astype(F32), axis=0, keepdims=True).astype(jnp.int32)
    slot = (routes[...] * 2 + earlier) * HEADS

    def prepare(s):
        tokT[s] = tokens[:, s * SLAB:(s + 1) * SLAB].T
        for h in range(HEADS):
            hot[s, :, h * ROWS:(h + 1) * ROWS] = (first_index + s * ROWS == slot + h).astype(F32).astype(BF16)

    started = []

    def forward(o):
        q = chunks[o].q
        columns = pl.ds(pl.multiple_of(q * SLAB, SLAB), SLAB)
        term = jnp.dot(tokens[:, columns], W[q].reshape(SLAB, COLS), preferred_element_type=F32)
        if not started:
            started.append(o)
            proj[...] = term
        else:
            proj[...] += term

    a_y = Group(W.at[pl.ds(0, 3), 0, every, :, ca])

    def a_row():
        a_x.wait()
        own = W.at[z, y, every, :, ca]
        for o in range(1, NY):
            a_y.send(own, own, along("y", o))

    position = lax.broadcasted_iota(jnp.int32, (ROWS, 1), 0)
    bound0 = counts[0, 0]
    bound1 = bound0 + counts[0, 1]
    bound2 = bound1 + counts[0, 2]
    row_width = jnp.where(position < bound0, widths[0], jnp.where(
        position < bound1, widths[1], jnp.where(position < bound2, widths[2], widths[3])))

    def norm_grads():
        for h in range(HEADS):
            cols = slice(h * HEAD_DIM, (h + 1) * HEAD_DIM)
            own = proj[:, cols]
            inverse = 1.0 / jnp.sqrt(jnp.mean(own * own, axis=1, keepdims=True) + EPSILON)
            outputs = own * inverse
            head_mask = (m * HEADS + h < row_width).astype(F32)
            upstream = cot[:, cols].astype(F32) * head_mask
            delta = (upstream - outputs * jnp.mean(upstream * outputs, axis=1, keepdims=True)) * inverse
            dl[:, cols] = delta.astype(BF16)
            D[h * ROWS:(h + 1) * ROWS] = delta.astype(BF16)

    def reduce(group, axis, lead, t, local, sbuf, rbuf):
        n, half = place[axis][0], lead // 2
        for d in range(2):
            by = n // 2 - t + 1
            j = turn(axis, by if d == 0 else -by)

            def put(lo, hi, arrived):
                value = local(j, lo, hi)
                if arrived:
                    value += rbuf[d, t - 2, lo:hi].astype(F32)
                sbuf[d, t - 1, lo:hi] = value.astype(BF16)

            first = d * half
            part = pl.ds(0, lead)
            if t == 1:
                put(first, first + half, False)
                part = pl.ds(first, half)
            elif t == 2:
                put(first, first + half, True)
                put(half - first, lead - first, False)
            else:
                put(0, half, True)
                put(half, lead, True)
            group.send(sbuf.at[d, t - 1, part], rbuf.at[d, t - 1, part], along(axis, 1 if d == 0 else -1))

    def ring_sum(axis, lead, local, rbuf):
        n, i = place[axis]
        s = n // 2 - 1
        return (local(i, 0, lead) + rbuf[0, s].astype(F32)) + rbuf[1, s].astype(F32)

    def a_local(j, lo, hi):
        return dW[j, lo:hi, :, :, A0:A1]

    a_group = {}

    def a_step(t):
        if t > 1:
            a_group[t - 1].wait()
        a_group[t] = Group(aZr.at[0, 0] if t == 1 else aZr.at[:, 0])
        reduce(a_group[t], "z", NY, t, a_local, aZs, aZr)

    class Unit:
        def __init__(self, at, o):
            self.at, self.o, self.q = at, o, turn("z", -o)
            q = self.q
            self.b_local = lambda j, lo, hi: dW[q, lo:hi, j, 0:16, 0:A0]
            self.c_local = lambda j, lo, hi: dW[q, j, lo:hi, 16:32, 0:A0]

        def term(self):
            part = jnp.dot(tokT[self.q], dl[...], preferred_element_type=F32)
            dW[self.q] = part.reshape(NY, NX, FEATS, COLS)

        def step(self, t):
            at = self.at
            if t > 1:
                self.group.wait()
            self.group = Group(bXr.at[at, :, 0] if t == 1 else bXr.at[at])
            reduce(self.group, "x", NY, t, self.b_local, bXs.at[at], bXr.at[at])
            reduce(self.group, "y", NX, t, self.c_local, cYs.at[at], cYr.at[at])

        def near(self):
            at = self.at
            self.group.wait()
            self.group = Group(W.at[pl.ds(0, 6), 0, 0, up, cb])
            total = ring_sum("x", NY, self.b_local, bXr.at[at])
            b1[at] = total
            bYs[at] = total.astype(BF16)
            for o in range(1, 4):
                self.group.send(bYs.at[at, turn("y", o)], bYr.at[at, o - 1], along("y", o))
            total = ring_sum("y", NX, self.c_local, cYr.at[at])
            c1[at] = total
            cXs[at] = total.astype(BF16)
            for o in range(1, 4):
                self.group.send(cXs.at[at, turn("x", o)], cXr.at[at, o - 1], along("x", o))

        def across(self):
            at = self.at
            self.group.wait()
            for mine, arrived, rows, i in ((b1, bYr, slice(0, 16), y), (c1, cXr, slice(16, 32), x)):
                total = mine[at, i]
                for k in range(3):
                    total += arrived[at, k].astype(F32)
                if self.o == 0:
                    Zf[rows] = total
                else:
                    Zs[at, rows] = total.astype(BF16)
            if self.o:
                to_z.send(Zs.at[at], Zr.at[self.o - 1], along("z", -self.o))

    to_z = Group(Zr)
    units = [Unit(at, o) for at, o in enumerate((4, 3, 5, 2, 6, 1, 7, 0))]

    r_z = Group(R1.at[pl.ds(0, 7)])
    r_xy = Group(W.at[pl.ds(0, 5), pl.ds(0, 3), pl.ds(0, 2), :, ca])
    all_z = pl.ds(0, NZ)

    def pack(o):
        j = turn("z", o)
        packed = jnp.dot(hot[j], D[...], preferred_element_type=F32)
        packed = packed.reshape(NY, NX, 8, HEAD_DIM).astype(BF16)
        if o:
            S[j] = packed
            r_z.send(S.at[j], R1.at[z], along("z", o))
        else:
            R1[z] = packed

    def route_plane():
        r_z.wait()
        for oy in range(NY):
            for ox in range(NX):
                jy, jx = turn("y", oy), turn("x", ox)
                if oy or ox:
                    r_xy.send(R1.at[all_z, jy, jx], R3.at[all_z, y, x], device(z, jy, jx, m))
        for s in range(NZ):
            R3[s, y, x] = R1[s, y, x]

    def unpack():
        r_xy.wait()
        Rf[...] = R3[...].astype(F32).reshape(8 * ROWS, HEAD_DIM)
        for h in range(HEADS):
            G[:, h * HEAD_DIM:(h + 1) * HEAD_DIM] = Rf[pl.ds(h, 2 * ROWS, stride=HEADS), :].astype(BF16)

    def product(tile):
        return lax.dot_general(G[...], W[tile].reshape(SLAB, COLS), (((1,), (1,)), ((), ())),
                               preferred_element_type=F32).astype(BF16)

    halves = []

    def give(t):
        DXs[t] = product((1 - m) * 4 + t)
        group = Group(DXr.at[t])
        group.send(DXs.at[t], DXr.at[t], partner)
        halves.append(group)

    def take(t):
        own = product(m * 4 + t).astype(F32)
        halves[t].wait()
        rows_out[:, t * SLAB:(t + 1) * SLAB] = (own + DXr[t].astype(F32)).astype(BF16)

    ra_y, ra_x = Group(aYr), Group(aXr)
    scale = 1.0 / 128.0

    def a_over_y():
        a_group[4].wait()
        total = ring_sum("z", NY, a_local, aZr)
        a1[...] = total
        aYs[...] = total.astype(BF16)
        for o in range(1, NY):
            ra_y.send(aYs.at[turn("y", o)], aYr.at[o - 1], along("y", o))

    def a_over_x():
        ra_y.wait()
        total = a1[y]
        for o in range(NY - 1):
            total += aYr[o].astype(F32)
        a2[...] = total
        aXs[...] = total.astype(BF16)
        for o in range(1, NX):
            ra_x.send(aXs.at[turn("x", o)], aXr.at[o - 1], along("x", o))

    def finish_bc():
        to_z.wait()
        total = Zf[...]
        for o in range(NZ - 1):
            total += Zr[o].astype(F32)
        grad_out[:, 0:A0] = total * scale

    def finish_a():
        ra_x.wait()
        total = a2[x]
        for o in range(NX - 1):
            total += aXr[o].astype(F32)
        grad_out[:, A0:A1] = total * scale

    fetch.wait()
    prepare(4)
    a_row()
    chunks[0].far(1)
    a_far(1, 0, 1)
    prepare(0)
    arrive(4)
    arrive(6)
    arrive(7)
    arrive(1)
    a_far(2, 0, 1)
    arrive(3)
    a_y.wait()
    a_far(1, 1, 4)
    arrive(2)
    prepare(6)
    chunks[0].far(2)
    arrive(5)
    a_far(3, 0, 1)
    chunks[4].far(1)
    prepare(1)
    chunks[6].far(1)
    chunks[3].far(1)
    a_far(2, 1, 4)
    prepare(7)
    chunks[2].far(1)
    prepare(5)
    chunks[1].far(1)
    chunks[7].far(1)
    chunks[5].far(1)
    chunks[3].far(2)
    a_far(3, 1, 4)
    a_far(4, 0, 1)
    chunks[2].far(2)
    prepare(3)
    chunks[1].far(2)
    chunks[6].far(2)
    chunks[0].group.wait()
    forward(0)
    chunks[4].far(2)
    chunks[5].far(2)
    chunks[7].far(2)
    a_far(4, 1, 4)
    chunks[4].group.wait()
    chunks[6].group.wait()
    forward(6)
    chunks[3].group.wait()
    forward(3)
    chunks[5].group.wait()
    forward(5)
    chunks[1].group.wait()
    forward(1)
    chunks[2].group.wait()
    forward(2)
    prepare(2)
    chunks[7].group.wait()
    forward(7)
    a_last[0].wait()
    a_last[1].wait()
    forward(4)
    norm_grads()
    pack(4)
    units[4].term()
    units[2].term()
    units[1].term()
    units[3].term()
    units[0].term()
    units[5].term()
    units[7].term()
    units[6].term()
    a_step(1)
    units[1].step(1)
    units[4].step(1)
    units[3].step(1)
    pack(5)
    pack(3)
    units[6].step(1)
    units[7].step(1)
    pack(0)
    units[0].step(1)
    units[1].step(2)
    a_step(2)
    pack(6)
    units[2].step(1)
    units[5].step(1)
    units[4].step(2)
    pack(2)
    units[6].step(2)
    units[1].near()
    pack(1)
    units[3].step(2)
    pack(7)
    units[2].step(2)
    a_step(3)
    units[5].step(2)
    units[0].step(2)
    units[4].near()
    route_plane()
    a_step(4)
    units[2].near()
    units[5].near()
    units[3].near()
    units[0].near()
    units[1].across()
    units[7].step(2)
    units[6].near()
    a_over_y()
    units[2].across()
    unpack()
    give(0)
    units[0].across()
    units[5].across()
    units[4].across()
    give(1)
    give(2)
    units[3].across()
    units[7].near()
    give(3)
    units[6].across()
    a_over_x()
    take(0)
    take(1)
    take(2)
    take(3)
    units[7].across()
    finish_bc()
    finish_a()
    assert len(groups) == ARRIVALS
    for copy in copies[-SENDS:]:
        copy.wait_send()


def per_device(tokens, key_cot, routes, counts, widths, key_weight):
    vmem = pl.BlockSpec(memory_space=pltpu.VMEM)
    smem = pl.BlockSpec(memory_space=pltpu.SMEM)
    anywhere = pl.BlockSpec(memory_space=pl.ANY)
    buffers = [
        ((ROWS, WIDTH), BF16),
        ((NZ, NY, NX, FEATS, COLS), BF16),
        ((NZ, SLAB, ROWS), BF16),
        ((NZ, NY, NX, FEATS, COLS), F32),
        ((ROWS, COLS), F32),
        ((ROWS, COLS), BF16),
        ((HEADS * ROWS, HEAD_DIM), BF16),
        ((NZ, ROWS, HEADS * ROWS), BF16),
        ((NZ, NY, NX, 8, HEAD_DIM), BF16),
        ((NZ, NY, NX, 8, HEAD_DIM), BF16),
        ((NZ, NY, NX, 8, HEAD_DIM), BF16),
        ((8 * ROWS, HEAD_DIM), F32),
        ((2 * ROWS, COLS), BF16),
        ((4, 2 * ROWS, SLAB), BF16),
        ((4, 2 * ROWS, SLAB), BF16),
        ((2, 4, NY, NX, FEATS, 128), BF16),
        ((2, 4, NY, NX, FEATS, 128), BF16),
        ((NY, NX, FEATS, 128), F32),
        ((NY, NX, FEATS, 128), BF16),
        ((NY - 1, NX, FEATS, 128), BF16),
        ((NX, FEATS, 128), F32),
        ((NX, FEATS, 128), BF16),
        ((NX - 1, FEATS, 128), BF16),
        ((NZ, 2, 2, NY, 16, 384), BF16),
        ((NZ, 2, 2, NY, 16, 384), BF16),
        ((NZ, NY, 16, 384), F32),
        ((NZ, NY, 16, 384), BF16),
        ((NZ, NY - 1, 16, 384), BF16),
        ((NZ, 2, 2, NX, 16, 384), BF16),
        ((NZ, 2, 2, NX, 16, 384), BF16),
        ((NZ, NX, 16, 384), F32),
        ((NZ, NX, 16, 384), BF16),
        ((NZ, NX - 1, 16, 384), BF16),
        ((FEATS, 384), F32),
        ((NZ, FEATS, 384), BF16),
        ((NZ - 1, FEATS, 384), BF16),
    ]
    rows, grad = pl.pallas_call(
        kernel,
        out_shape=(pltpu.VMEM((2 * ROWS, WIDTH // 2), BF16), pltpu.VMEM((FEATS, COLS), F32)),
        in_specs=[anywhere, vmem, vmem, smem, smem, vmem],
        out_specs=(vmem, vmem),
        scratch_shapes=[pltpu.VMEM(shape, dtype) for shape, dtype in buffers]
        + [pltpu.SemaphoreType.DMA((1,)), pltpu.SemaphoreType.DMA((SENDS,)), pltpu.SemaphoreType.DMA((ARRIVALS,))],
        compiler_params=pltpu.CompilerParams(
            collective_id=0, has_side_effects=True, vmem_limit_bytes=58 << 20),
    )(tokens, key_cot, routes.reshape(1, ROWS), counts, widths, key_weight)
    return rows, grad


def solution(mesh):
    return jax.shard_map(
        per_device,
        mesh=mesh,
        in_specs=(P("dp", None), P("dp", "mp"), P("dp", None), P("dp", None), P(), P("dp", "mp")),
        out_specs=(P("dp", "mp"), P("dp", "mp")),
        check_vma=False,
    )
```

```python
import math

import jax
import jax.numpy as jnp
from jax import lax
from jax.experimental import pallas as pl
from jax.experimental.pallas import tpu as pltpu
from jax.sharding import PartitionSpec as P

HEAD_DIM = 128
EPSILON = 1e-06
MESH = pl.DeviceIdType.MESH
NZ, NY, NX = 8, 4, 4
ROWS, WIDTH, COLS, FEATS = 128, 4096, 512, 32
SLAB = WIDTH // NZ
HEADS = COLS // HEAD_DIM
A0, A1 = 384, 512
F32, BF16 = jnp.float32, jnp.bfloat16
SENDS, ARRIVALS = 48, 98


def kernel(tokens_in, cot, routes, counts, widths, shard, rows_out, grad_out,
           tokens, W, tokT, dW, proj, dl, D, hot, S, R1, R3, Rf, G, DXs, DXr,
           aZs, aZr, a1, aYs, aYr, a2, aXs, aXr,
           bXs, bXr, b1, bYs, bYr, cYs, cYr, c1, cXs, cXr, Zf, Zs, Zr,
           local_sem, send_sem, recv_sem):
    me, m = lax.axis_index("dp"), lax.axis_index("mp")
    x, y, z = lax.rem(me, NX), lax.rem(me // NX, NY), me // (NX * NY)

    def device(zz, yy, xx, mm):
        return ((zz * NY + yy) * NX + xx, mm)

    place = {"x": (NX, x), "y": (NY, y), "z": (NZ, z)}

    def turn(axis, by):
        n, i = place[axis]
        return lax.rem(i + (by % n), n)

    def along(axis, by):
        j = turn(axis, by)
        return {"x": device(z, y, j, m), "y": device(z, j, x, m), "z": device(j, y, x, m)}[axis]

    partner = device(z, y, x, 1 - m)
    copies, groups = [], []

    class Group:
        def __init__(self, ref):
            self.ref, self.sem, self.bytes, self.done = ref, recv_sem.at[len(groups)], 0, False
            groups.append(self)

        def send(self, src, dst, to):
            at = len(copies)
            if at >= SENDS:
                copies[at - SENDS].wait_send()
            copy = pltpu.make_async_remote_copy(
                src_ref=src, dst_ref=dst, send_sem=send_sem.at[at % SENDS], recv_sem=self.sem,
                device_id=to, device_id_type=MESH)
            copy.start()
            copies.append(copy)
            self.bytes += math.prod(src.shape) * src.dtype.itemsize

        def wait(self):
            assert self.bytes == math.prod(self.ref.shape) * self.ref.dtype.itemsize
            self.done = True
            pltpu.make_async_remote_copy(
                src_ref=self.ref, dst_ref=self.ref, send_sem=send_sem.at[0], recv_sem=self.sem,
                device_id=partner, device_id_type=MESH).wait_recv()

    fetch = pltpu.make_async_copy(tokens_in, tokens, local_sem.at[0])
    fetch.start()

    barrier = pltpu.get_barrier_semaphore()
    peers = [along(axis, o) for axis in "xyz" for o in range(1, place[axis][0])] + [partner]
    for peer in peers:
        pl.semaphore_signal(barrier, inc=1, device_id=peer, device_id_type=MESH)
    W[z, y, x] = shard[...]
    pl.semaphore_wait(barrier, len(peers))

    up, down = pl.ds(0, 16), pl.ds(16, 16)
    ca, cb = pl.ds(A0, A1 - A0), pl.ds(0, A0)
    every = pl.ds(0, 4)

    def span(half):
        return every if half is None else pl.ds(half * 2, 2)

    def ring(group, axis, k, region):
        halves = (0, 1) if k == place[axis][0] // 2 else (None, None)
        right, left = region(turn(axis, 1 - k), halves[0]), region(turn(axis, k - 1), halves[1])
        group.send(right, right, along(axis, 1))
        group.send(left, left, along(axis, -1))

    class Chunk:
        def __init__(self, q):
            self.q = q

        def near(self):
            q = self.q
            self.group = Group(W.at[pl.ds(0, 6), 0, 0, up, cb])
            upper, lower = W.at[q, y, x, up, cb], W.at[q, y, x, down, cb]
            for o in range(1, 4):
                self.group.send(upper, upper, along("y", o))
                self.group.send(lower, lower, along("x", o))

        def far(self, k):
            q = self.q
            self.group.wait()
            self.group = Group(W.at[pl.ds(0, 4 // k), every, 0, up, cb])
            ring(self.group, "x", k, lambda j, h: W.at[q, span(h), j, up, cb])
            ring(self.group, "y", k, lambda j, h: W.at[q, j, span(h), down, cb])

    chunks = [Chunk(turn("z", -o)) for o in range(NZ)]
    own_bc = W.at[z, y, x, :, cb]
    from_z = {}
    for o in (4, 3, 5, 2, 6, 1, 7):
        from_z[o] = Group(W.at[0, 0, 0, :, cb])
        from_z[o].send(own_bc, own_bc, along("z", o))
    chunks[0].near()
    own_a = W.at[z, y, x, :, ca]
    a_x = Group(W.at[pl.ds(0, 3), 0, 0, :, ca])
    for o in range(1, NX):
        a_x.send(own_a, own_a, along("x", o))

    def arrive(*offsets):
        for o in offsets:
            from_z[o].wait()
            chunks[o].near()

    def far(k, *offsets):
        for o in offsets:
            chunks[o].far(k)

    a_last = {}

    def a_far(k, oy):
        if k > 1:
            a_last[oy].wait()
        a_last[oy] = Group(W.at[0, 0, every, :, ca] if k == 4 else W.at[pl.ds(0, 2), 0, every, :, ca])
        row = turn("y", -oy)
        ring(a_last[oy], "z", k, lambda j, h: W.at[j, row, span(h), :, ca])

    named = jnp.broadcast_to(routes[...], (ROWS, ROWS))
    first_index = lax.broadcasted_iota(jnp.int32, (ROWS, ROWS), 0)
    second_index = lax.broadcasted_iota(jnp.int32, (ROWS, ROWS), 1)
    same = (named == named.astype(F32).T.astype(jnp.int32)) & (first_index < second_index)
    earlier = jnp.sum(same.astype(F32), axis=0, keepdims=True).astype(jnp.int32)
    slot = (routes[...] * 2 + earlier) * HEADS

    def prepare(s):
        tokT[s] = tokens[:, s * SLAB:(s + 1) * SLAB].T
        for h in range(HEADS):
            hot[s, :, h * ROWS:(h + 1) * ROWS] = (first_index + s * ROWS == slot + h).astype(F32).astype(BF16)

    started = []

    def forward(o):
        q = chunks[o].q
        columns = pl.ds(pl.multiple_of(q * SLAB, SLAB), SLAB)
        term = jnp.dot(tokens[:, columns], W[q].reshape(SLAB, COLS), preferred_element_type=F32)
        if not started:
            started.append(o)
            proj[...] = term
        else:
            proj[...] += term

    a_y = Group(W.at[pl.ds(0, 3), 0, every, :, ca])

    def a_row():
        a_x.wait()
        own = W.at[z, y, every, :, ca]
        for o in range(1, NY):
            a_y.send(own, own, along("y", o))

    position = lax.broadcasted_iota(jnp.int32, (ROWS, 1), 0)
    bound0 = counts[0, 0]
    bound1 = bound0 + counts[0, 1]
    bound2 = bound1 + counts[0, 2]
    row_width = jnp.where(position < bound0, widths[0], jnp.where(
        position < bound1, widths[1], jnp.where(position < bound2, widths[2], widths[3])))

    def norm_grads():
        for h in range(HEADS):
            cols = slice(h * HEAD_DIM, (h + 1) * HEAD_DIM)
            own = proj[:, cols]
            inverse = 1.0 / jnp.sqrt(jnp.mean(own * own, axis=1, keepdims=True) + EPSILON)
            outputs = own * inverse
            head_mask = (m * HEADS + h < row_width).astype(F32)
            upstream = cot[:, cols].astype(F32) * head_mask
            delta = (upstream - outputs * jnp.mean(upstream * outputs, axis=1, keepdims=True)) * inverse
            dl[:, cols] = delta.astype(BF16)
            D[h * ROWS:(h + 1) * ROWS] = delta.astype(BF16)

    def reduce(group, axis, lead, t, local, sbuf, rbuf):
        n, half = place[axis][0], lead // 2
        for d in range(2):
            by = n // 2 - t + 1
            j = turn(axis, by if d == 0 else -by)

            def put(lo, hi, arrived):
                value = local(j, lo, hi)
                if arrived:
                    value += rbuf[d, t - 2, lo:hi].astype(F32)
                sbuf[d, t - 1, lo:hi] = value.astype(BF16)

            first = d * half
            part = pl.ds(0, lead)
            if t == 1:
                put(first, first + half, False)
                part = pl.ds(first, half)
            elif t == 2:
                put(first, first + half, True)
                put(half - first, lead - first, False)
            else:
                put(0, half, True)
                put(half, lead, True)
            group.send(sbuf.at[d, t - 1, part], rbuf.at[d, t - 1, part], along(axis, 1 if d == 0 else -1))

    def ring_sum(axis, lead, local, rbuf):
        n, i = place[axis]
        s = n // 2 - 1
        return (local(i, 0, lead) + rbuf[0, s].astype(F32)) + rbuf[1, s].astype(F32)

    def a_local(k):
        row = turn("y", k)
        return lambda j, lo, hi: dW[j, row, lo:hi, :, A0:A1]

    a_group = {}

    def a_step(t, k):
        if t > 1:
            a_group[k].wait()
        a_group[k] = Group(aZr.at[k, 0, 0] if t == 1 else aZr.at[k, :, 0])
        reduce(a_group[k], "z", NX, t, a_local(k), aZs.at[k], aZr.at[k])

    class Unit:
        def __init__(self, at, o):
            self.at, self.o, self.q = at, o, turn("z", -o)
            q = self.q
            self.b_local = lambda j, lo, hi: dW[q, lo:hi, j, 0:16, 0:A0]
            self.c_local = lambda j, lo, hi: dW[q, j, lo:hi, 16:32, 0:A0]

        def term(self):
            part = jnp.dot(tokT[self.q], dl[...], preferred_element_type=F32)
            dW[self.q] = part.reshape(NY, NX, FEATS, COLS)

        def step(self, t):
            at = self.at
            if t > 1:
                self.group.wait()
            self.group = Group(bXr.at[at, :, 0] if t == 1 else bXr.at[at])
            reduce(self.group, "x", NY, t, self.b_local, bXs.at[at], bXr.at[at])
            reduce(self.group, "y", NX, t, self.c_local, cYs.at[at], cYr.at[at])

        def near(self):
            at = self.at
            self.group.wait()
            self.group = Group(W.at[pl.ds(0, 6), 0, 0, up, cb])
            total = ring_sum("x", NY, self.b_local, bXr.at[at])
            b1[at] = total
            bYs[at] = total.astype(BF16)
            for o in range(1, 4):
                self.group.send(bYs.at[at, turn("y", o)], bYr.at[at, o - 1], along("y", o))
            total = ring_sum("y", NX, self.c_local, cYr.at[at])
            c1[at] = total
            cXs[at] = total.astype(BF16)
            for o in range(1, 4):
                self.group.send(cXs.at[at, turn("x", o)], cXr.at[at, o - 1], along("x", o))

        def across(self):
            at = self.at
            self.group.wait()
            for mine, arrived, rows, i in ((b1, bYr, slice(0, 16), y), (c1, cXr, slice(16, 32), x)):
                total = mine[at, i]
                for k in range(3):
                    total += arrived[at, k].astype(F32)
                if self.o == 0:
                    Zf[rows] = total
                else:
                    Zs[at, rows] = total.astype(BF16)
            if self.o:
                to_z.send(Zs.at[at], Zr.at[self.o - 1], along("z", -self.o))

    to_z = Group(Zr)
    units = [Unit(at, o) for at, o in enumerate((4, 3, 5, 2, 6, 1, 7, 0))]

    r_z = Group(R1.at[pl.ds(0, 7)])
    r_xy = Group(W.at[pl.ds(0, 5), pl.ds(0, 3), pl.ds(0, 2), :, ca])
    all_z = pl.ds(0, NZ)

    def pack(o):
        j = turn("z", o)
        packed = jnp.dot(hot[j], D[...], preferred_element_type=F32)
        packed = packed.reshape(NY, NX, 8, HEAD_DIM).astype(BF16)
        if o:
            S[j] = packed
            r_z.send(S.at[j], R1.at[z], along("z", o))
        else:
            R1[z] = packed

    def route_plane():
        r_z.wait()
        for oy in range(NY):
            for ox in range(NX):
                jy, jx = turn("y", oy), turn("x", ox)
                if oy or ox:
                    r_xy.send(R1.at[all_z, jy, jx], R3.at[all_z, y, x], device(z, jy, jx, m))
        for s in range(NZ):
            R3[s, y, x] = R1[s, y, x]

    def unpack():
        r_xy.wait()
        Rf[...] = R3[...].astype(F32).reshape(8 * ROWS, HEAD_DIM)
        for h in range(HEADS):
            G[:, h * HEAD_DIM:(h + 1) * HEAD_DIM] = Rf[pl.ds(h, 2 * ROWS, stride=HEADS), :].astype(BF16)

    def product(tile):
        return lax.dot_general(G[...], W[tile].reshape(SLAB, COLS), (((1,), (1,)), ((), ())),
                               preferred_element_type=F32).astype(BF16)

    halves = []

    def give(t):
        DXs[t] = product((1 - m) * 4 + t)
        group = Group(DXr.at[t])
        group.send(DXs.at[t], DXr.at[t], partner)
        halves.append(group)

    def take(t):
        own = product(m * 4 + t).astype(F32)
        halves[t].wait()
        rows_out[:, t * SLAB:(t + 1) * SLAB] = (own + DXr[t].astype(F32)).astype(BF16)

    ra_y, ra_x = Group(aYr), Group(aXr)
    scale = 1.0 / 128.0

    def a_over_y(k):
        a_group[k].wait()
        total = ring_sum("z", NX, a_local(k), aZr.at[k])
        if k == 0:
            a1[...] = total
        else:
            aYs[k - 1] = total.astype(BF16)
            ra_y.send(aYs.at[k - 1], aYr.at[k - 1], along("y", k))

    def a_over_x():
        ra_y.wait()
        total = a1[...]
        for o in range(NY - 1):
            total += aYr[o].astype(F32)
        a2[...] = total
        aXs[...] = total.astype(BF16)
        for o in range(1, NX):
            ra_x.send(aXs.at[turn("x", o)], aXr.at[o - 1], along("x", o))

    def finish_bc():
        to_z.wait()
        total = Zf[...]
        for o in range(NZ - 1):
            total += Zr[o].astype(F32)
        grad_out[:, 0:A0] = total * scale

    def finish_a():
        ra_x.wait()
        total = a2[x]
        for o in range(NX - 1):
            total += aXr[o].astype(F32)
        grad_out[:, A0:A1] = total * scale

    fetch.wait()
    a_row()
    a_far(1, 0)
    prepare(1)
    arrive(4)
    chunks[0].far(1)
    prepare(4)
    arrive(5)
    arrive(3)
    arrive(2)
    arrive(1)
    a_far(2, 0)
    arrive(6)
    a_y.wait()
    a_far(1, 1)
    a_far(1, 2)
    a_far(1, 3)
    prepare(5)
    arrive(7)
    chunks[0].far(2)
    chunks[4].far(1)
    chunks[3].far(1)
    prepare(6)
    a_far(3, 0)
    a_far(2, 1)
    chunks[2].far(1)
    prepare(3)
    a_far(2, 2)
    chunks[7].far(1)
    a_far(2, 3)
    chunks[1].far(1)
    a_far(4, 0)
    chunks[6].far(1)
    a_far(3, 1)
    chunks[5].far(1)
    a_far(3, 2)
    prepare(0)
    a_far(3, 3)
    chunks[0].group.wait()
    forward(0)
    chunks[4].far(2)
    chunks[7].far(2)
    chunks[3].far(2)
    chunks[1].far(2)
    a_far(4, 1)
    chunks[2].far(2)
    chunks[6].far(2)
    a_far(4, 2)
    chunks[5].far(2)
    a_far(4, 3)
    chunks[4].group.wait()
    chunks[3].group.wait()
    forward(3)
    prepare(7)
    chunks[2].group.wait()
    forward(2)
    chunks[7].group.wait()
    forward(7)
    chunks[1].group.wait()
    forward(1)
    prepare(2)
    chunks[6].group.wait()
    forward(6)
    a_last[0].wait()
    a_last[1].wait()
    a_last[2].wait()
    a_last[3].wait()
    forward(4)
    chunks[5].group.wait()
    forward(5)
    norm_grads()
    units[6].term()
    pack(4)
    units[6].step(1)
    units[5].term()
    units[5].step(1)
    units[0].term()
    units[0].step(1)
    a_step(1, 2)
    a_step(1, 3)
    units[4].term()
    units[4].step(1)
    units[1].term()
    a_step(1, 1)
    units[1].step(1)
    pack(5)
    units[3].term()
    units[3].step(1)
    pack(3)
    units[2].term()
    units[2].step(1)
    units[7].term()
    units[7].step(1)
    units[6].step(2)
    a_step(1, 0)
    pack(7)
    a_step(2, 2)
    units[0].step(2)
    a_step(2, 1)
    units[4].step(2)
    a_step(2, 3)
    pack(6)
    pack(2)
    units[2].step(2)
    units[1].step(2)
    pack(1)
    units[5].step(2)
    units[6].near()
    a_step(2, 0)
    a_step(3, 2)
    units[0].near()
    units[3].step(2)
    units[4].near()
    a_step(3, 1)
    a_step(3, 3)
    pack(0)
    route_plane()
    units[1].near()
    a_step(3, 0)
    units[2].near()
    a_step(4, 2)
    a_step(4, 1)
    units[5].near()
    a_step(4, 3)
    units[3].near()
    units[7].step(2)
    a_step(4, 0)
    units[4].across()
    a_over_y(2)
    a_over_y(1)
    a_over_y(3)
    units[0].across()
    units[1].across()
    unpack()
    units[2].across()
    give(0)
    give(1)
    give(2)
    give(3)
    units[3].across()
    units[7].near()
    units[5].across()
    units[6].across()
    a_over_y(0)
    a_over_x()
    take(0)
    take(1)
    take(2)
    units[7].across()
    take(3)
    finish_bc()
    finish_a()
    assert len(groups) == ARRIVALS
    for copy in copies[-SENDS:]:
        copy.wait_send()


def per_device(tokens, key_cot, routes, counts, widths, key_weight):
    vmem = pl.BlockSpec(memory_space=pltpu.VMEM)
    smem = pl.BlockSpec(memory_space=pltpu.SMEM)
    anywhere = pl.BlockSpec(memory_space=pl.ANY)
    buffers = [
        ((ROWS, WIDTH), BF16),
        ((NZ, NY, NX, FEATS, COLS), BF16),
        ((NZ, SLAB, ROWS), BF16),
        ((NZ, NY, NX, FEATS, COLS), F32),
        ((ROWS, COLS), F32),
        ((ROWS, COLS), BF16),
        ((HEADS * ROWS, HEAD_DIM), BF16),
        ((NZ, ROWS, HEADS * ROWS), BF16),
        ((NZ, NY, NX, 8, HEAD_DIM), BF16),
        ((NZ, NY, NX, 8, HEAD_DIM), BF16),
        ((NZ, NY, NX, 8, HEAD_DIM), BF16),
        ((8 * ROWS, HEAD_DIM), F32),
        ((2 * ROWS, COLS), BF16),
        ((4, 2 * ROWS, SLAB), BF16),
        ((4, 2 * ROWS, SLAB), BF16),
        ((NY, 2, 4, NX, FEATS, 128), BF16),
        ((NY, 2, 4, NX, FEATS, 128), BF16),
        ((NX, FEATS, 128), F32),
        ((NY - 1, NX, FEATS, 128), BF16),
        ((NY - 1, NX, FEATS, 128), BF16),
        ((NX, FEATS, 128), F32),
        ((NX, FEATS, 128), BF16),
        ((NX - 1, FEATS, 128), BF16),
        ((NZ, 2, 2, NY, 16, 384), BF16),
        ((NZ, 2, 2, NY, 16, 384), BF16),
        ((NZ, NY, 16, 384), F32),
        ((NZ, NY, 16, 384), BF16),
        ((NZ, NY - 1, 16, 384), BF16),
        ((NZ, 2, 2, NX, 16, 384), BF16),
        ((NZ, 2, 2, NX, 16, 384), BF16),
        ((NZ, NX, 16, 384), F32),
        ((NZ, NX, 16, 384), BF16),
        ((NZ, NX - 1, 16, 384), BF16),
        ((FEATS, 384), F32),
        ((NZ, FEATS, 384), BF16),
        ((NZ - 1, FEATS, 384), BF16),
    ]
    rows, grad = pl.pallas_call(
        kernel,
        out_shape=(pltpu.VMEM((2 * ROWS, WIDTH // 2), BF16), pltpu.VMEM((FEATS, COLS), F32)),
        in_specs=[anywhere, vmem, vmem, smem, smem, vmem],
        out_specs=(vmem, vmem),
        scratch_shapes=[pltpu.VMEM(shape, dtype) for shape, dtype in buffers]
        + [pltpu.SemaphoreType.DMA((1,)), pltpu.SemaphoreType.DMA((SENDS,)), pltpu.SemaphoreType.DMA((ARRIVALS,))],
        compiler_params=pltpu.CompilerParams(
            collective_id=0, has_side_effects=True, vmem_limit_bytes=58 << 20),
    )(tokens, key_cot, routes.reshape(1, ROWS), counts, widths, key_weight)
    return rows, grad


def solution(mesh):
    return jax.shard_map(
        per_device,
        mesh=mesh,
        in_specs=(P("dp", None), P("dp", "mp"), P("dp", None), P("dp", None), P(), P("dp", "mp")),
        out_specs=(P("dp", "mp"), P("dp", "mp")),
        check_vma=False,
    )
```

```python
import math

import jax
import jax.numpy as jnp
from jax import lax
from jax.experimental import pallas as pl
from jax.experimental.pallas import tpu as pltpu
from jax.sharding import PartitionSpec as P

HEAD_DIM = 128
EPSILON = 1e-06
MESH = pl.DeviceIdType.MESH
NZ, NY, NX = 8, 4, 4
ROWS, WIDTH, COLS, FEATS = 128, 4096, 512, 32
SLAB = WIDTH // NZ
HEADS = COLS // HEAD_DIM
A0, A1 = 384, 512
F32, BF16 = jnp.float32, jnp.bfloat16
SENDS, ARRIVALS, METER = 8, 98, 1024


def kernel(tokens_in, cot, routes, counts, widths, shard, rows_out, grad_out,
           meter, tokens, W, tokT, dW, proj, dl, D, hot, S, R1, R3, Rf, G, DXs, DXr,
           aZs, aZr, a1, aYs, aYr, a2, aXs, aXr,
           bXs, bXr, b1, bYs, bYr, cYs, cYr, c1, cXs, cXr, Zf, Zs, Zr,
           local_sem, send_sem, recv_sem):
    me, m = lax.axis_index("dp"), lax.axis_index("mp")
    x, y, z = lax.rem(me, NX), lax.rem(me // NX, NY), me // (NX * NY)

    def device(zz, yy, xx, mm):
        return ((zz * NY + yy) * NX + xx, mm)

    place = {"x": (NX, x), "y": (NY, y), "z": (NZ, z)}

    def turn(axis, by):
        n, i = place[axis]
        return lax.rem(i + (by % n), n)

    def along(axis, by):
        j = turn(axis, by)
        return {"x": device(z, y, j, m), "y": device(z, j, x, m), "z": device(j, y, x, m)}[axis]

    partner = device(z, y, x, 1 - m)
    copies, groups, sent = [], [], [0] * SENDS

    class Group:
        def __init__(self, ref):
            self.ref, self.sem, self.bytes, self.done = ref, recv_sem.at[len(groups)], 0, False
            groups.append(self)

        def send(self, src, dst, to):
            at = len(copies)
            size = math.prod(src.shape) * src.dtype.itemsize
            copy = pltpu.make_async_remote_copy(
                src_ref=src, dst_ref=dst, send_sem=send_sem.at[at % SENDS], recv_sem=self.sem,
                device_id=to, device_id_type=MESH)
            copy.start()
            copies.append(copy)
            self.bytes += size
            sent[at % SENDS] += size

        def wait(self):
            assert self.bytes == math.prod(self.ref.shape) * self.ref.dtype.itemsize
            self.done = True
            pltpu.make_async_remote_copy(
                src_ref=self.ref, dst_ref=self.ref, send_sem=send_sem.at[0], recv_sem=self.sem,
                device_id=partner, device_id_type=MESH).wait_recv()

    fetch = pltpu.make_async_copy(tokens_in, tokens, local_sem.at[0])
    fetch.start()

    barrier = pltpu.get_barrier_semaphore()
    peers = [along(axis, o) for axis in "xyz" for o in range(1, place[axis][0])] + [partner]
    for peer in peers:
        pl.semaphore_signal(barrier, inc=1, device_id=peer, device_id_type=MESH)
    W[z, y, x] = shard[...]
    pl.semaphore_wait(barrier, len(peers))

    up, down = pl.ds(0, 16), pl.ds(16, 16)
    ca, cb = pl.ds(A0, A1 - A0), pl.ds(0, A0)
    every = pl.ds(0, 4)

    def span(half):
        return every if half is None else pl.ds(half * 2, 2)

    def ring(group, axis, k, region):
        halves = (0, 1) if k == place[axis][0] // 2 else (None, None)
        right, left = region(turn(axis, 1 - k), halves[0]), region(turn(axis, k - 1), halves[1])
        group.send(right, right, along(axis, 1))
        group.send(left, left, along(axis, -1))

    class Chunk:
        def __init__(self, q):
            self.q = q

        def near(self):
            q = self.q
            self.group = Group(W.at[pl.ds(0, 6), 0, 0, up, cb])
            upper, lower = W.at[q, y, x, up, cb], W.at[q, y, x, down, cb]
            for o in range(1, 4):
                self.group.send(upper, upper, along("y", o))
                self.group.send(lower, lower, along("x", o))

        def far(self, k):
            q = self.q
            self.group.wait()
            self.group = Group(W.at[pl.ds(0, 4 // k), every, 0, up, cb])
            ring(self.group, "x", k, lambda j, h: W.at[q, span(h), j, up, cb])
            ring(self.group, "y", k, lambda j, h: W.at[q, j, span(h), down, cb])

    chunks = [Chunk(turn("z", -o)) for o in range(NZ)]
    own_bc = W.at[z, y, x, :, cb]
    from_z = {}
    for o in (4, 3, 5, 2, 6, 1, 7):
        from_z[o] = Group(W.at[0, 0, 0, :, cb])
        from_z[o].send(own_bc, own_bc, along("z", o))
    chunks[0].near()
    own_a = W.at[z, y, x, :, ca]
    a_x = Group(W.at[pl.ds(0, 3), 0, 0, :, ca])
    for o in range(1, NX):
        a_x.send(own_a, own_a, along("x", o))

    def arrive(*offsets):
        for o in offsets:
            from_z[o].wait()
            chunks[o].near()

    def far(k, *offsets):
        for o in offsets:
            chunks[o].far(k)

    a_last = {}

    def a_far(k, oy):
        if k > 1:
            a_last[oy].wait()
        a_last[oy] = Group(W.at[0, 0, every, :, ca] if k == 4 else W.at[pl.ds(0, 2), 0, every, :, ca])
        row = turn("y", -oy)
        ring(a_last[oy], "z", k, lambda j, h: W.at[j, row, span(h), :, ca])

    named = jnp.broadcast_to(routes[...], (ROWS, ROWS))
    first_index = lax.broadcasted_iota(jnp.int32, (ROWS, ROWS), 0)
    second_index = lax.broadcasted_iota(jnp.int32, (ROWS, ROWS), 1)
    same = (named == named.astype(F32).T.astype(jnp.int32)) & (first_index < second_index)
    earlier = jnp.sum(same.astype(F32), axis=0, keepdims=True).astype(jnp.int32)
    slot = (routes[...] * 2 + earlier) * HEADS

    def prepare(s):
        tokT[s] = tokens[:, s * SLAB:(s + 1) * SLAB].T
        for h in range(HEADS):
            hot[s, :, h * ROWS:(h + 1) * ROWS] = (first_index + s * ROWS == slot + h).astype(F32).astype(BF16)

    started = []

    def forward(o):
        q = chunks[o].q
        columns = pl.ds(pl.multiple_of(q * SLAB, SLAB), SLAB)
        term = jnp.dot(tokens[:, columns], W[q].reshape(SLAB, COLS), preferred_element_type=F32)
        if not started:
            started.append(o)
            proj[...] = term
        else:
            proj[...] += term

    a_y = Group(W.at[pl.ds(0, 3), 0, every, :, ca])

    def a_row():
        a_x.wait()
        own = W.at[z, y, every, :, ca]
        for o in range(1, NY):
            a_y.send(own, own, along("y", o))

    position = lax.broadcasted_iota(jnp.int32, (ROWS, 1), 0)
    bound0 = counts[0, 0]
    bound1 = bound0 + counts[0, 1]
    bound2 = bound1 + counts[0, 2]
    row_width = jnp.where(position < bound0, widths[0], jnp.where(
        position < bound1, widths[1], jnp.where(position < bound2, widths[2], widths[3])))

    def norm_grads():
        for h in range(HEADS):
            cols = slice(h * HEAD_DIM, (h + 1) * HEAD_DIM)
            own = proj[:, cols]
            inverse = 1.0 / jnp.sqrt(jnp.mean(own * own, axis=1, keepdims=True) + EPSILON)
            outputs = own * inverse
            head_mask = (m * HEADS + h < row_width).astype(F32)
            upstream = cot[:, cols].astype(F32) * head_mask
            delta = (upstream - outputs * jnp.mean(upstream * outputs, axis=1, keepdims=True)) * inverse
            dl[:, cols] = delta.astype(BF16)
            D[h * ROWS:(h + 1) * ROWS] = delta.astype(BF16)

    def reduce(group, axis, lead, t, local, sbuf, rbuf):
        n, half = place[axis][0], lead // 2
        for d in range(2):
            by = n // 2 - t + 1
            j = turn(axis, by if d == 0 else -by)

            def put(lo, hi, arrived):
                value = local(j, lo, hi)
                if arrived:
                    value += rbuf[d, t - 2, lo:hi].astype(F32)
                sbuf[d, t - 1, lo:hi] = value.astype(BF16)

            first = d * half
            part = pl.ds(0, lead)
            if t == 1:
                put(first, first + half, False)
                part = pl.ds(first, half)
            elif t == 2:
                put(first, first + half, True)
                put(half - first, lead - first, False)
            else:
                put(0, half, True)
                put(half, lead, True)
            group.send(sbuf.at[d, t - 1, part], rbuf.at[d, t - 1, part], along(axis, 1 if d == 0 else -1))

    def ring_sum(axis, lead, local, rbuf):
        n, i = place[axis]
        s = n // 2 - 1
        return (local(i, 0, lead) + rbuf[0, s].astype(F32)) + rbuf[1, s].astype(F32)

    def a_local(k):
        row = turn("y", k)
        return lambda j, lo, hi: dW[j, row, lo:hi, :, A0:A1]

    a_group = {}

    def a_step(t, k):
        if t > 1:
            a_group[k].wait()
        a_group[k] = Group(aZr.at[k, 0, 0] if t == 1 else aZr.at[k, :, 0])
        reduce(a_group[k], "z", NX, t, a_local(k), aZs.at[k], aZr.at[k])

    class Unit:
        def __init__(self, at, o):
            self.at, self.o, self.q = at, o, turn("z", -o)
            q = self.q
            self.b_local = lambda j, lo, hi: dW[q, lo:hi, j, 0:16, 0:A0]
            self.c_local = lambda j, lo, hi: dW[q, j, lo:hi, 16:32, 0:A0]

        def term(self):
            part = jnp.dot(tokT[self.q], dl[...], preferred_element_type=F32)
            dW[self.q] = part.reshape(NY, NX, FEATS, COLS)

        def step(self, t):
            at = self.at
            if t > 1:
                self.group.wait()
            self.group = Group(bXr.at[at, :, 0] if t == 1 else bXr.at[at])
            reduce(self.group, "x", NY, t, self.b_local, bXs.at[at], bXr.at[at])
            reduce(self.group, "y", NX, t, self.c_local, cYs.at[at], cYr.at[at])

        def near(self):
            at = self.at
            self.group.wait()
            self.group = Group(W.at[pl.ds(0, 6), 0, 0, up, cb])
            total = ring_sum("x", NY, self.b_local, bXr.at[at])
            b1[at] = total
            bYs[at] = total.astype(BF16)
            for o in range(1, 4):
                self.group.send(bYs.at[at, turn("y", o)], bYr.at[at, o - 1], along("y", o))
            total = ring_sum("y", NX, self.c_local, cYr.at[at])
            c1[at] = total
            cXs[at] = total.astype(BF16)
            for o in range(1, 4):
                self.group.send(cXs.at[at, turn("x", o)], cXr.at[at, o - 1], along("x", o))

        def across(self):
            at = self.at
            self.group.wait()
            for mine, arrived, rows, i in ((b1, bYr, slice(0, 16), y), (c1, cXr, slice(16, 32), x)):
                total = mine[at, i]
                for k in range(3):
                    total += arrived[at, k].astype(F32)
                if self.o == 0:
                    Zf[rows] = total
                else:
                    Zs[at, rows] = total.astype(BF16)
            if self.o:
                to_z.send(Zs.at[at], Zr.at[self.o - 1], along("z", -self.o))

    to_z = Group(Zr)
    units = [Unit(at, o) for at, o in enumerate((4, 3, 5, 2, 6, 1, 7, 0))]

    r_z = Group(R1.at[pl.ds(0, 7)])
    r_xy = Group(W.at[pl.ds(0, 5), pl.ds(0, 3), pl.ds(0, 2), :, ca])
    all_z = pl.ds(0, NZ)

    def pack(o):
        j = turn("z", o)
        packed = jnp.dot(hot[j], D[...], preferred_element_type=F32)
        packed = packed.reshape(NY, NX, 8, HEAD_DIM).astype(BF16)
        if o:
            S[j] = packed
            r_z.send(S.at[j], R1.at[z], along("z", o))
        else:
            R1[z] = packed

    def route_plane():
        r_z.wait()
        for oy in range(NY):
            for ox in range(NX):
                jy, jx = turn("y", oy), turn("x", ox)
                if oy or ox:
                    r_xy.send(R1.at[all_z, jy, jx], R3.at[all_z, y, x], device(z, jy, jx, m))
        for s in range(NZ):
            R3[s, y, x] = R1[s, y, x]

    def unpack():
        r_xy.wait()
        Rf[...] = R3[...].astype(F32).reshape(8 * ROWS, HEAD_DIM)
        for h in range(HEADS):
            G[:, h * HEAD_DIM:(h + 1) * HEAD_DIM] = Rf[pl.ds(h, 2 * ROWS, stride=HEADS), :].astype(BF16)

    def product(tile):
        return lax.dot_general(G[...], W[tile].reshape(SLAB, COLS), (((1,), (1,)), ((), ())),
                               preferred_element_type=F32).astype(BF16)

    halves = []

    def give(t):
        DXs[t] = product((1 - m) * 4 + t)
        group = Group(DXr.at[t])
        group.send(DXs.at[t], DXr.at[t], partner)
        halves.append(group)

    def take(t):
        own = product(m * 4 + t).astype(F32)
        halves[t].wait()
        rows_out[:, t * SLAB:(t + 1) * SLAB] = (own + DXr[t].astype(F32)).astype(BF16)

    ra_y, ra_x = Group(aYr), Group(aXr)
    scale = 1.0 / 128.0

    def a_over_y(k):
        a_group[k].wait()
        total = ring_sum("z", NX, a_local(k), aZr.at[k])
        if k == 0:
            a1[...] = total
        else:
            aYs[k - 1] = total.astype(BF16)
            ra_y.send(aYs.at[k - 1], aYr.at[k - 1], along("y", k))

    def a_over_x():
        ra_y.wait()
        total = a1[...]
        for o in range(NY - 1):
            total += aYr[o].astype(F32)
        a2[...] = total
        aXs[...] = total.astype(BF16)
        for o in range(1, NX):
            ra_x.send(aXs.at[turn("x", o)], aXr.at[o - 1], along("x", o))

    def finish_bc():
        to_z.wait()
        total = Zf[...]
        for o in range(NZ - 1):
            total += Zr[o].astype(F32)
        grad_out[:, 0:A0] = total * scale

    def finish_a():
        ra_x.wait()
        total = a2[x]
        for o in range(NX - 1):
            total += aXr[o].astype(F32)
        grad_out[:, A0:A1] = total * scale

    fetch.wait()
    a_row()
    a_far(1, 0)
    prepare(1)
    arrive(4)
    chunks[0].far(1)
    prepare(4)
    arrive(5)
    arrive(3)
    arrive(2)
    arrive(1)
    a_far(2, 0)
    arrive(6)
    a_y.wait()
    a_far(1, 1)
    a_far(1, 2)
    a_far(1, 3)
    prepare(5)
    arrive(7)
    chunks[0].far(2)
    chunks[4].far(1)
    chunks[3].far(1)
    prepare(6)
    a_far(3, 0)
    a_far(2, 1)
    chunks[2].far(1)
    prepare(3)
    a_far(2, 2)
    chunks[7].far(1)
    a_far(2, 3)
    chunks[1].far(1)
    a_far(4, 0)
    chunks[6].far(1)
    a_far(3, 1)
    chunks[5].far(1)
    a_far(3, 2)
    prepare(0)
    a_far(3, 3)
    chunks[0].group.wait()
    forward(0)
    chunks[4].far(2)
    chunks[7].far(2)
    chunks[3].far(2)
    chunks[1].far(2)
    a_far(4, 1)
    chunks[2].far(2)
    chunks[6].far(2)
    a_far(4, 2)
    chunks[5].far(2)
    a_far(4, 3)
    chunks[4].group.wait()
    chunks[3].group.wait()
    forward(3)
    prepare(7)
    chunks[2].group.wait()
    forward(2)
    chunks[7].group.wait()
    forward(7)
    chunks[1].group.wait()
    forward(1)
    prepare(2)
    chunks[6].group.wait()
    forward(6)
    a_last[0].wait()
    a_last[1].wait()
    a_last[2].wait()
    a_last[3].wait()
    forward(4)
    chunks[5].group.wait()
    forward(5)
    norm_grads()
    units[6].term()
    pack(4)
    units[6].step(1)
    units[5].term()
    units[5].step(1)
    units[0].term()
    units[0].step(1)
    a_step(1, 2)
    a_step(1, 3)
    units[4].term()
    units[4].step(1)
    units[1].term()
    a_step(1, 1)
    units[1].step(1)
    pack(5)
    units[3].term()
    units[3].step(1)
    pack(3)
    units[2].term()
    units[2].step(1)
    units[7].term()
    units[7].step(1)
    units[6].step(2)
    a_step(1, 0)
    pack(7)
    a_step(2, 2)
    units[0].step(2)
    a_step(2, 1)
    units[4].step(2)
    a_step(2, 3)
    pack(6)
    pack(2)
    units[2].step(2)
    units[1].step(2)
    pack(1)
    units[5].step(2)
    units[6].near()
    a_step(2, 0)
    a_step(3, 2)
    units[0].near()
    units[3].step(2)
    units[4].near()
    a_step(3, 1)
    a_step(3, 3)
    pack(0)
    route_plane()
    units[1].near()
    a_step(3, 0)
    units[2].near()
    a_step(4, 2)
    a_step(4, 1)
    units[5].near()
    a_step(4, 3)
    units[3].near()
    units[7].step(2)
    a_step(4, 0)
    units[4].across()
    a_over_y(2)
    a_over_y(1)
    a_over_y(3)
    units[0].across()
    units[1].across()
    unpack()
    units[2].across()
    give(0)
    give(1)
    give(2)
    give(3)
    units[3].across()
    units[7].near()
    units[5].across()
    units[6].across()
    a_over_y(0)
    a_over_x()
    take(0)
    take(1)
    take(2)
    units[7].across()
    take(3)
    finish_bc()
    finish_a()
    assert len(groups) == ARRIVALS
    for k in range(SENDS):
        assert sent[k] % 4096 == 0 and sent[k] <= METER * 4096
        all_of_them = meter.at[pl.ds(0, sent[k] // 4096)]
        pltpu.make_async_remote_copy(
            src_ref=all_of_them, dst_ref=all_of_them, send_sem=send_sem.at[k], recv_sem=recv_sem.at[0],
            device_id=partner, device_id_type=MESH).wait_send()


def per_device(tokens, key_cot, routes, counts, widths, key_weight):
    vmem = pl.BlockSpec(memory_space=pltpu.VMEM)
    smem = pl.BlockSpec(memory_space=pltpu.SMEM)
    anywhere = pl.BlockSpec(memory_space=pl.ANY)
    buffers = [
        ((METER, 8, 128), F32),
        ((ROWS, WIDTH), BF16),
        ((NZ, NY, NX, FEATS, COLS), BF16),
        ((NZ, SLAB, ROWS), BF16),
        ((NZ, NY, NX, FEATS, COLS), F32),
        ((ROWS, COLS), F32),
        ((ROWS, COLS), BF16),
        ((HEADS * ROWS, HEAD_DIM), BF16),
        ((NZ, ROWS, HEADS * ROWS), BF16),
        ((NZ, NY, NX, 8, HEAD_DIM), BF16),
        ((NZ, NY, NX, 8, HEAD_DIM), BF16),
        ((NZ, NY, NX, 8, HEAD_DIM), BF16),
        ((8 * ROWS, HEAD_DIM), F32),
        ((2 * ROWS, COLS), BF16),
        ((4, 2 * ROWS, SLAB), BF16),
        ((4, 2 * ROWS, SLAB), BF16),
        ((NY, 2, 4, NX, FEATS, 128), BF16),
        ((NY, 2, 4, NX, FEATS, 128), BF16),
        ((NX, FEATS, 128), F32),
        ((NY - 1, NX, FEATS, 128), BF16),
        ((NY - 1, NX, FEATS, 128), BF16),
        ((NX, FEATS, 128), F32),
        ((NX, FEATS, 128), BF16),
        ((NX - 1, FEATS, 128), BF16),
        ((NZ, 2, 2, NY, 16, 384), BF16),
        ((NZ, 2, 2, NY, 16, 384), BF16),
        ((NZ, NY, 16, 384), F32),
        ((NZ, NY, 16, 384), BF16),
        ((NZ, NY - 1, 16, 384), BF16),
        ((NZ, 2, 2, NX, 16, 384), BF16),
        ((NZ, 2, 2, NX, 16, 384), BF16),
        ((NZ, NX, 16, 384), F32),
        ((NZ, NX, 16, 384), BF16),
        ((NZ, NX - 1, 16, 384), BF16),
        ((FEATS, 384), F32),
        ((NZ, FEATS, 384), BF16),
        ((NZ - 1, FEATS, 384), BF16),
    ]
    rows, grad = pl.pallas_call(
        kernel,
        out_shape=(pltpu.VMEM((2 * ROWS, WIDTH // 2), BF16), pltpu.VMEM((FEATS, COLS), F32)),
        in_specs=[anywhere, vmem, vmem, smem, smem, vmem],
        out_specs=(vmem, vmem),
        scratch_shapes=[pltpu.VMEM(shape, dtype) for shape, dtype in buffers]
        + [pltpu.SemaphoreType.DMA((1,)), pltpu.SemaphoreType.DMA((SENDS,)), pltpu.SemaphoreType.DMA((ARRIVALS,))],
        compiler_params=pltpu.CompilerParams(
            collective_id=0, has_side_effects=True, vmem_limit_bytes=58 << 20),
    )(tokens, key_cot, routes.reshape(1, ROWS), counts, widths, key_weight)
    return rows, grad


def solution(mesh):
    return jax.shard_map(
        per_device,
        mesh=mesh,
        in_specs=(P("dp", None), P("dp", "mp"), P("dp", None), P("dp", None), P(), P("dp", "mp")),
        out_specs=(P("dp", "mp"), P("dp", "mp")),
        check_vma=False,
    )
```

```python
import math

import jax
import jax.numpy as jnp
from jax import lax
from jax.experimental import pallas as pl
from jax.experimental.pallas import tpu as pltpu
from jax.sharding import PartitionSpec as P

HEAD_DIM = 128
EPSILON = 1e-06
MESH = pl.DeviceIdType.MESH
NZ, NY, NX = 8, 4, 4
ROWS, WIDTH, COLS, FEATS = 128, 4096, 512, 32
SLAB = WIDTH // NZ
HEADS = COLS // HEAD_DIM
A0, A1 = 384, 512
F32, BF16 = jnp.float32, jnp.bfloat16
SENDS, ARRIVALS, METER = 8, 98, 1024


def kernel(tokens_in, cot_in, routes_in, counts_in, widths_in, shard, rows_out, grad_out,
           meter, tokens, cot, routes, counts, widths, W, tokT, dW, proj, dl, D, hot, S, R1, R3, Rf, G, DXs, DXr,
           aZs, aZr, a1, aYs, aYr, a2, aXs, aXr,
           bXs, bXr, b1, bYs, bYr, cYs, cYr, c1, cXs, cXr, Zf, Zs, Zr,
           local_sem, send_sem, recv_sem):
    me, m = lax.axis_index("dp"), lax.axis_index("mp")
    x, y, z = lax.rem(me, NX), lax.rem(me // NX, NY), me // (NX * NY)

    def device(zz, yy, xx, mm):
        return ((zz * NY + yy) * NX + xx, mm)

    place = {"x": (NX, x), "y": (NY, y), "z": (NZ, z)}

    def turn(axis, by):
        n, i = place[axis]
        return lax.rem(i + (by % n), n)

    def along(axis, by):
        j = turn(axis, by)
        return {"x": device(z, y, j, m), "y": device(z, j, x, m), "z": device(j, y, x, m)}[axis]

    partner = device(z, y, x, 1 - m)
    copies, groups, sent = [], [], [0] * SENDS

    class Group:
        def __init__(self, ref):
            self.ref, self.sem, self.bytes, self.done = ref, recv_sem.at[len(groups)], 0, False
            groups.append(self)

        def send(self, src, dst, to):
            at = len(copies)
            size = math.prod(src.shape) * src.dtype.itemsize
            copy = pltpu.make_async_remote_copy(
                src_ref=src, dst_ref=dst, send_sem=send_sem.at[at % SENDS], recv_sem=self.sem,
                device_id=to, device_id_type=MESH)
            copy.start()
            copies.append(copy)
            self.bytes += size
            sent[at % SENDS] += size

        def wait(self):
            assert self.bytes == math.prod(self.ref.shape) * self.ref.dtype.itemsize
            self.done = True
            pltpu.make_async_remote_copy(
                src_ref=self.ref, dst_ref=self.ref, send_sem=send_sem.at[0], recv_sem=self.sem,
                device_id=partner, device_id_type=MESH).wait_recv()

    own_shard = pltpu.make_async_copy(shard, W.at[z, y, x], local_sem.at[0])
    own_shard.start()
    fetches = [pltpu.make_async_copy(src, dst, local_sem.at[at + 1]) for at, (src, dst) in enumerate((
        (routes_in, routes), (counts_in, counts), (widths_in, widths), (cot_in, cot), (tokens_in, tokens)))]
    for fetch in fetches:
        fetch.start()

    barrier = pltpu.get_barrier_semaphore()
    peers = [along(axis, o) for axis in "xyz" for o in range(1, place[axis][0])] + [partner]
    for peer in peers:
        pl.semaphore_signal(barrier, inc=1, device_id=peer, device_id_type=MESH)
    own_shard.wait()
    pl.semaphore_wait(barrier, len(peers))

    up, down = pl.ds(0, 16), pl.ds(16, 16)
    ca, cb = pl.ds(A0, A1 - A0), pl.ds(0, A0)
    every = pl.ds(0, 4)

    def span(half):
        return every if half is None else pl.ds(half * 2, 2)

    def ring(group, axis, k, region):
        halves = (0, 1) if k == place[axis][0] // 2 else (None, None)
        right, left = region(turn(axis, 1 - k), halves[0]), region(turn(axis, k - 1), halves[1])
        group.send(right, right, along(axis, 1))
        group.send(left, left, along(axis, -1))

    class Chunk:
        def __init__(self, q):
            self.q = q

        def near(self):
            q = self.q
            self.group = Group(W.at[pl.ds(0, 6), 0, 0, up, cb])
            upper, lower = W.at[q, y, x, up, cb], W.at[q, y, x, down, cb]
            for o in range(1, 4):
                self.group.send(upper, upper, along("y", o))
                self.group.send(lower, lower, along("x", o))

        def far(self, k):
            q = self.q
            self.group.wait()
            self.group = Group(W.at[pl.ds(0, 4 // k), every, 0, up, cb])
            ring(self.group, "x", k, lambda j, h: W.at[q, span(h), j, up, cb])
            ring(self.group, "y", k, lambda j, h: W.at[q, j, span(h), down, cb])

    chunks = [Chunk(turn("z", -o)) for o in range(NZ)]
    own_bc = W.at[z, y, x, :, cb]
    from_z = {}
    for o in (4, 3, 5, 2, 6, 1, 7):
        from_z[o] = Group(W.at[0, 0, 0, :, cb])
        from_z[o].send(own_bc, own_bc, along("z", o))
    chunks[0].near()
    own_a = W.at[z, y, x, :, ca]
    a_x = Group(W.at[pl.ds(0, 3), 0, 0, :, ca])
    for o in range(1, NX):
        a_x.send(own_a, own_a, along("x", o))

    def arrive(*offsets):
        for o in offsets:
            from_z[o].wait()
            chunks[o].near()

    def far(k, *offsets):
        for o in offsets:
            chunks[o].far(k)

    a_last = {}

    def a_far(k, oy):
        if k > 1:
            a_last[oy].wait()
        a_last[oy] = Group(W.at[0, 0, every, :, ca] if k == 4 else W.at[pl.ds(0, 2), 0, every, :, ca])
        row = turn("y", -oy)
        ring(a_last[oy], "z", k, lambda j, h: W.at[j, row, span(h), :, ca])

    for fetch in fetches:
        fetch.wait()
    named = jnp.broadcast_to(routes[...], (ROWS, ROWS))
    first_index = lax.broadcasted_iota(jnp.int32, (ROWS, ROWS), 0)
    second_index = lax.broadcasted_iota(jnp.int32, (ROWS, ROWS), 1)
    same = (named == named.astype(F32).T.astype(jnp.int32)) & (first_index < second_index)
    earlier = jnp.sum(same.astype(F32), axis=0, keepdims=True).astype(jnp.int32)
    slot = (routes[...] * 2 + earlier) * HEADS

    def prepare(s):
        tokT[s] = tokens[:, s * SLAB:(s + 1) * SLAB].T
        for h in range(HEADS):
            hot[s, :, h * ROWS:(h + 1) * ROWS] = (first_index + s * ROWS == slot + h).astype(F32).astype(BF16)

    started = []

    def forward(o):
        q = chunks[o].q
        columns = pl.ds(pl.multiple_of(q * SLAB, SLAB), SLAB)
        term = jnp.dot(tokens[:, columns], W[q].reshape(SLAB, COLS), preferred_element_type=F32)
        if not started:
            started.append(o)
            proj[...] = term
        else:
            proj[...] += term

    a_y = Group(W.at[pl.ds(0, 3), 0, every, :, ca])

    def a_row():
        a_x.wait()
        own = W.at[z, y, every, :, ca]
        for o in range(1, NY):
            a_y.send(own, own, along("y", o))

    position = lax.broadcasted_iota(jnp.int32, (ROWS, 1), 0)
    bound0 = counts[0, 0]
    bound1 = bound0 + counts[0, 1]
    bound2 = bound1 + counts[0, 2]
    row_width = jnp.where(position < bound0, widths[0], jnp.where(
        position < bound1, widths[1], jnp.where(position < bound2, widths[2], widths[3])))

    def norm_grads():
        for h in range(HEADS):
            cols = slice(h * HEAD_DIM, (h + 1) * HEAD_DIM)
            own = proj[:, cols]
            inverse = 1.0 / jnp.sqrt(jnp.mean(own * own, axis=1, keepdims=True) + EPSILON)
            outputs = own * inverse
            head_mask = (m * HEADS + h < row_width).astype(F32)
            upstream = cot[:, cols].astype(F32) * head_mask
            delta = (upstream - outputs * jnp.mean(upstream * outputs, axis=1, keepdims=True)) * inverse
            dl[:, cols] = delta.astype(BF16)
            D[h * ROWS:(h + 1) * ROWS] = delta.astype(BF16)

    def reduce(group, axis, lead, t, local, sbuf, rbuf):
        n, half = place[axis][0], lead // 2
        for d in range(2):
            by = n // 2 - t + 1
            j = turn(axis, by if d == 0 else -by)

            def put(lo, hi, arrived):
                value = local(j, lo, hi)
                if arrived:
                    value += rbuf[d, t - 2, lo:hi].astype(F32)
                sbuf[d, t - 1, lo:hi] = value.astype(BF16)

            first = d * half
            part = pl.ds(0, lead)
            if t == 1:
                put(first, first + half, False)
                part = pl.ds(first, half)
            elif t == 2:
                put(first, first + half, True)
                put(half - first, lead - first, False)
            else:
                put(0, half, True)
                put(half, lead, True)
            group.send(sbuf.at[d, t - 1, part], rbuf.at[d, t - 1, part], along(axis, 1 if d == 0 else -1))

    def ring_sum(axis, lead, local, rbuf):
        n, i = place[axis]
        s = n // 2 - 1
        return (local(i, 0, lead) + rbuf[0, s].astype(F32)) + rbuf[1, s].astype(F32)

    def a_local(k):
        row = turn("y", k)
        return lambda j, lo, hi: dW[j, row, lo:hi, :, A0:A1]

    a_group = {}

    def a_step(t, k):
        if t > 1:
            a_group[k].wait()
        a_group[k] = Group(aZr.at[k, 0, 0] if t == 1 else aZr.at[k, :, 0])
        reduce(a_group[k], "z", NX, t, a_local(k), aZs.at[k], aZr.at[k])

    class Unit:
        def __init__(self, at, o):
            self.at, self.o, self.q = at, o, turn("z", -o)
            q = self.q
            self.b_local = lambda j, lo, hi: dW[q, lo:hi, j, 0:16, 0:A0]
            self.c_local = lambda j, lo, hi: dW[q, j, lo:hi, 16:32, 0:A0]

        def term(self):
            part = jnp.dot(tokT[self.q], dl[...], preferred_element_type=F32)
            dW[self.q] = part.reshape(NY, NX, FEATS, COLS)

        def step(self, t):
            at = self.at
            if t > 1:
                self.group.wait()
            self.group = Group(bXr.at[at, :, 0] if t == 1 else bXr.at[at])
            reduce(self.group, "x", NY, t, self.b_local, bXs.at[at], bXr.at[at])
            reduce(self.group, "y", NX, t, self.c_local, cYs.at[at], cYr.at[at])

        def near(self):
            at = self.at
            self.group.wait()
            self.group = Group(W.at[pl.ds(0, 6), 0, 0, up, cb])
            total = ring_sum("x", NY, self.b_local, bXr.at[at])
            b1[at] = total
            bYs[at] = total.astype(BF16)
            for o in range(1, 4):
                self.group.send(bYs.at[at, turn("y", o)], bYr.at[at, o - 1], along("y", o))
            total = ring_sum("y", NX, self.c_local, cYr.at[at])
            c1[at] = total
            cXs[at] = total.astype(BF16)
            for o in range(1, 4):
                self.group.send(cXs.at[at, turn("x", o)], cXr.at[at, o - 1], along("x", o))

        def across(self):
            at = self.at
            self.group.wait()
            for mine, arrived, rows, i in ((b1, bYr, slice(0, 16), y), (c1, cXr, slice(16, 32), x)):
                total = mine[at, i]
                for k in range(3):
                    total += arrived[at, k].astype(F32)
                if self.o == 0:
                    Zf[rows] = total
                else:
                    Zs[at, rows] = total.astype(BF16)
            if self.o:
                to_z.send(Zs.at[at], Zr.at[self.o - 1], along("z", -self.o))

    to_z = Group(Zr)
    units = [Unit(at, o) for at, o in enumerate((4, 3, 5, 2, 6, 1, 7, 0))]

    r_z = Group(R1.at[pl.ds(0, 7)])
    r_xy = Group(W.at[pl.ds(0, 5), pl.ds(0, 3), pl.ds(0, 2), :, ca])
    all_z = pl.ds(0, NZ)

    def pack(o):
        j = turn("z", o)
        packed = jnp.dot(hot[j], D[...], preferred_element_type=F32)
        packed = packed.reshape(NY, NX, 8, HEAD_DIM).astype(BF16)
        if o:
            S[j] = packed
            r_z.send(S.at[j], R1.at[z], along("z", o))
        else:
            R1[z] = packed

    def route_plane():
        r_z.wait()
        for oy in range(NY):
            for ox in range(NX):
                jy, jx = turn("y", oy), turn("x", ox)
                if oy or ox:
                    r_xy.send(R1.at[all_z, jy, jx], R3.at[all_z, y, x], device(z, jy, jx, m))
        for s in range(NZ):
            R3[s, y, x] = R1[s, y, x]

    def unpack():
        r_xy.wait()
        Rf[...] = R3[...].astype(F32).reshape(8 * ROWS, HEAD_DIM)
        for h in range(HEADS):
            G[:, h * HEAD_DIM:(h + 1) * HEAD_DIM] = Rf[pl.ds(h, 2 * ROWS, stride=HEADS), :].astype(BF16)

    def product(tile):
        return lax.dot_general(G[...], W[tile].reshape(SLAB, COLS), (((1,), (1,)), ((), ())),
                               preferred_element_type=F32).astype(BF16)

    halves = []

    def give(t):
        DXs[t] = product((1 - m) * 4 + t)
        group = Group(DXr.at[t])
        group.send(DXs.at[t], DXr.at[t], partner)
        halves.append(group)

    def take(t):
        own = product(m * 4 + t).astype(F32)
        halves[t].wait()
        rows_out[:, t * SLAB:(t + 1) * SLAB] = (own + DXr[t].astype(F32)).astype(BF16)

    ra_y, ra_x = Group(aYr), Group(aXr)
    scale = 1.0 / 128.0

    def a_over_y(k):
        a_group[k].wait()
        total = ring_sum("z", NX, a_local(k), aZr.at[k])
        if k == 0:
            a1[...] = total
        else:
            aYs[k - 1] = total.astype(BF16)
            ra_y.send(aYs.at[k - 1], aYr.at[k - 1], along("y", k))

    def a_over_x():
        ra_y.wait()
        total = a1[...]
        for o in range(NY - 1):
            total += aYr[o].astype(F32)
        a2[...] = total
        aXs[...] = total.astype(BF16)
        for o in range(1, NX):
            ra_x.send(aXs.at[turn("x", o)], aXr.at[o - 1], along("x", o))

    def finish_bc():
        to_z.wait()
        total = Zf[...]
        for o in range(NZ - 1):
            total += Zr[o].astype(F32)
        grad_out[:, 0:A0] = total * scale

    def finish_a():
        ra_x.wait()
        total = a2[x]
        for o in range(NX - 1):
            total += aXr[o].astype(F32)
        grad_out[:, A0:A1] = total * scale

    a_row()
    a_far(1, 0)
    prepare(1)
    arrive(4)
    chunks[0].far(1)
    prepare(4)
    arrive(5)
    arrive(3)
    arrive(2)
    arrive(1)
    a_far(2, 0)
    arrive(6)
    a_y.wait()
    a_far(1, 1)
    a_far(1, 2)
    a_far(1, 3)
    prepare(5)
    arrive(7)
    chunks[0].far(2)
    chunks[4].far(1)
    chunks[3].far(1)
    prepare(6)
    a_far(3, 0)
    a_far(2, 1)
    chunks[2].far(1)
    prepare(3)
    a_far(2, 2)
    chunks[7].far(1)
    a_far(2, 3)
    chunks[1].far(1)
    a_far(4, 0)
    chunks[6].far(1)
    a_far(3, 1)
    chunks[5].far(1)
    a_far(3, 2)
    prepare(0)
    a_far(3, 3)
    chunks[0].group.wait()
    forward(0)
    chunks[4].far(2)
    chunks[7].far(2)
    chunks[3].far(2)
    chunks[1].far(2)
    a_far(4, 1)
    chunks[2].far(2)
    chunks[6].far(2)
    a_far(4, 2)
    chunks[5].far(2)
    a_far(4, 3)
    chunks[4].group.wait()
    chunks[3].group.wait()
    forward(3)
    prepare(7)
    chunks[2].group.wait()
    forward(2)
    chunks[7].group.wait()
    forward(7)
    chunks[1].group.wait()
    forward(1)
    prepare(2)
    chunks[6].group.wait()
    forward(6)
    a_last[0].wait()
    a_last[1].wait()
    a_last[2].wait()
    a_last[3].wait()
    forward(4)
    chunks[5].group.wait()
    forward(5)
    norm_grads()
    units[6].term()
    pack(4)
    units[6].step(1)
    units[5].term()
    units[5].step(1)
    units[0].term()
    units[0].step(1)
    a_step(1, 2)
    a_step(1, 3)
    units[4].term()
    units[4].step(1)
    units[1].term()
    a_step(1, 1)
    units[1].step(1)
    pack(5)
    units[3].term()
    units[3].step(1)
    pack(3)
    units[2].term()
    units[2].step(1)
    units[7].term()
    units[7].step(1)
    units[6].step(2)
    a_step(1, 0)
    pack(7)
    a_step(2, 2)
    units[0].step(2)
    a_step(2, 1)
    units[4].step(2)
    a_step(2, 3)
    pack(6)
    pack(2)
    units[2].step(2)
    units[1].step(2)
    pack(1)
    units[5].step(2)
    units[6].near()
    a_step(2, 0)
    a_step(3, 2)
    units[0].near()
    units[3].step(2)
    units[4].near()
    a_step(3, 1)
    a_step(3, 3)
    pack(0)
    route_plane()
    units[1].near()
    a_step(3, 0)
    units[2].near()
    a_step(4, 2)
    a_step(4, 1)
    units[5].near()
    a_step(4, 3)
    units[3].near()
    units[7].step(2)
    a_step(4, 0)
    units[4].across()
    a_over_y(2)
    a_over_y(1)
    a_over_y(3)
    units[0].across()
    units[1].across()
    unpack()
    units[2].across()
    give(0)
    give(1)
    give(2)
    give(3)
    units[3].across()
    units[7].near()
    units[5].across()
    units[6].across()
    a_over_y(0)
    a_over_x()
    take(0)
    take(1)
    take(2)
    units[7].across()
    take(3)
    finish_bc()
    finish_a()
    assert len(groups) == ARRIVALS
    for k in range(SENDS):
        assert sent[k] % 4096 == 0 and sent[k] <= METER * 4096
        all_of_them = meter.at[pl.ds(0, sent[k] // 4096)]
        pltpu.make_async_remote_copy(
            src_ref=all_of_them, dst_ref=all_of_them, send_sem=send_sem.at[k], recv_sem=recv_sem.at[0],
            device_id=partner, device_id_type=MESH).wait_send()


def per_device(tokens, key_cot, routes, counts, widths, key_weight):
    vmem = pl.BlockSpec(memory_space=pltpu.VMEM)
    anywhere = pl.BlockSpec(memory_space=pl.ANY)
    buffers = [
        ((METER, 8, 128), F32),
        ((ROWS, WIDTH), BF16),
        ((ROWS, COLS), BF16),
        ((1, ROWS), jnp.int32),
        ((NZ, NY, NX, FEATS, COLS), BF16),
        ((NZ, SLAB, ROWS), BF16),
        ((NZ, NY, NX, FEATS, COLS), F32),
        ((ROWS, COLS), F32),
        ((ROWS, COLS), BF16),
        ((HEADS * ROWS, HEAD_DIM), BF16),
        ((NZ, ROWS, HEADS * ROWS), BF16),
        ((NZ, NY, NX, 8, HEAD_DIM), BF16),
        ((NZ, NY, NX, 8, HEAD_DIM), BF16),
        ((NZ, NY, NX, 8, HEAD_DIM), BF16),
        ((8 * ROWS, HEAD_DIM), F32),
        ((2 * ROWS, COLS), BF16),
        ((4, 2 * ROWS, SLAB), BF16),
        ((4, 2 * ROWS, SLAB), BF16),
        ((NY, 2, 4, NX, FEATS, 128), BF16),
        ((NY, 2, 4, NX, FEATS, 128), BF16),
        ((NX, FEATS, 128), F32),
        ((NY - 1, NX, FEATS, 128), BF16),
        ((NY - 1, NX, FEATS, 128), BF16),
        ((NX, FEATS, 128), F32),
        ((NX, FEATS, 128), BF16),
        ((NX - 1, FEATS, 128), BF16),
        ((NZ, 2, 2, NY, 16, 384), BF16),
        ((NZ, 2, 2, NY, 16, 384), BF16),
        ((NZ, NY, 16, 384), F32),
        ((NZ, NY, 16, 384), BF16),
        ((NZ, NY - 1, 16, 384), BF16),
        ((NZ, 2, 2, NX, 16, 384), BF16),
        ((NZ, 2, 2, NX, 16, 384), BF16),
        ((NZ, NX, 16, 384), F32),
        ((NZ, NX, 16, 384), BF16),
        ((NZ, NX - 1, 16, 384), BF16),
        ((FEATS, 384), F32),
        ((NZ, FEATS, 384), BF16),
        ((NZ - 1, FEATS, 384), BF16),
    ]
    rows, grad = pl.pallas_call(
        kernel,
        out_shape=(pltpu.VMEM((2 * ROWS, WIDTH // 2), BF16), pltpu.VMEM((FEATS, COLS), F32)),
        in_specs=[anywhere] * 6,
        out_specs=(vmem, vmem),
        scratch_shapes=[pltpu.VMEM(shape, dtype) for shape, dtype in buffers[:4]]
        + [pltpu.SMEM((1, 4), jnp.int32), pltpu.SMEM((4,), jnp.int32)]
        + [pltpu.VMEM(shape, dtype) for shape, dtype in buffers[4:]]
        + [pltpu.SemaphoreType.DMA((6,)), pltpu.SemaphoreType.DMA((SENDS,)), pltpu.SemaphoreType.DMA((ARRIVALS,))],
        compiler_params=pltpu.CompilerParams(
            collective_id=0, has_side_effects=True, vmem_limit_bytes=58 << 20),
    )(tokens, key_cot, routes.reshape(1, ROWS), counts, widths, key_weight)
    return rows, grad


def solution(mesh):
    return jax.shard_map(
        per_device,
        mesh=mesh,
        in_specs=(P("dp", None), P("dp", "mp"), P("dp", None), P("dp", None), P(), P("dp", "mp")),
        out_specs=(P("dp", "mp"), P("dp", "mp")),
        check_vma=False,
    )
```

```python
import math

import jax
import jax.numpy as jnp
from jax import lax
from jax.experimental import pallas as pl
from jax.experimental.pallas import tpu as pltpu
from jax.sharding import PartitionSpec as P

HEAD_DIM = 128
EPSILON = 1e-06
MESH = pl.DeviceIdType.MESH
NZ, NY, NX = 8, 4, 4
ROWS, WIDTH, COLS, FEATS = 128, 4096, 512, 32
SLAB = WIDTH // NZ
HEADS = COLS // HEAD_DIM
A0, A1 = 384, 512
F32, BF16 = jnp.float32, jnp.bfloat16
SENDS, ARRIVALS, METER = 8, 98, 1024


def kernel(tokens_in, cot_in, routes_in, counts_in, widths_in, shard, rows_out, grad_out,
           meter, tokens, cot, routes, counts, widths, W, tokT, dW, proj, dl, D, hot, S, R1, R3, Rf, G, DXs, DXr,
           aZs, aZr, a1, aYs, aYr, a2, aXs, aXr,
           bXs, bXr, b1, bYs, bYr, cYs, cYr, c1, cXs, cXr, Zf, Zs, Zr,
           local_sem, send_sem, recv_sem):
    me, m = lax.axis_index("dp"), lax.axis_index("mp")
    x, y, z = lax.rem(me, NX), lax.rem(me // NX, NY), me // (NX * NY)

    def device(zz, yy, xx, mm):
        return ((zz * NY + yy) * NX + xx, mm)

    place = {"x": (NX, x), "y": (NY, y), "z": (NZ, z)}

    def turn(axis, by):
        n, i = place[axis]
        return lax.rem(i + (by % n), n)

    def along(axis, by):
        j = turn(axis, by)
        return {"x": device(z, y, j, m), "y": device(z, j, x, m), "z": device(j, y, x, m)}[axis]

    partner = device(z, y, x, 1 - m)
    copies, groups, sent = [], [], [0] * SENDS

    class Group:
        def __init__(self, ref):
            self.ref, self.sem, self.bytes, self.done = ref, recv_sem.at[len(groups)], 0, False
            groups.append(self)

        def send(self, src, dst, to):
            at = len(copies)
            size = math.prod(src.shape) * src.dtype.itemsize
            copy = pltpu.make_async_remote_copy(
                src_ref=src, dst_ref=dst, send_sem=send_sem.at[at % SENDS], recv_sem=self.sem,
                device_id=to, device_id_type=MESH)
            copy.start()
            copies.append(copy)
            self.bytes += size
            sent[at % SENDS] += size

        def wait(self):
            assert self.bytes == math.prod(self.ref.shape) * self.ref.dtype.itemsize
            self.done = True
            pltpu.make_async_remote_copy(
                src_ref=self.ref, dst_ref=self.ref, send_sem=send_sem.at[0], recv_sem=self.sem,
                device_id=partner, device_id_type=MESH).wait_recv()

    barrier = pltpu.get_barrier_semaphore()
    peers = [along(axis, o) for axis in "xyz" for o in range(1, place[axis][0])] + [partner]
    for peer in peers:
        pl.semaphore_signal(barrier, inc=1, device_id=peer, device_id_type=MESH)

    own_shard = pltpu.make_async_copy(shard, W.at[z, y, x], local_sem.at[0])
    own_shard.start()
    fetches = [pltpu.make_async_copy(src, dst, local_sem.at[at + 1]) for at, (src, dst) in enumerate((
        (routes_in, routes), (counts_in, counts), (widths_in, widths), (cot_in, cot), (tokens_in, tokens)))]
    for fetch in fetches:
        fetch.start()
    own_shard.wait()
    pl.semaphore_wait(barrier, len(peers))

    up, down = pl.ds(0, 16), pl.ds(16, 16)
    ca, cb = pl.ds(A0, A1 - A0), pl.ds(0, A0)
    every = pl.ds(0, 4)

    def span(half):
        return every if half is None else pl.ds(half * 2, 2)

    def ring(group, axis, k, region):
        halves = (0, 1) if k == place[axis][0] // 2 else (None, None)
        right, left = region(turn(axis, 1 - k), halves[0]), region(turn(axis, k - 1), halves[1])
        group.send(right, right, along(axis, 1))
        group.send(left, left, along(axis, -1))

    class Chunk:
        def __init__(self, q):
            self.q = q

        def near(self):
            q = self.q
            self.group = Group(W.at[pl.ds(0, 6), 0, 0, up, cb])
            upper, lower = W.at[q, y, x, up, cb], W.at[q, y, x, down, cb]
            for o in range(1, 4):
                self.group.send(upper, upper, along("y", o))
                self.group.send(lower, lower, along("x", o))

        def far(self, k):
            q = self.q
            self.group.wait()
            self.group = Group(W.at[pl.ds(0, 4 // k), every, 0, up, cb])
            ring(self.group, "x", k, lambda j, h: W.at[q, span(h), j, up, cb])
            ring(self.group, "y", k, lambda j, h: W.at[q, j, span(h), down, cb])

    chunks = [Chunk(turn("z", -o)) for o in range(NZ)]
    own_bc = W.at[z, y, x, :, cb]
    from_z = {}
    for o in (4, 3, 5, 2, 6, 1, 7):
        from_z[o] = Group(W.at[0, 0, 0, :, cb])
        from_z[o].send(own_bc, own_bc, along("z", o))
    chunks[0].near()
    own_a = W.at[z, y, x, :, ca]
    a_x = Group(W.at[pl.ds(0, 3), 0, 0, :, ca])
    for o in range(1, NX):
        a_x.send(own_a, own_a, along("x", o))

    def arrive(*offsets):
        for o in offsets:
            from_z[o].wait()
            chunks[o].near()

    def far(k, *offsets):
        for o in offsets:
            chunks[o].far(k)

    a_last = {}

    def a_far(k, oy):
        if k > 1:
            a_last[oy].wait()
        a_last[oy] = Group(W.at[0, 0, every, :, ca] if k == 4 else W.at[pl.ds(0, 2), 0, every, :, ca])
        row = turn("y", -oy)
        ring(a_last[oy], "z", k, lambda j, h: W.at[j, row, span(h), :, ca])

    for fetch in fetches:
        fetch.wait()
    named = jnp.broadcast_to(routes[...], (ROWS, ROWS))
    first_index = lax.broadcasted_iota(jnp.int32, (ROWS, ROWS), 0)
    second_index = lax.broadcasted_iota(jnp.int32, (ROWS, ROWS), 1)
    same = (named == named.astype(F32).T.astype(jnp.int32)) & (first_index < second_index)
    earlier = jnp.sum(same.astype(F32), axis=0, keepdims=True).astype(jnp.int32)
    slot = (routes[...] * 2 + earlier) * HEADS

    def prepare(s):
        tokT[s] = tokens[:, s * SLAB:(s + 1) * SLAB].T
        for h in range(HEADS):
            hot[s, :, h * ROWS:(h + 1) * ROWS] = (first_index + s * ROWS == slot + h).astype(F32).astype(BF16)

    started = []

    def forward(o):
        q = chunks[o].q
        columns = pl.ds(pl.multiple_of(q * SLAB, SLAB), SLAB)
        term = jnp.dot(tokens[:, columns], W[q].reshape(SLAB, COLS), preferred_element_type=F32)
        if not started:
            started.append(o)
            proj[...] = term
        else:
            proj[...] += term

    a_y = Group(W.at[pl.ds(0, 3), 0, every, :, ca])

    def a_row():
        a_x.wait()
        own = W.at[z, y, every, :, ca]
        for o in range(1, NY):
            a_y.send(own, own, along("y", o))

    position = lax.broadcasted_iota(jnp.int32, (ROWS, 1), 0)
    bound0 = counts[0, 0]
    bound1 = bound0 + counts[0, 1]
    bound2 = bound1 + counts[0, 2]
    row_width = jnp.where(position < bound0, widths[0], jnp.where(
        position < bound1, widths[1], jnp.where(position < bound2, widths[2], widths[3])))

    def norm_grads():
        for h in range(HEADS):
            cols = slice(h * HEAD_DIM, (h + 1) * HEAD_DIM)
            own = proj[:, cols]
            inverse = 1.0 / jnp.sqrt(jnp.mean(own * own, axis=1, keepdims=True) + EPSILON)
            outputs = own * inverse
            head_mask = (m * HEADS + h < row_width).astype(F32)
            upstream = cot[:, cols].astype(F32) * head_mask
            delta = (upstream - outputs * jnp.mean(upstream * outputs, axis=1, keepdims=True)) * inverse
            dl[:, cols] = delta.astype(BF16)
            D[h * ROWS:(h + 1) * ROWS] = delta.astype(BF16)

    def reduce(group, axis, lead, t, local, sbuf, rbuf):
        n, half = place[axis][0], lead // 2
        for d in range(2):
            by = n // 2 - t + 1
            j = turn(axis, by if d == 0 else -by)

            def put(lo, hi, arrived):
                value = local(j, lo, hi)
                if arrived:
                    value += rbuf[d, t - 2, lo:hi].astype(F32)
                sbuf[d, t - 1, lo:hi] = value.astype(BF16)

            first = d * half
            part = pl.ds(0, lead)
            if t == 1:
                put(first, first + half, False)
                part = pl.ds(first, half)
            elif t == 2:
                put(first, first + half, True)
                put(half - first, lead - first, False)
            else:
                put(0, half, True)
                put(half, lead, True)
            group.send(sbuf.at[d, t - 1, part], rbuf.at[d, t - 1, part], along(axis, 1 if d == 0 else -1))

    def ring_sum(axis, lead, local, rbuf):
        n, i = place[axis]
        s = n // 2 - 1
        return (local(i, 0, lead) + rbuf[0, s].astype(F32)) + rbuf[1, s].astype(F32)

    def a_local(k):
        row = turn("y", k)
        return lambda j, lo, hi: dW[j, row, lo:hi, :, A0:A1]

    a_group = {}

    def a_step(t, k):
        if t > 1:
            a_group[k].wait()
        a_group[k] = Group(aZr.at[k, 0, 0] if t == 1 else aZr.at[k, :, 0])
        reduce(a_group[k], "z", NX, t, a_local(k), aZs.at[k], aZr.at[k])

    class Unit:
        def __init__(self, at, o):
            self.at, self.o, self.q = at, o, turn("z", -o)
            q = self.q
            self.b_local = lambda j, lo, hi: dW[q, lo:hi, j, 0:16, 0:A0]
            self.c_local = lambda j, lo, hi: dW[q, j, lo:hi, 16:32, 0:A0]

        def term(self):
            part = jnp.dot(tokT[self.q], dl[...], preferred_element_type=F32)
            dW[self.q] = part.reshape(NY, NX, FEATS, COLS)

        def step(self, t):
            at = self.at
            if t > 1:
                self.group.wait()
            self.group = Group(bXr.at[at, :, 0] if t == 1 else bXr.at[at])
            reduce(self.group, "x", NY, t, self.b_local, bXs.at[at], bXr.at[at])
            reduce(self.group, "y", NX, t, self.c_local, cYs.at[at], cYr.at[at])

        def near(self):
            at = self.at
            self.group.wait()
            self.group = Group(W.at[pl.ds(0, 6), 0, 0, up, cb])
            total = ring_sum("x", NY, self.b_local, bXr.at[at])
            b1[at] = total
            bYs[at] = total.astype(BF16)
            for o in range(1, 4):
                self.group.send(bYs.at[at, turn("y", o)], bYr.at[at, o - 1], along("y", o))
            total = ring_sum("y", NX, self.c_local, cYr.at[at])
            c1[at] = total
            cXs[at] = total.astype(BF16)
            for o in range(1, 4):
                self.group.send(cXs.at[at, turn("x", o)], cXr.at[at, o - 1], along("x", o))

        def across(self):
            at = self.at
            self.group.wait()
            for mine, arrived, rows, i in ((b1, bYr, slice(0, 16), y), (c1, cXr, slice(16, 32), x)):
                total = mine[at, i]
                for k in range(3):
                    total += arrived[at, k].astype(F32)
                if self.o == 0:
                    Zf[rows] = total
                else:
                    Zs[at, rows] = total.astype(BF16)
            if self.o:
                to_z.send(Zs.at[at], Zr.at[self.o - 1], along("z", -self.o))

    to_z = Group(Zr)
    units = [Unit(at, o) for at, o in enumerate((4, 3, 5, 2, 6, 1, 7, 0))]

    r_z = Group(R1.at[pl.ds(0, 7)])
    r_xy = Group(W.at[pl.ds(0, 5), pl.ds(0, 3), pl.ds(0, 2), :, ca])
    all_z = pl.ds(0, NZ)

    def pack(o):
        j = turn("z", o)
        packed = jnp.dot(hot[j], D[...], preferred_element_type=F32)
        packed = packed.reshape(NY, NX, 8, HEAD_DIM).astype(BF16)
        if o:
            S[j] = packed
            r_z.send(S.at[j], R1.at[z], along("z", o))
        else:
            R1[z] = packed

    def route_plane():
        r_z.wait()
        for oy in range(NY):
            for ox in range(NX):
                jy, jx = turn("y", oy), turn("x", ox)
                if oy or ox:
                    r_xy.send(R1.at[all_z, jy, jx], R3.at[all_z, y, x], device(z, jy, jx, m))
        for s in range(NZ):
            R3[s, y, x] = R1[s, y, x]

    def unpack():
        r_xy.wait()
        Rf[...] = R3[...].astype(F32).reshape(8 * ROWS, HEAD_DIM)
        for h in range(HEADS):
            G[:, h * HEAD_DIM:(h + 1) * HEAD_DIM] = Rf[pl.ds(h, 2 * ROWS, stride=HEADS), :].astype(BF16)

    def product(tile):
        return lax.dot_general(G[...], W[tile].reshape(SLAB, COLS), (((1,), (1,)), ((), ())),
                               preferred_element_type=F32).astype(BF16)

    halves = []

    def give(t):
        DXs[t] = product((1 - m) * 4 + t)
        group = Group(DXr.at[t])
        group.send(DXs.at[t], DXr.at[t], partner)
        halves.append(group)

    def take(t):
        own = product(m * 4 + t).astype(F32)
        halves[t].wait()
        rows_out[:, t * SLAB:(t + 1) * SLAB] = (own + DXr[t].astype(F32)).astype(BF16)

    ra_y, ra_x = Group(aYr), Group(aXr)
    scale = 1.0 / 128.0

    def a_over_y(k):
        a_group[k].wait()
        total = ring_sum("z", NX, a_local(k), aZr.at[k])
        if k == 0:
            a1[...] = total
        else:
            aYs[k - 1] = total.astype(BF16)
            ra_y.send(aYs.at[k - 1], aYr.at[k - 1], along("y", k))

    def a_over_x():
        ra_y.wait()
        total = a1[...]
        for o in range(NY - 1):
            total += aYr[o].astype(F32)
        a2[...] = total
        aXs[...] = total.astype(BF16)
        for o in range(1, NX):
            ra_x.send(aXs.at[turn("x", o)], aXr.at[o - 1], along("x", o))

    def finish_bc():
        to_z.wait()
        total = Zf[...]
        for o in range(NZ - 1):
            total += Zr[o].astype(F32)
        grad_out[:, 0:A0] = total * scale

    def finish_a():
        ra_x.wait()
        total = a2[x]
        for o in range(NX - 1):
            total += aXr[o].astype(F32)
        grad_out[:, A0:A1] = total * scale

    prepare(2)
    a_row()
    chunks[0].far(1)
    a_far(1, 0)
    arrive(3)
    arrive(5)
    arrive(1)
    prepare(7)
    arrive(2)
    arrive(4)
    prepare(5)
    a_far(2, 0)
    arrive(7)
    arrive(6)
    a_y.wait()
    a_far(1, 3)
    chunks[0].far(2)
    a_far(1, 1)
    a_far(1, 2)
    chunks[3].far(1)
    a_far(3, 0)
    chunks[5].far(1)
    a_far(2, 3)
    chunks[2].far(1)
    chunks[4].far(1)
    a_far(2, 1)
    a_far(2, 2)
    chunks[1].far(1)
    chunks[6].far(1)
    chunks[7].far(1)
    prepare(6)
    prepare(0)
    a_far(3, 3)
    chunks[5].far(2)
    chunks[3].far(2)
    a_far(3, 1)
    prepare(4)
    chunks[0].group.wait()
    forward(0)
    a_far(3, 2)
    prepare(3)
    chunks[2].far(2)
    a_far(4, 0)
    prepare(1)
    chunks[1].far(2)
    chunks[4].far(2)
    chunks[6].far(2)
    a_far(4, 3)
    a_far(4, 1)
    chunks[7].far(2)
    a_far(4, 2)
    chunks[3].group.wait()
    forward(3)
    chunks[2].group.wait()
    forward(2)
    chunks[5].group.wait()
    forward(5)
    chunks[1].group.wait()
    forward(1)
    chunks[4].group.wait()
    chunks[6].group.wait()
    forward(6)
    a_last[0].wait()
    a_last[1].wait()
    a_last[2].wait()
    a_last[3].wait()
    forward(4)
    chunks[7].group.wait()
    forward(7)
    norm_grads()
    units[7].term()
    units[7].step(1)
    pack(4)
    units[0].term()
    units[0].step(1)
    units[6].term()
    units[6].step(1)
    units[4].term()
    units[4].step(1)
    a_step(1, 1)
    a_step(1, 3)
    units[1].term()
    units[1].step(1)
    units[5].term()
    a_step(1, 2)
    units[5].step(1)
    pack(5)
    pack(2)
    units[3].term()
    units[3].step(1)
    units[2].term()
    units[2].step(1)
    a_step(1, 0)
    pack(3)
    units[0].step(2)
    a_step(2, 1)
    units[6].step(2)
    pack(6)
    units[1].step(2)
    a_step(2, 2)
    units[3].step(2)
    a_step(2, 3)
    pack(1)
    units[5].step(2)
    units[2].step(2)
    pack(7)
    units[4].step(2)
    a_step(2, 0)
    pack(0)
    units[0].near()
    a_step(3, 1)
    a_step(3, 2)
    units[1].near()
    a_step(3, 3)
    route_plane()
    a_step(3, 0)
    units[6].near()
    a_step(4, 1)
    a_step(4, 2)
    units[3].near()
    a_step(4, 3)
    units[2].near()
    units[5].near()
    a_step(4, 0)
    units[4].near()
    units[7].step(2)
    units[0].across()
    a_over_y(2)
    units[1].across()
    a_over_y(1)
    a_over_y(3)
    units[6].across()
    unpack()
    units[2].across()
    give(0)
    give(1)
    units[5].across()
    give(2)
    units[3].across()
    units[4].across()
    units[7].near()
    a_over_y(0)
    give(3)
    a_over_x()
    take(0)
    take(1)
    take(2)
    units[7].across()
    finish_bc()
    take(3)
    finish_a()
    assert len(groups) == ARRIVALS
    for k in range(SENDS):
        assert sent[k] % 4096 == 0 and sent[k] <= METER * 4096
        all_of_them = meter.at[pl.ds(0, sent[k] // 4096)]
        pltpu.make_async_remote_copy(
            src_ref=all_of_them, dst_ref=all_of_them, send_sem=send_sem.at[k], recv_sem=recv_sem.at[0],
            device_id=partner, device_id_type=MESH).wait_send()


def per_device(tokens, key_cot, routes, counts, widths, key_weight):
    vmem = pl.BlockSpec(memory_space=pltpu.VMEM)
    anywhere = pl.BlockSpec(memory_space=pl.ANY)
    buffers = [
        ((METER, 8, 128), F32),
        ((ROWS, WIDTH), BF16),
        ((ROWS, COLS), BF16),
        ((1, ROWS), jnp.int32),
        ((NZ, NY, NX, FEATS, COLS), BF16),
        ((NZ, SLAB, ROWS), BF16),
        ((NZ, NY, NX, FEATS, COLS), F32),
        ((ROWS, COLS), F32),
        ((ROWS, COLS), BF16),
        ((HEADS * ROWS, HEAD_DIM), BF16),
        ((NZ, ROWS, HEADS * ROWS), BF16),
        ((NZ, NY, NX, 8, HEAD_DIM), BF16),
        ((NZ, NY, NX, 8, HEAD_DIM), BF16),
        ((NZ, NY, NX, 8, HEAD_DIM), BF16),
        ((8 * ROWS, HEAD_DIM), F32),
        ((2 * ROWS, COLS), BF16),
        ((4, 2 * ROWS, SLAB), BF16),
        ((4, 2 * ROWS, SLAB), BF16),
        ((NY, 2, 4, NX, FEATS, 128), BF16),
        ((NY, 2, 4, NX, FEATS, 128), BF16),
        ((NX, FEATS, 128), F32),
        ((NY - 1, NX, FEATS, 128), BF16),
        ((NY - 1, NX, FEATS, 128), BF16),
        ((NX, FEATS, 128), F32),
        ((NX, FEATS, 128), BF16),
        ((NX - 1, FEATS, 128), BF16),
        ((NZ, 2, 2, NY, 16, 384), BF16),
        ((NZ, 2, 2, NY, 16, 384), BF16),
        ((NZ, NY, 16, 384), F32),
        ((NZ, NY, 16, 384), BF16),
        ((NZ, NY - 1, 16, 384), BF16),
        ((NZ, 2, 2, NX, 16, 384), BF16),
        ((NZ, 2, 2, NX, 16, 384), BF16),
        ((NZ, NX, 16, 384), F32),
        ((NZ, NX, 16, 384), BF16),
        ((NZ, NX - 1, 16, 384), BF16),
        ((FEATS, 384), F32),
        ((NZ, FEATS, 384), BF16),
        ((NZ - 1, FEATS, 384), BF16),
    ]
    rows, grad = pl.pallas_call(
        kernel,
        out_shape=(pltpu.VMEM((2 * ROWS, WIDTH // 2), BF16), pltpu.VMEM((FEATS, COLS), F32)),
        in_specs=[anywhere] * 6,
        out_specs=(vmem, vmem),
        scratch_shapes=[pltpu.VMEM(shape, dtype) for shape, dtype in buffers[:4]]
        + [pltpu.SMEM((1, 4), jnp.int32), pltpu.SMEM((4,), jnp.int32)]
        + [pltpu.VMEM(shape, dtype) for shape, dtype in buffers[4:]]
        + [pltpu.SemaphoreType.DMA((6,)), pltpu.SemaphoreType.DMA((SENDS,)), pltpu.SemaphoreType.DMA((ARRIVALS,))],
        compiler_params=pltpu.CompilerParams(
            collective_id=0, has_side_effects=True, vmem_limit_bytes=58 << 20),
    )(tokens, key_cot, routes.reshape(1, ROWS), counts, widths, key_weight)
    return rows, grad


def solution(mesh):
    return jax.shard_map(
        per_device,
        mesh=mesh,
        in_specs=(P("dp", None), P("dp", "mp"), P("dp", None), P("dp", None), P(), P("dp", "mp")),
        out_specs=(P("dp", "mp"), P("dp", "mp")),
        check_vma=False,
    )
```

```python
import math

import jax
import jax.numpy as jnp
from jax import lax
from jax.experimental import pallas as pl
from jax.experimental.pallas import tpu as pltpu
from jax.sharding import PartitionSpec as P

HEAD_DIM = 128
EPSILON = 1e-06
MESH = pl.DeviceIdType.MESH
NZ, NY, NX = 8, 4, 4
ROWS, WIDTH, COLS, FEATS = 128, 4096, 512, 32
SLAB = WIDTH // NZ
HEADS = COLS // HEAD_DIM
A0, A1 = 384, 512
F32, BF16 = jnp.float32, jnp.bfloat16
SENDS, ARRIVALS, METER = 8, 98, 1024


def kernel(tokens_in, cot_in, routes_in, counts_in, widths_in, shard, rows_out, grad_out,
           meter, tokens, cot, routes, counts, widths, W, tokT, dW, proj, dl, D, hot, S, R1, R3, Rf, G, DXs, DXr,
           aZs, aZr, a1, aYs, aYr, a2, aXs, aXr,
           bXs, bXr, b1, bYs, bYr, cYs, cYr, c1, cXs, cXr, Zf, Zs, Zr,
           local_sem, send_sem, recv_sem):
    me, m = lax.axis_index("dp"), lax.axis_index("mp")
    x, y, z = lax.rem(me, NX), lax.rem(me // NX, NY), me // (NX * NY)

    def device(zz, yy, xx, mm):
        return ((zz * NY + yy) * NX + xx, mm)

    place = {"x": (NX, x), "y": (NY, y), "z": (NZ, z)}

    def turn(axis, by):
        n, i = place[axis]
        return lax.rem(i + (by % n), n)

    def along(axis, by):
        j = turn(axis, by)
        return {"x": device(z, y, j, m), "y": device(z, j, x, m), "z": device(j, y, x, m)}[axis]

    partner = device(z, y, x, 1 - m)
    copies, groups, sent = [], [], [0] * SENDS

    class Group:
        def __init__(self, ref):
            self.ref, self.sem, self.bytes, self.done = ref, recv_sem.at[len(groups)], 0, False
            groups.append(self)

        def send(self, src, dst, to):
            at = len(copies)
            size = math.prod(src.shape) * src.dtype.itemsize
            copy = pltpu.make_async_remote_copy(
                src_ref=src, dst_ref=dst, send_sem=send_sem.at[at % SENDS], recv_sem=self.sem,
                device_id=to, device_id_type=MESH)
            copy.start()
            copies.append(copy)
            self.bytes += size
            sent[at % SENDS] += size

        def wait(self):
            assert self.bytes == math.prod(self.ref.shape) * self.ref.dtype.itemsize
            self.done = True
            pltpu.make_async_remote_copy(
                src_ref=self.ref, dst_ref=self.ref, send_sem=send_sem.at[0], recv_sem=self.sem,
                device_id=partner, device_id_type=MESH).wait_recv()

    barrier = pltpu.get_barrier_semaphore()
    peers = [along(axis, o) for axis in "xyz" for o in range(1, place[axis][0])] + [partner]
    for peer in peers:
        pl.semaphore_signal(barrier, inc=1, device_id=peer, device_id_type=MESH)

    own_shard = pltpu.make_async_copy(shard, W.at[z, y, x], local_sem.at[0])
    own_shard.start()
    fetches = [pltpu.make_async_copy(src, dst, local_sem.at[at + 1]) for at, (src, dst) in enumerate((
        (routes_in, routes), (counts_in, counts), (widths_in, widths), (cot_in, cot), (tokens_in, tokens)))]
    for fetch in fetches:
        fetch.start()
    own_shard.wait()
    pl.semaphore_wait(barrier, len(peers))

    up, down = pl.ds(0, 16), pl.ds(16, 16)
    ca, cb = pl.ds(A0, A1 - A0), pl.ds(0, A0)
    every = pl.ds(0, 4)

    def span(half):
        return every if half is None else pl.ds(half * 2, 2)

    def ring(group, axis, k, region):
        halves = (0, 1) if k == place[axis][0] // 2 else (None, None)
        right, left = region(turn(axis, 1 - k), halves[0]), region(turn(axis, k - 1), halves[1])
        group.send(right, right, along(axis, 1))
        group.send(left, left, along(axis, -1))

    class Chunk:
        def __init__(self, q):
            self.q = q

        def near(self):
            q = self.q
            self.group = Group(W.at[pl.ds(0, 6), 0, 0, up, cb])
            upper, lower = W.at[q, y, x, up, cb], W.at[q, y, x, down, cb]
            for o in range(1, 4):
                self.group.send(upper, upper, along("y", o))
                self.group.send(lower, lower, along("x", o))

        def far(self, k):
            q = self.q
            self.group.wait()
            self.group = Group(W.at[pl.ds(0, 4 // k), every, 0, up, cb])
            ring(self.group, "x", k, lambda j, h: W.at[q, span(h), j, up, cb])
            ring(self.group, "y", k, lambda j, h: W.at[q, j, span(h), down, cb])

    chunks = [Chunk(turn("z", -o)) for o in range(NZ)]
    own_bc = W.at[z, y, x, :, cb]
    from_z = {}
    for o in (4, 3, 5, 2, 6, 1, 7):
        from_z[o] = Group(W.at[0, 0, 0, :, cb])
        from_z[o].send(own_bc, own_bc, along("z", o))
    chunks[0].near()
    own_a = W.at[z, y, x, :, ca]
    a_x = Group(W.at[pl.ds(0, 3), 0, 0, :, ca])
    for o in range(1, NX):
        a_x.send(own_a, own_a, along("x", o))

    def arrive(*offsets):
        for o in offsets:
            from_z[o].wait()
            chunks[o].near()

    def far(k, *offsets):
        for o in offsets:
            chunks[o].far(k)

    a_last = {}

    def a_far(k, oy):
        if k > 1:
            a_last[oy].wait()
        a_last[oy] = Group(W.at[0, 0, every, :, ca] if k == 4 else W.at[pl.ds(0, 2), 0, every, :, ca])
        row = turn("y", -oy)
        ring(a_last[oy], "z", k, lambda j, h: W.at[j, row, span(h), :, ca])

    for fetch in fetches:
        fetch.wait()
    named = jnp.broadcast_to(routes[...], (ROWS, ROWS))
    first_index = lax.broadcasted_iota(jnp.int32, (ROWS, ROWS), 0)
    second_index = lax.broadcasted_iota(jnp.int32, (ROWS, ROWS), 1)
    same = (named == named.astype(F32).T.astype(jnp.int32)) & (first_index < second_index)
    earlier = jnp.sum(same.astype(F32), axis=0, keepdims=True).astype(jnp.int32)
    slot = (routes[...] * 2 + earlier) * HEADS

    def prepare(s):
        tokT[s] = tokens[:, s * SLAB:(s + 1) * SLAB].T
        for h in range(HEADS):
            hot[s, :, h * ROWS:(h + 1) * ROWS] = (first_index + s * ROWS == slot + h).astype(F32).astype(BF16)

    started = []

    def forward(o):
        q = chunks[o].q
        columns = pl.ds(pl.multiple_of(q * SLAB, SLAB), SLAB)
        term = jnp.dot(tokens[:, columns], W[q].reshape(SLAB, COLS), preferred_element_type=F32)
        if not started:
            started.append(o)
            proj[...] = term
        else:
            proj[...] += term

    a_y = Group(W.at[pl.ds(0, 3), 0, every, :, ca])

    def a_row():
        a_x.wait()
        own = W.at[z, y, every, :, ca]
        for o in range(1, NY):
            a_y.send(own, own, along("y", o))

    position = lax.broadcasted_iota(jnp.int32, (ROWS, 1), 0)
    bound0 = counts[0, 0]
    bound1 = bound0 + counts[0, 1]
    bound2 = bound1 + counts[0, 2]
    row_width = jnp.where(position < bound0, widths[0], jnp.where(
        position < bound1, widths[1], jnp.where(position < bound2, widths[2], widths[3])))

    def norm_grads():
        for h in range(HEADS):
            cols = slice(h * HEAD_DIM, (h + 1) * HEAD_DIM)
            own = proj[:, cols]
            inverse = 1.0 / jnp.sqrt(jnp.mean(own * own, axis=1, keepdims=True) + EPSILON)
            outputs = own * inverse
            head_mask = (m * HEADS + h < row_width).astype(F32)
            upstream = cot[:, cols].astype(F32) * head_mask
            delta = (upstream - outputs * jnp.mean(upstream * outputs, axis=1, keepdims=True)) * inverse
            dl[:, cols] = delta.astype(BF16)
            D[h * ROWS:(h + 1) * ROWS] = delta.astype(BF16)

    def reduce(group, axis, lead, t, local, sbuf, rbuf):
        n, half = place[axis][0], lead // 2
        for d in range(2):
            by = n // 2 - t + 1
            j = turn(axis, by if d == 0 else -by)

            def put(lo, hi, arrived):
                value = local(j, lo, hi)
                if arrived:
                    value += rbuf[d, t - 2, lo:hi].astype(F32)
                sbuf[d, t - 1, lo:hi] = value.astype(BF16)

            first = d * half
            part = pl.ds(0, lead)
            if t == 1:
                put(first, first + half, False)
                part = pl.ds(first, half)
            elif t == 2:
                put(first, first + half, True)
                put(half - first, lead - first, False)
            else:
                put(0, half, True)
                put(half, lead, True)
            group.send(sbuf.at[d, t - 1, part], rbuf.at[d, t - 1, part], along(axis, 1 if d == 0 else -1))

    def ring_sum(axis, lead, local, rbuf):
        n, i = place[axis]
        s = n // 2 - 1
        return (local(i, 0, lead) + rbuf[0, s].astype(F32)) + rbuf[1, s].astype(F32)

    def a_local(k):
        row = turn("y", k)
        return lambda j, lo, hi: dW[j, row, lo:hi, :, A0:A1]

    a_group = {}

    def a_step(t, k):
        if t > 1:
            a_group[k].wait()
        a_group[k] = Group(aZr.at[k, 0, 0] if t == 1 else aZr.at[k, :, 0])
        reduce(a_group[k], "z", NX, t, a_local(k), aZs.at[k], aZr.at[k])

    class Unit:
        def __init__(self, at, o):
            self.at, self.o, self.q = at, o, turn("z", -o)
            q = self.q
            self.b_local = lambda j, lo, hi: dW[q, lo:hi, j, 0:16, 0:A0]
            self.c_local = lambda j, lo, hi: dW[q, j, lo:hi, 16:32, 0:A0]

        def term(self):
            part = jnp.dot(tokT[self.q], dl[...], preferred_element_type=F32)
            dW[self.q] = part.reshape(NY, NX, FEATS, COLS)

        def step(self, t):
            at = self.at
            if t > 1:
                self.group.wait()
            self.group = Group(bXr.at[at, :, 0] if t == 1 else bXr.at[at])
            reduce(self.group, "x", NY, t, self.b_local, bXs.at[at], bXr.at[at])
            reduce(self.group, "y", NX, t, self.c_local, cYs.at[at], cYr.at[at])

        def near(self):
            at = self.at
            self.group.wait()
            self.group = Group(W.at[pl.ds(0, 6), 0, 0, up, cb])
            total = ring_sum("x", NY, self.b_local, bXr.at[at])
            b1[at] = total
            bYs[at] = total.astype(BF16)
            for o in range(1, 4):
                self.group.send(bYs.at[at, turn("y", o)], bYr.at[at, o - 1], along("y", o))
            total = ring_sum("y", NX, self.c_local, cYr.at[at])
            c1[at] = total
            cXs[at] = total.astype(BF16)
            for o in range(1, 4):
                self.group.send(cXs.at[at, turn("x", o)], cXr.at[at, o - 1], along("x", o))

        def across(self):
            at = self.at
            self.group.wait()
            for mine, arrived, rows, i in ((b1, bYr, slice(0, 16), y), (c1, cXr, slice(16, 32), x)):
                total = mine[at, i]
                for k in range(3):
                    total += arrived[at, k].astype(F32)
                if self.o == 0:
                    Zf[rows] = total
                else:
                    Zs[at, rows] = total.astype(BF16)
            if self.o:
                to_z.send(Zs.at[at], Zr.at[self.o - 1], along("z", -self.o))

    to_z = Group(Zr)
    units = [Unit(at, o) for at, o in enumerate((4, 3, 5, 2, 6, 1, 7, 0))]

    r_z = Group(R1.at[pl.ds(0, 7)])
    r_xy = Group(W.at[pl.ds(0, 5), pl.ds(0, 3), pl.ds(0, 2), :, ca])
    all_z = pl.ds(0, NZ)

    def pack(o):
        j = turn("z", o)
        packed = jnp.dot(hot[j], D[...], preferred_element_type=F32)
        packed = packed.reshape(NY, NX, 8, HEAD_DIM).astype(BF16)
        if o:
            S[j] = packed
            r_z.send(S.at[j], R1.at[z], along("z", o))
        else:
            R1[z] = packed

    def route_plane():
        r_z.wait()
        for oy in range(NY):
            for ox in range(NX):
                jy, jx = turn("y", oy), turn("x", ox)
                if oy or ox:
                    r_xy.send(R1.at[all_z, jy, jx], R3.at[all_z, y, x], device(z, jy, jx, m))
        for s in range(NZ):
            R3[s, y, x] = R1[s, y, x]

    def unpack():
        r_xy.wait()
        Rf[...] = R3[...].astype(F32).reshape(8 * ROWS, HEAD_DIM)
        for h in range(HEADS):
            G[:, h * HEAD_DIM:(h + 1) * HEAD_DIM] = Rf[pl.ds(h, 2 * ROWS, stride=HEADS), :].astype(BF16)

    def product(tile):
        return lax.dot_general(G[...], W[tile].reshape(SLAB, COLS), (((1,), (1,)), ((), ())),
                               preferred_element_type=F32).astype(BF16)

    halves = []

    def give(t):
        DXs[t] = product((1 - m) * 4 + t)
        group = Group(DXr.at[t])
        group.send(DXs.at[t], DXr.at[t], partner)
        halves.append(group)

    def take(t):
        own = product(m * 4 + t).astype(F32)
        halves[t].wait()
        rows_out[:, t * SLAB:(t + 1) * SLAB] = (own + DXr[t].astype(F32)).astype(BF16)

    ra_y, ra_x = Group(aYr), Group(aXr)
    scale = 1.0 / 128.0

    def a_over_y(k):
        a_group[k].wait()
        total = ring_sum("z", NX, a_local(k), aZr.at[k])
        if k == 0:
            a1[...] = total
        else:
            aYs[k - 1] = total.astype(BF16)
            ra_y.send(aYs.at[k - 1], aYr.at[k - 1], along("y", k))

    def a_over_x():
        ra_y.wait()
        total = a1[...]
        for o in range(NY - 1):
            total += aYr[o].astype(F32)
        a2[...] = total
        aXs[...] = total.astype(BF16)
        for o in range(1, NX):
            ra_x.send(aXs.at[turn("x", o)], aXr.at[o - 1], along("x", o))

    def finish_bc():
        to_z.wait()
        total = Zf[...]
        for o in range(NZ - 1):
            total += Zr[o].astype(F32)
        grad_out[:, 0:A0] = total * scale

    def finish_a():
        ra_x.wait()
        total = a2[x]
        for o in range(NX - 1):
            total += aXr[o].astype(F32)
        grad_out[:, A0:A1] = total * scale

    prepare(2)
    a_row()
    chunks[0].far(1)
    a_far(1, 0)
    arrive(3)
    arrive(5)
    arrive(1)
    prepare(7)
    arrive(2)
    arrive(4)
    prepare(5)
    a_far(2, 0)
    arrive(7)
    arrive(6)
    a_y.wait()
    a_far(1, 3)
    chunks[0].far(2)
    a_far(1, 1)
    a_far(1, 2)
    chunks[3].far(1)
    a_far(3, 0)
    chunks[5].far(1)
    a_far(2, 3)
    chunks[2].far(1)
    chunks[4].far(1)
    a_far(2, 1)
    a_far(2, 2)
    chunks[1].far(1)
    chunks[6].far(1)
    chunks[7].far(1)
    prepare(6)
    prepare(0)
    a_far(3, 3)
    chunks[5].far(2)
    chunks[3].far(2)
    a_far(3, 1)
    prepare(4)
    chunks[0].group.wait()
    forward(0)
    a_far(3, 2)
    prepare(3)
    chunks[2].far(2)
    a_far(4, 0)
    prepare(1)
    chunks[1].far(2)
    chunks[4].far(2)
    chunks[6].far(2)
    a_far(4, 3)
    a_far(4, 1)
    chunks[7].far(2)
    a_far(4, 2)
    chunks[3].group.wait()
    forward(3)
    chunks[2].group.wait()
    forward(2)
    chunks[5].group.wait()
    forward(5)
    chunks[1].group.wait()
    forward(1)
    chunks[4].group.wait()
    chunks[6].group.wait()
    forward(6)
    a_last[0].wait()
    a_last[1].wait()
    a_last[2].wait()
    a_last[3].wait()
    forward(4)
    chunks[7].group.wait()
    forward(7)
    norm_grads()
    units[7].term()
    units[7].step(1)
    pack(4)
    units[0].term()
    units[0].step(1)
    units[6].term()
    units[6].step(1)
    units[4].term()
    units[4].step(1)
    a_step(1, 1)
    a_step(1, 3)
    units[1].term()
    units[1].step(1)
    units[5].term()
    a_step(1, 2)
    units[5].step(1)
    pack(5)
    pack(2)
    units[3].term()
    units[3].step(1)
    units[2].term()
    units[2].step(1)
    a_step(1, 0)
    pack(3)
    units[0].step(2)
    a_step(2, 1)
    units[6].step(2)
    pack(6)
    units[1].step(2)
    a_step(2, 2)
    units[3].step(2)
    a_step(2, 3)
    pack(1)
    units[5].step(2)
    units[2].step(2)
    pack(7)
    units[4].step(2)
    a_step(2, 0)
    pack(0)
    units[0].near()
    a_step(3, 1)
    a_step(3, 2)
    units[1].near()
    a_step(3, 3)
    route_plane()
    a_step(3, 0)
    units[6].near()
    a_step(4, 1)
    a_step(4, 2)
    units[3].near()
    a_step(4, 3)
    units[2].near()
    units[5].near()
    a_step(4, 0)
    units[4].near()
    units[7].step(2)
    units[0].across()
    a_over_y(2)
    units[1].across()
    a_over_y(1)
    a_over_y(3)
    units[6].across()
    unpack()
    units[2].across()
    give(0)
    give(1)
    units[5].across()
    give(2)
    units[3].across()
    units[4].across()
    units[7].near()
    a_over_y(0)
    give(3)
    a_over_x()
    take(0)
    take(1)
    take(2)
    units[7].across()
    finish_bc()
    take(3)
    finish_a()
    assert len(groups) == ARRIVALS
    for k in range(SENDS):
        assert sent[k] % 4096 == 0 and sent[k] <= METER * 4096
        all_of_them = meter.at[pl.ds(0, sent[k] // 4096)]
        pltpu.make_async_remote_copy(
            src_ref=all_of_them, dst_ref=all_of_them, send_sem=send_sem.at[k], recv_sem=recv_sem.at[0],
            device_id=partner, device_id_type=MESH).wait_send()


PIECES = 4


def hand_on(rows, grad, rows_out, grad_out, sem):
    copies = [pltpu.make_async_copy(grad, grad_out, sem.at[PIECES])]
    size = rows.shape[0] // PIECES
    for i in range(PIECES):
        part = pl.ds(i * size, size)
        copies.append(pltpu.make_async_copy(rows.at[part], rows_out.at[part], sem.at[i]))
    for copy in copies:
        copy.start()
    for copy in copies:
        copy.wait()


def per_device(tokens, key_cot, routes, counts, widths, key_weight):
    vmem = pl.BlockSpec(memory_space=pltpu.VMEM)
    anywhere = pl.BlockSpec(memory_space=pl.ANY)
    buffers = [
        ((METER, 8, 128), F32),
        ((ROWS, WIDTH), BF16),
        ((ROWS, COLS), BF16),
        ((1, ROWS), jnp.int32),
        ((NZ, NY, NX, FEATS, COLS), BF16),
        ((NZ, SLAB, ROWS), BF16),
        ((NZ, NY, NX, FEATS, COLS), F32),
        ((ROWS, COLS), F32),
        ((ROWS, COLS), BF16),
        ((HEADS * ROWS, HEAD_DIM), BF16),
        ((NZ, ROWS, HEADS * ROWS), BF16),
        ((NZ, NY, NX, 8, HEAD_DIM), BF16),
        ((NZ, NY, NX, 8, HEAD_DIM), BF16),
        ((NZ, NY, NX, 8, HEAD_DIM), BF16),
        ((8 * ROWS, HEAD_DIM), F32),
        ((2 * ROWS, COLS), BF16),
        ((4, 2 * ROWS, SLAB), BF16),
        ((4, 2 * ROWS, SLAB), BF16),
        ((NY, 2, 4, NX, FEATS, 128), BF16),
        ((NY, 2, 4, NX, FEATS, 128), BF16),
        ((NX, FEATS, 128), F32),
        ((NY - 1, NX, FEATS, 128), BF16),
        ((NY - 1, NX, FEATS, 128), BF16),
        ((NX, FEATS, 128), F32),
        ((NX, FEATS, 128), BF16),
        ((NX - 1, FEATS, 128), BF16),
        ((NZ, 2, 2, NY, 16, 384), BF16),
        ((NZ, 2, 2, NY, 16, 384), BF16),
        ((NZ, NY, 16, 384), F32),
        ((NZ, NY, 16, 384), BF16),
        ((NZ, NY - 1, 16, 384), BF16),
        ((NZ, 2, 2, NX, 16, 384), BF16),
        ((NZ, 2, 2, NX, 16, 384), BF16),
        ((NZ, NX, 16, 384), F32),
        ((NZ, NX, 16, 384), BF16),
        ((NZ, NX - 1, 16, 384), BF16),
        ((FEATS, 384), F32),
        ((NZ, FEATS, 384), BF16),
        ((NZ - 1, FEATS, 384), BF16),
    ]
    rows, grad = pl.pallas_call(
        kernel,
        out_shape=(pltpu.VMEM((2 * ROWS, WIDTH // 2), BF16), pltpu.VMEM((FEATS, COLS), F32)),
        in_specs=[anywhere] * 6,
        out_specs=(vmem, vmem),
        scratch_shapes=[pltpu.VMEM(shape, dtype) for shape, dtype in buffers[:4]]
        + [pltpu.SMEM((1, 4), jnp.int32), pltpu.SMEM((4,), jnp.int32)]
        + [pltpu.VMEM(shape, dtype) for shape, dtype in buffers[4:]]
        + [pltpu.SemaphoreType.DMA((6,)), pltpu.SemaphoreType.DMA((SENDS,)), pltpu.SemaphoreType.DMA((ARRIVALS,))],
        compiler_params=pltpu.CompilerParams(
            collective_id=0, has_side_effects=True, vmem_limit_bytes=58 << 20),
    )(tokens, key_cot, routes.reshape(1, ROWS), counts, widths, key_weight)
    return pl.pallas_call(
        hand_on,
        out_shape=(jax.ShapeDtypeStruct(rows.shape, BF16), jax.ShapeDtypeStruct(grad.shape, F32)),
        in_specs=[vmem, vmem],
        out_specs=(anywhere, anywhere),
        scratch_shapes=[pltpu.SemaphoreType.DMA((PIECES + 1,))],
    )(*(pltpu.with_memory_space_constraint(held, pltpu.VMEM) for held in (rows, grad)))


def solution(mesh):
    return jax.shard_map(
        per_device,
        mesh=mesh,
        in_specs=(P("dp", None), P("dp", "mp"), P("dp", None), P("dp", None), P(), P("dp", "mp")),
        out_specs=(P("dp", "mp"), P("dp", "mp")),
        check_vma=False,
    )
```

```python
import math

import jax
import jax.numpy as jnp
from jax import lax
from jax.experimental import pallas as pl
from jax.experimental.pallas import tpu as pltpu
from jax.sharding import PartitionSpec as P

HEAD_DIM = 128
EPSILON = 1e-06
MESH = pl.DeviceIdType.MESH
NZ, NY, NX = 8, 4, 4
ROWS, WIDTH, COLS, FEATS = 128, 4096, 512, 32
SLAB = WIDTH // NZ
HEADS = COLS // HEAD_DIM
A0, A1 = 384, 512
F32, BF16 = jnp.float32, jnp.bfloat16
SENDS, ARRIVALS, METER = 8, 98, 1024


def kernel(tokens_in, cot_in, routes_in, counts_in, widths_in, shard, rows_out, grad_out,
           meter, tokens, cot, routes, counts, widths, W, tokT, dW, proj, dl, D, hot, S, R1, R3, Rf, G, DXs, DXr,
           aZs, aZr, a1, aYs, aYr, a2, aXs, aXr,
           bXs, bXr, b1, bYs, bYr, cYs, cYr, c1, cXs, cXr, Zf, Zs, Zr,
           local_sem, send_sem, recv_sem):
    me, m = lax.axis_index("dp"), lax.axis_index("mp")
    x, y, z = lax.rem(me, NX), lax.rem(me // NX, NY), me // (NX * NY)

    def device(zz, yy, xx, mm):
        return ((zz * NY + yy) * NX + xx, mm)

    place = {"x": (NX, x), "y": (NY, y), "z": (NZ, z)}

    def turn(axis, by):
        n, i = place[axis]
        return lax.rem(i + (by % n), n)

    def along(axis, by):
        j = turn(axis, by)
        return {"x": device(z, y, j, m), "y": device(z, j, x, m), "z": device(j, y, x, m)}[axis]

    partner = device(z, y, x, 1 - m)
    copies, groups, sent = [], [], [0] * SENDS

    class Group:
        def __init__(self, ref):
            self.ref, self.sem, self.bytes, self.done = ref, recv_sem.at[len(groups)], 0, False
            groups.append(self)

        def send(self, src, dst, to):
            at = len(copies)
            size = math.prod(src.shape) * src.dtype.itemsize
            copy = pltpu.make_async_remote_copy(
                src_ref=src, dst_ref=dst, send_sem=send_sem.at[at % SENDS], recv_sem=self.sem,
                device_id=to, device_id_type=MESH)
            copy.start()
            copies.append(copy)
            self.bytes += size
            sent[at % SENDS] += size

        def wait(self):
            assert self.bytes == math.prod(self.ref.shape) * self.ref.dtype.itemsize
            self.done = True
            pltpu.make_async_remote_copy(
                src_ref=self.ref, dst_ref=self.ref, send_sem=send_sem.at[0], recv_sem=self.sem,
                device_id=partner, device_id_type=MESH).wait_recv()

    barrier = pltpu.get_barrier_semaphore()
    peers = [along(axis, o) for axis in "xyz" for o in range(1, place[axis][0])] + [partner]
    for peer in peers:
        pl.semaphore_signal(barrier, inc=1, device_id=peer, device_id_type=MESH)

    own_shard = pltpu.make_async_copy(shard, W.at[z, y, x], local_sem.at[0])
    own_shard.start()
    fetches = [pltpu.make_async_copy(src, dst, local_sem.at[at + 1]) for at, (src, dst) in enumerate((
        (routes_in, routes), (counts_in, counts), (widths_in, widths), (cot_in, cot), (tokens_in, tokens)))]
    for fetch in fetches:
        fetch.start()
    own_shard.wait()
    pl.semaphore_wait(barrier, len(peers))

    up, down = pl.ds(0, 16), pl.ds(16, 16)
    ca, cb = pl.ds(A0, A1 - A0), pl.ds(0, A0)
    every = pl.ds(0, 4)

    def span(half):
        return every if half is None else pl.ds(half * 2, 2)

    def ring(group, axis, k, region):
        halves = (0, 1) if k == place[axis][0] // 2 else (None, None)
        right, left = region(turn(axis, 1 - k), halves[0]), region(turn(axis, k - 1), halves[1])
        group.send(right, right, along(axis, 1))
        group.send(left, left, along(axis, -1))

    class Chunk:
        def __init__(self, q):
            self.q = q

        def near(self):
            q = self.q
            self.group = Group(W.at[pl.ds(0, 6), 0, 0, up, cb])
            upper, lower = W.at[q, y, x, up, cb], W.at[q, y, x, down, cb]
            for o in range(1, 4):
                self.group.send(upper, upper, along("y", o))
                self.group.send(lower, lower, along("x", o))

        def far(self, k):
            q = self.q
            self.group.wait()
            self.group = Group(W.at[pl.ds(0, 4 // k), every, 0, up, cb])
            ring(self.group, "x", k, lambda j, h: W.at[q, span(h), j, up, cb])
            ring(self.group, "y", k, lambda j, h: W.at[q, j, span(h), down, cb])

    chunks = [Chunk(turn("z", -o)) for o in range(NZ)]
    own_bc = W.at[z, y, x, :, cb]
    from_z = {}
    for o in (4, 3, 5, 2, 6, 1, 7):
        from_z[o] = Group(W.at[0, 0, 0, :, cb])
        from_z[o].send(own_bc, own_bc, along("z", o))
    chunks[0].near()
    own_a = W.at[z, y, x, :, ca]
    a_x = Group(W.at[pl.ds(0, 3), 0, 0, :, ca])
    for o in range(1, NX):
        a_x.send(own_a, own_a, along("x", o))

    def arrive(*offsets):
        for o in offsets:
            from_z[o].wait()
            chunks[o].near()

    def far(k, *offsets):
        for o in offsets:
            chunks[o].far(k)

    a_last = {}

    def a_far(k, oy):
        if k > 1:
            a_last[oy].wait()
        a_last[oy] = Group(W.at[0, 0, every, :, ca] if k == 4 else W.at[pl.ds(0, 2), 0, every, :, ca])
        row = turn("y", -oy)
        ring(a_last[oy], "z", k, lambda j, h: W.at[j, row, span(h), :, ca])

    for fetch in fetches:
        fetch.wait()
    named = jnp.broadcast_to(routes[...], (ROWS, ROWS))
    first_index = lax.broadcasted_iota(jnp.int32, (ROWS, ROWS), 0)
    second_index = lax.broadcasted_iota(jnp.int32, (ROWS, ROWS), 1)
    same = (named == named.astype(F32).T.astype(jnp.int32)) & (first_index < second_index)
    earlier = jnp.sum(same.astype(F32), axis=0, keepdims=True).astype(jnp.int32)
    slot = (routes[...] * 2 + earlier) * HEADS

    def prepare(s):
        tokT[s] = tokens[:, s * SLAB:(s + 1) * SLAB].T
        for h in range(HEADS):
            hot[s, :, h * ROWS:(h + 1) * ROWS] = (first_index + s * ROWS == slot + h).astype(F32).astype(BF16)

    started = []

    def forward(o):
        q = chunks[o].q
        columns = pl.ds(pl.multiple_of(q * SLAB, SLAB), SLAB)
        term = jnp.dot(tokens[:, columns], W[q].reshape(SLAB, COLS), preferred_element_type=F32)
        if not started:
            started.append(o)
            proj[...] = term
        else:
            proj[...] += term

    a_y = Group(W.at[pl.ds(0, 3), 0, every, :, ca])

    def a_row():
        a_x.wait()
        own = W.at[z, y, every, :, ca]
        for o in range(1, NY):
            a_y.send(own, own, along("y", o))

    position = lax.broadcasted_iota(jnp.int32, (ROWS, 1), 0)
    bound0 = counts[0, 0]
    bound1 = bound0 + counts[0, 1]
    bound2 = bound1 + counts[0, 2]
    row_width = jnp.where(position < bound0, widths[0], jnp.where(
        position < bound1, widths[1], jnp.where(position < bound2, widths[2], widths[3])))

    def norm_grads():
        for h in range(HEADS):
            cols = slice(h * HEAD_DIM, (h + 1) * HEAD_DIM)
            own = proj[:, cols]
            inverse = 1.0 / jnp.sqrt(jnp.mean(own * own, axis=1, keepdims=True) + EPSILON)
            outputs = own * inverse
            head_mask = (m * HEADS + h < row_width).astype(F32)
            upstream = cot[:, cols].astype(F32) * head_mask
            delta = (upstream - outputs * jnp.mean(upstream * outputs, axis=1, keepdims=True)) * inverse
            dl[:, cols] = delta.astype(BF16)
            D[h * ROWS:(h + 1) * ROWS] = delta.astype(BF16)

    def reduce(group, axis, lead, t, local, sbuf, rbuf):
        n, half = place[axis][0], lead // 2
        for d in range(2):
            by = n // 2 - t + 1
            j = turn(axis, by if d == 0 else -by)

            def put(lo, hi, arrived):
                value = local(j, lo, hi)
                if arrived:
                    value += rbuf[d, t - 2, lo:hi].astype(F32)
                sbuf[d, t - 1, lo:hi] = value.astype(BF16)

            first = d * half
            part = pl.ds(0, lead)
            if t == 1:
                put(first, first + half, False)
                part = pl.ds(first, half)
            elif t == 2:
                put(first, first + half, True)
                put(half - first, lead - first, False)
            else:
                put(0, half, True)
                put(half, lead, True)
            group.send(sbuf.at[d, t - 1, part], rbuf.at[d, t - 1, part], along(axis, 1 if d == 0 else -1))

    def ring_sum(axis, lead, local, rbuf):
        n, i = place[axis]
        s = n // 2 - 1
        return (local(i, 0, lead) + rbuf[0, s].astype(F32)) + rbuf[1, s].astype(F32)

    def a_local(k):
        row = turn("y", k)
        return lambda j, lo, hi: dW[j, row, lo:hi, :, A0:A1]

    a_group = {}

    def a_step(t, k):
        if t > 1:
            a_group[k].wait()
        a_group[k] = Group(aZr.at[k, 0, 0] if t == 1 else aZr.at[k, :, 0])
        reduce(a_group[k], "z", NX, t, a_local(k), aZs.at[k], aZr.at[k])

    class Unit:
        def __init__(self, at, o):
            self.at, self.o, self.q = at, o, turn("z", -o)
            q = self.q
            self.b_local = lambda j, lo, hi: dW[q, lo:hi, j, 0:16, 0:A0]
            self.c_local = lambda j, lo, hi: dW[q, j, lo:hi, 16:32, 0:A0]

        def term(self):
            part = jnp.dot(tokT[self.q], dl[...], preferred_element_type=F32)
            dW[self.q] = part.reshape(NY, NX, FEATS, COLS)

        def step(self, t):
            at = self.at
            if t > 1:
                self.group.wait()
            self.group = Group(bXr.at[at, :, 0] if t == 1 else bXr.at[at])
            reduce(self.group, "x", NY, t, self.b_local, bXs.at[at], bXr.at[at])
            reduce(self.group, "y", NX, t, self.c_local, cYs.at[at], cYr.at[at])

        def near(self):
            at = self.at
            self.group.wait()
            self.group = Group(W.at[pl.ds(0, 6), 0, 0, up, cb])
            total = ring_sum("x", NY, self.b_local, bXr.at[at])
            b1[at] = total
            bYs[at] = total.astype(BF16)
            for o in range(1, 4):
                self.group.send(bYs.at[at, turn("y", o)], bYr.at[at, o - 1], along("y", o))
            total = ring_sum("y", NX, self.c_local, cYr.at[at])
            c1[at] = total
            cXs[at] = total.astype(BF16)
            for o in range(1, 4):
                self.group.send(cXs.at[at, turn("x", o)], cXr.at[at, o - 1], along("x", o))

        def across(self):
            at = self.at
            self.group.wait()
            for mine, arrived, rows, i in ((b1, bYr, slice(0, 16), y), (c1, cXr, slice(16, 32), x)):
                total = mine[at, i]
                for k in range(3):
                    total += arrived[at, k].astype(F32)
                if self.o == 0:
                    Zf[rows] = total
                else:
                    Zs[at, rows] = total.astype(BF16)
            if self.o:
                to_z.send(Zs.at[at], Zr.at[self.o - 1], along("z", -self.o))

    to_z = Group(Zr)
    units = [Unit(at, o) for at, o in enumerate((4, 3, 5, 2, 6, 1, 7, 0))]

    r_z = Group(R1.at[pl.ds(0, 7)])
    r_xy = Group(W.at[pl.ds(0, 5), pl.ds(0, 3), pl.ds(0, 2), :, ca])
    all_z = pl.ds(0, NZ)

    def pack(o):
        j = turn("z", o)
        packed = jnp.dot(hot[j], D[...], preferred_element_type=F32)
        packed = packed.reshape(NY, NX, 8, HEAD_DIM).astype(BF16)
        if o:
            S[j] = packed
            r_z.send(S.at[j], R1.at[z], along("z", o))
        else:
            R1[z] = packed

    def route_plane():
        r_z.wait()
        for oy in range(NY):
            for ox in range(NX):
                jy, jx = turn("y", oy), turn("x", ox)
                if oy or ox:
                    r_xy.send(R1.at[all_z, jy, jx], R3.at[all_z, y, x], device(z, jy, jx, m))
        for s in range(NZ):
            R3[s, y, x] = R1[s, y, x]

    def unpack():
        r_xy.wait()
        Rf[...] = R3[...].astype(F32).reshape(8 * ROWS, HEAD_DIM)
        for h in range(HEADS):
            G[:, h * HEAD_DIM:(h + 1) * HEAD_DIM] = Rf[pl.ds(h, 2 * ROWS, stride=HEADS), :].astype(BF16)

    def product(tile):
        return lax.dot_general(G[...], W[tile].reshape(SLAB, COLS), (((1,), (1,)), ((), ())),
                               preferred_element_type=F32).astype(BF16)

    halves = []

    def give(t):
        DXs[t] = product((1 - m) * 4 + t)
        group = Group(DXr.at[t])
        group.send(DXs.at[t], DXr.at[t], partner)
        halves.append(group)

    def take(t):
        own = product(m * 4 + t).astype(F32)
        halves[t].wait()
        rows_out[:, t * SLAB:(t + 1) * SLAB] = (own + DXr[t].astype(F32)).astype(BF16)

    ra_y, ra_x = Group(aYr), Group(aXr)
    scale = 1.0 / 128.0

    def a_over_y(k):
        a_group[k].wait()
        total = ring_sum("z", NX, a_local(k), aZr.at[k])
        if k == 0:
            a1[...] = total
        else:
            aYs[k - 1] = total.astype(BF16)
            ra_y.send(aYs.at[k - 1], aYr.at[k - 1], along("y", k))

    def a_over_x():
        ra_y.wait()
        total = a1[...]
        for o in range(NY - 1):
            total += aYr[o].astype(F32)
        a2[...] = total
        aXs[...] = total.astype(BF16)
        for o in range(1, NX):
            ra_x.send(aXs.at[turn("x", o)], aXr.at[o - 1], along("x", o))

    def finish_bc():
        to_z.wait()
        total = Zf[...]
        for o in range(NZ - 1):
            total += Zr[o].astype(F32)
        grad_out[:, 0:A0] = total * scale

    def finish_a():
        ra_x.wait()
        total = a2[x]
        for o in range(NX - 1):
            total += aXr[o].astype(F32)
        grad_out[:, A0:A1] = total * scale

    a_row()
    prepare(3)
    a_far(1, 0)
    chunks[0].far(1)
    arrive(5)
    arrive(1)
    arrive(2)
    arrive(3)
    arrive(6)
    prepare(4)
    a_far(2, 0)
    arrive(7)
    a_y.wait()
    a_far(1, 3)
    arrive(4)
    chunks[0].far(2)
    a_far(1, 2)
    a_far(1, 1)
    chunks[5].far(1)
    chunks[1].far(1)
    prepare(0)
    chunks[2].far(1)
    prepare(5)
    chunks[3].far(1)
    prepare(7)
    a_far(2, 3)
    a_far(2, 2)
    a_far(2, 1)
    chunks[7].far(1)
    prepare(6)
    a_far(3, 0)
    chunks[4].far(1)
    prepare(1)
    chunks[6].far(1)
    a_far(3, 3)
    a_far(3, 2)
    a_far(3, 1)
    prepare(2)
    chunks[0].group.wait()
    forward(0)
    chunks[3].far(2)
    chunks[5].far(2)
    a_far(4, 0)
    chunks[1].far(2)
    chunks[2].far(2)
    a_far(4, 3)
    chunks[4].far(2)
    chunks[7].far(2)
    a_far(4, 2)
    a_far(4, 1)
    chunks[6].far(2)
    chunks[5].group.wait()
    forward(5)
    chunks[3].group.wait()
    forward(3)
    chunks[4].group.wait()
    chunks[2].group.wait()
    forward(2)
    chunks[1].group.wait()
    forward(1)
    chunks[7].group.wait()
    forward(7)
    a_last[0].wait()
    a_last[1].wait()
    a_last[2].wait()
    a_last[3].wait()
    forward(4)
    chunks[6].group.wait()
    forward(6)
    norm_grads()
    units[0].term()
    a_step(1, 2)
    units[0].step(1)
    a_step(1, 3)
    units[2].term()
    units[2].step(1)
    pack(4)
    units[4].term()
    units[4].step(1)
    units[5].term()
    units[5].step(1)
    a_step(1, 1)
    units[1].term()
    units[1].step(1)
    pack(5)
    pack(2)
    units[3].term()
    units[3].step(1)
    units[7].term()
    units[7].step(1)
    units[6].term()
    units[6].step(1)
    a_step(1, 0)
    a_step(2, 3)
    units[0].step(2)
    units[2].step(2)
    a_step(2, 2)
    pack(3)
    units[4].step(2)
    a_step(2, 1)
    units[5].step(2)
    pack(1)
    pack(6)
    units[6].step(2)
    units[1].step(2)
    pack(7)
    a_step(2, 0)
    units[3].step(2)
    pack(0)
    a_step(3, 2)
    a_step(3, 3)
    units[0].near()
    a_step(3, 1)
    units[2].near()
    route_plane()
    units[4].near()
    a_step(3, 0)
    a_step(4, 2)
    a_step(4, 3)
    units[3].near()
    a_step(4, 1)
    units[1].near()
    units[6].near()
    units[5].near()
    a_step(4, 0)
    units[2].across()
    units[7].step(2)
    a_over_y(2)
    units[0].across()
    a_over_y(3)
    a_over_y(1)
    unpack()
    give(0)
    units[1].across()
    units[3].across()
    units[6].across()
    a_over_y(0)
    give(1)
    units[5].across()
    units[4].across()
    give(2)
    give(3)
    units[7].near()
    a_over_x()
    take(0)
    take(1)
    take(2)
    take(3)
    units[7].across()
    finish_bc()
    finish_a()
    assert len(groups) == ARRIVALS
    for k in range(SENDS):
        assert sent[k] % 4096 == 0 and sent[k] <= METER * 4096
        all_of_them = meter.at[pl.ds(0, sent[k] // 4096)]
        pltpu.make_async_remote_copy(
            src_ref=all_of_them, dst_ref=all_of_them, send_sem=send_sem.at[k], recv_sem=recv_sem.at[0],
            device_id=partner, device_id_type=MESH).wait_send()


PIECES = 4


def hand_on(rows, grad, rows_out, grad_out, sem):
    copies = [pltpu.make_async_copy(grad, grad_out, sem.at[PIECES])]
    size = rows.shape[0] // PIECES
    for i in range(PIECES):
        part = pl.ds(i * size, size)
        copies.append(pltpu.make_async_copy(rows.at[part], rows_out.at[part], sem.at[i]))
    for copy in copies:
        copy.start()
    for copy in copies:
        copy.wait()


def per_device(tokens, key_cot, routes, counts, widths, key_weight):
    vmem = pl.BlockSpec(memory_space=pltpu.VMEM)
    anywhere = pl.BlockSpec(memory_space=pl.ANY)
    buffers = [
        ((METER, 8, 128), F32),
        ((ROWS, WIDTH), BF16),
        ((ROWS, COLS), BF16),
        ((1, ROWS), jnp.int32),
        ((NZ, NY, NX, FEATS, COLS), BF16),
        ((NZ, SLAB, ROWS), BF16),
        ((NZ, NY, NX, FEATS, COLS), F32),
        ((ROWS, COLS), F32),
        ((ROWS, COLS), BF16),
        ((HEADS * ROWS, HEAD_DIM), BF16),
        ((NZ, ROWS, HEADS * ROWS), BF16),
        ((NZ, NY, NX, 8, HEAD_DIM), BF16),
        ((NZ, NY, NX, 8, HEAD_DIM), BF16),
        ((NZ, NY, NX, 8, HEAD_DIM), BF16),
        ((8 * ROWS, HEAD_DIM), F32),
        ((2 * ROWS, COLS), BF16),
        ((4, 2 * ROWS, SLAB), BF16),
        ((4, 2 * ROWS, SLAB), BF16),
        ((NY, 2, 4, NX, FEATS, 128), BF16),
        ((NY, 2, 4, NX, FEATS, 128), BF16),
        ((NX, FEATS, 128), F32),
        ((NY - 1, NX, FEATS, 128), BF16),
        ((NY - 1, NX, FEATS, 128), BF16),
        ((NX, FEATS, 128), F32),
        ((NX, FEATS, 128), BF16),
        ((NX - 1, FEATS, 128), BF16),
        ((NZ, 2, 2, NY, 16, 384), BF16),
        ((NZ, 2, 2, NY, 16, 384), BF16),
        ((NZ, NY, 16, 384), F32),
        ((NZ, NY, 16, 384), BF16),
        ((NZ, NY - 1, 16, 384), BF16),
        ((NZ, 2, 2, NX, 16, 384), BF16),
        ((NZ, 2, 2, NX, 16, 384), BF16),
        ((NZ, NX, 16, 384), F32),
        ((NZ, NX, 16, 384), BF16),
        ((NZ, NX - 1, 16, 384), BF16),
        ((FEATS, 384), F32),
        ((NZ, FEATS, 384), BF16),
        ((NZ - 1, FEATS, 384), BF16),
    ]
    rows, grad = pl.pallas_call(
        kernel,
        out_shape=(pltpu.VMEM((2 * ROWS, WIDTH // 2), BF16), pltpu.VMEM((FEATS, COLS), F32)),
        in_specs=[anywhere] * 6,
        out_specs=(vmem, vmem),
        scratch_shapes=[pltpu.VMEM(shape, dtype) for shape, dtype in buffers[:4]]
        + [pltpu.SMEM((1, 4), jnp.int32), pltpu.SMEM((4,), jnp.int32)]
        + [pltpu.VMEM(shape, dtype) for shape, dtype in buffers[4:]]
        + [pltpu.SemaphoreType.DMA((6,)), pltpu.SemaphoreType.DMA((SENDS,)), pltpu.SemaphoreType.DMA((ARRIVALS,))],
        compiler_params=pltpu.CompilerParams(
            collective_id=0, has_side_effects=True, vmem_limit_bytes=58 << 20),
    )(tokens, key_cot, routes.reshape(1, ROWS), counts, widths, key_weight)
    return pl.pallas_call(
        hand_on,
        out_shape=(jax.ShapeDtypeStruct(rows.shape, BF16), jax.ShapeDtypeStruct(grad.shape, F32)),
        in_specs=[vmem, vmem],
        out_specs=(anywhere, anywhere),
        scratch_shapes=[pltpu.SemaphoreType.DMA((PIECES + 1,))],
    )(*(pltpu.with_memory_space_constraint(held, pltpu.VMEM) for held in (rows, grad)))


def solution(mesh):
    return jax.shard_map(
        per_device,
        mesh=mesh,
        in_specs=(P("dp", None), P("dp", "mp"), P("dp", None), P("dp", None), P(), P("dp", "mp")),
        out_specs=(P("dp", "mp"), P("dp", "mp")),
        check_vma=False,
    )
```
